32 devices in a mesh: seq: 8 (over z, x), ch: 4 (over y, core).
Axes of the slice: x: 2, y: 2, z: 4, core: 2. Of those that a mesh axis runs over, the one named last changes fastest.
Arguments:
- out_grad: float32 [128, 32768], P('ch', 'seq'), may hold values from -6 to 6
- gated_input: float32 [128, 32768], P('ch', 'seq'), may hold values from -6 to 6
- features: float32 [64, 32768], P(None, 'seq'), may hold values from -1 to 1
- filter_weight: float32 [64, 128], replicated, may hold values from -0.0078125 to 0.0078125
- rates: float32 [128], replicated, may hold values from 3 to 15
- skip_bias: float32 [128], replicated, may hold values from -3 to 3
Outputs:
- in_grad: float32 [128, 32768], P('ch', 'seq')
- feat_grad: float32 [64, 32768], P(None, ('seq', 'ch'))
The draws below stay inside these ranges and needn't reach their ends.
All inputs are finite; a program needn't handle non-finite values.
Results may differ from the reference program's by a relative error of at most 0.0003.
Values sent between devices are 32-bit elements; how exact they have to be, the bound alone decides.
A program may use at most 128 MiB of HBM per device.

```python
import math
import jax
import jax.numpy as jnp
from jax import lax

CH = 128
FO = 64
L = 32768


def block_levels(own_key, shape, pieces, least, largest):
    loudness, own = 1.0, jax.random.fold_in(own_key, 6)
    for dim, parts in pieces:
        steps = jnp.exp(jax.random.uniform(jax.random.fold_in(own, dim), (parts,), jnp.float32, least / len(pieces), largest / len(pieces)))
        loudness = loudness * jnp.repeat(steps, shape[dim] // parts).reshape([-1 if axis == dim else 1 for axis in range(len(shape))])
    return loudness


def normal_values(rng, shape, spread, most, split=(), held_as=jnp.bfloat16):
    values = jax.random.normal(rng, shape, jnp.float32) * spread
    if len(split) > 0:
        values = block_levels(rng, shape, split, -0.22, 0.18) * values
    return jnp.clip(values, min=-most, max=most).astype(held_as)


def setup_inputs(seed: int = 0) -> dict:
    key_of = jax.random.split(jax.random.key(seed), 7)
    return {
        "out_grad": normal_values(key_of[0], (CH, L), 1.0, 6.0, ((0, 4), (1, 8)), jnp.float32),
        "gated_input": normal_values(key_of[1], (CH, L), 1.0, 6.0, ((0, 4), (1, 8)), jnp.float32),
        "features": jnp.clip(jax.random.uniform(key_of[2], (FO, L), jnp.float32, -1.0, 1.0) * block_levels(key_of[2], (FO, L), ((1, 8),), -0.4, 0.0), -1.0, 1.0),
        "filter_weight": normal_values(key_of[3], (FO, CH), (FO * L // 4) ** -0.5, 0.0078125, (), jnp.float32),
        "rates": jnp.clip(jnp.exp(jax.random.uniform(key_of[4], (CH,), jnp.float32, math.log(3.0), math.log(15.0))), 3.0, 15.0),
        "skip_bias": normal_values(key_of[5], (CH,), 1.0, 3.0, (), jnp.float32),
    }


shift_term = 0.05


def reference(out_grad, gated_input, features, filter_weight, rates, skip_bias):
    steps_t = jnp.arange(L).astype(jnp.float32) / L
    window = jnp.exp(-rates[:, None] * steps_t[None, :]) + shift_term
    filter_vals = jnp.dot(filter_weight.T, features, precision=lax.Precision.HIGHEST, preferred_element_type=jnp.float32) * window
    group_size = math.gcd(CH, 8)
    padded_len = 2 * L

    def one_group(operands):
        grad_block, input_block, filter_block = operands
        grad_spec = jnp.fft.rfft(grad_block, n=padded_len, axis=-1)
        input_spec = jnp.fft.rfft(input_block, n=padded_len, axis=-1)
        filter_spec = jnp.fft.rfft(filter_block, n=padded_len, axis=-1)
        conv_part = jnp.fft.irfft(jnp.conj(filter_spec) * grad_spec, n=padded_len, axis=-1)[:, :L]
        lag_part = jnp.fft.irfft(jnp.conj(input_spec) * grad_spec, n=padded_len, axis=-1)[:, :L]
        return conv_part.astype(jnp.float32), lag_part.astype(jnp.float32)

    def stacked(values):
        return values.reshape(CH // group_size, group_size, L)

    conv_grad, filt_grad = lax.map(one_group, (stacked(out_grad), stacked(gated_input), stacked(filter_vals)))
    conv_grad = conv_grad.reshape(CH, L)
    filt_grad = filt_grad.reshape(CH, L)
    in_grad = conv_grad + skip_bias[:, None] * out_grad
    feat_grad = jnp.dot(filter_weight, filt_grad * window, precision=lax.Precision.HIGHEST, preferred_element_type=jnp.float32)
    return in_grad, feat_grad
```

```python
import functools
import math

import jax
import jax.numpy as jnp
import numpy as np
from jax import lax
from jax.experimental import pallas as pl
from jax.experimental.pallas import tpu as pltpu
from jax.sharding import PartitionSpec as P

shift_term = 0.05
highest = lax.Precision.HIGHEST


def matmul_high(operand, matrix):
    return jnp.dot(operand, matrix, precision=highest, preferred_element_type=jnp.float32)


def angle_table(first_ids, second_ids, period):
    product = first_ids[:, None] * second_ids[None, :] % period
    angles = product.astype(jnp.float32) * (2.0 * math.pi / period)
    return (jnp.cos(angles), jnp.sin(angles))


def contract(real_part, imag_part, cos_table, sin_table, einsum_form):

    def multiply_by(operand, matrix):
        return jnp.einsum(
            einsum_form, operand, matrix, precision=highest, preferred_element_type=jnp.float32
        )

    return (
        multiply_by(real_part, cos_table) - multiply_by(imag_part, sin_table),
        multiply_by(real_part, sin_table) + multiply_by(imag_part, cos_table),
    )


def group_width(channels, block_len):
    return math.gcd(channels, max(1, 128 // block_len)) * block_len


def group_table(width, block_len, sign_term):
    ids = jnp.arange(width, dtype=jnp.int32)
    same = ids[:, None] // block_len == ids[None, :] // block_len
    inner = ids % block_len
    product = inner[:, None] * inner[None, :] % block_len
    angles = product.astype(jnp.float32) * (2.0 * math.pi / block_len)
    return (
        jnp.where(same, jnp.cos(angles), 0.0).astype(jnp.float32),
        jnp.where(same, sign_term * jnp.sin(angles), 0.0).astype(jnp.float32),
    )


def local_transform(real_part, imag_part, block_len, inverse):
    rows, seq_count, width_all = real_part.shape
    channels = width_all // block_len
    local_len = seq_count * block_len
    width = group_width(channels, block_len)
    sign_term = 1.0 if inverse else -1.0
    seq_ids = jnp.arange(seq_count, dtype=jnp.int32)
    block_ids = jnp.arange(block_len, dtype=jnp.int32)
    cos_seq, sin_seq = angle_table(seq_ids, seq_ids, seq_count)
    sin_seq = sign_term * sin_seq
    cos_twist, sin_twist = angle_table(seq_ids, block_ids, local_len)
    cos_twist = jnp.tile(cos_twist, (1, channels))
    sin_twist = sign_term * jnp.tile(sin_twist, (1, channels))
    cos_group, sin_group = group_table(width, block_len, sign_term)
    grouped = (rows, seq_count, width_all // width, width)
    flat = (rows, seq_count, width_all)

    def twist(re_part, im_part):
        return (
            re_part * cos_twist - im_part * sin_twist,
            re_part * sin_twist + im_part * cos_twist,
        )

    def across_groups(re_part, im_part):
        re_part, im_part = contract(
            re_part.reshape(grouped),
            im_part.reshape(grouped),
            cos_group,
            sin_group,
            "rkgm,mq->rkgq",
        )
        return (re_part.reshape(flat), im_part.reshape(flat))

    if inverse:
        real_part, imag_part = across_groups(real_part, imag_part)
        real_part, imag_part = twist(real_part, imag_part)
        real_part, imag_part = contract(real_part, imag_part, cos_seq, sin_seq, "rsx,sk->rkx")
    else:
        real_part, imag_part = contract(real_part, imag_part, cos_seq, sin_seq, "rsx,sk->rkx")
        real_part, imag_part = twist(real_part, imag_part)
        real_part, imag_part = across_groups(real_part, imag_part)
    return (real_part, imag_part)


def first_section(row_block, cos_fwd, sin_fwd, twid_cos, twid_sin):
    real_part = matmul_high(cos_fwd, row_block)
    imag_part = -matmul_high(sin_fwd, row_block)
    real_out = real_part * twid_cos + imag_part * twid_sin
    imag_out = imag_part * twid_cos - real_part * twid_sin
    return (real_out[:, None, :], imag_out[:, None, :])


def rotate_back(real_part, imag_part, twid_cos, twid_sin):
    return (
        real_part * twid_cos - imag_part * twid_sin,
        real_part * twid_sin + imag_part * twid_cos,
    )


def forward_products(
    block_len, grad_real, grad_imag, input_real, input_imag, filter_real, filter_imag
):
    grad_real, grad_imag = local_transform(grad_real, grad_imag, block_len, False)
    input_real, input_imag = local_transform(input_real, input_imag, block_len, False)
    filter_real, filter_imag = local_transform(filter_real, filter_imag, block_len, False)
    corr_real = filter_real * grad_real + filter_imag * grad_imag
    corr_imag = filter_real * grad_imag - filter_imag * grad_real
    lag_real = input_real * grad_real + input_imag * grad_imag
    lag_imag = input_real * grad_imag - input_imag * grad_real
    return (corr_real, corr_imag, lag_real, lag_imag)


def products_inverted(block_len, operands):
    corr_real, corr_imag, lag_real, lag_imag = forward_products(block_len, *operands)
    corr_real, corr_imag = local_transform(corr_real, corr_imag, block_len, True)
    lag_real, lag_imag = local_transform(lag_real, lag_imag, block_len, True)
    return (corr_real, corr_imag, lag_real, lag_imag)


def paired_rows(block_len, operands):
    seq_count = operands[0].shape[1]
    channels = operands[0].shape[2] // block_len
    local_len = seq_count * block_len
    positions = (
        jnp.arange(seq_count, dtype=jnp.int32)[:, None] * block_len
        + jnp.arange(block_len, dtype=jnp.int32)[None, :]
    )
    angles = positions.astype(jnp.float32) * (math.pi / local_len)
    half_cos = jnp.tile(jnp.cos(angles), (1, channels))
    half_sin = jnp.tile(jnp.sin(angles), (1, channels))
    stacked = []
    for index in range(3):
        low_row = operands[2 * index]
        high_row = operands[2 * index + 1]
        stacked.append(jnp.concatenate([low_row, high_row * half_cos], axis=0))
        stacked.append(jnp.concatenate([jnp.zeros_like(low_row), -high_row * half_sin], axis=0))
    corr_real, corr_imag, lag_real, lag_imag = products_inverted(block_len, tuple(stacked))
    return (
        corr_real[0:1],
        corr_real[1:2] * half_cos - corr_imag[1:2] * half_sin,
        lag_real[0:1],
        lag_real[1:2] * half_cos - lag_imag[1:2] * half_sin,
    )


def local(out_grad, gated_input, features, filter_weight, rates, skip_bias):
    channels, local_len = out_grad.shape
    seq_count = lax.axis_size("seq")
    block_len = local_len // seq_count
    width_all = channels * block_len
    freq_count = 2 * seq_count
    full_len = local_len * seq_count
    padded_len = 2 * full_len
    seq_place = lax.axis_index("seq")
    first_chan = lax.axis_index("ch") * channels
    local_rates = lax.dynamic_slice_in_dim(rates, first_chan, channels)
    local_bias = lax.dynamic_slice_in_dim(skip_bias, first_chan, channels)
    local_weight = lax.dynamic_slice_in_dim(filter_weight, first_chan, channels, 1)
    position = seq_place * local_len + jnp.arange(local_len, dtype=jnp.int32)
    window = (
        jnp.exp(-local_rates[:, None] * (position.astype(jnp.float32) / full_len)[None, :])
        + shift_term
    )
    filter_vals = matmul_high(local_weight.T, features) * window

    def to_rows(values):
        return (
            values.reshape(channels, seq_count, block_len)
            .transpose(1, 0, 2)
            .reshape(seq_count, width_all)
        )

    received = (
        lax.all_to_all(to_rows(out_grad), "seq", split_axis=0, concat_axis=0, tiled=True),
        lax.all_to_all(to_rows(gated_input), "seq", split_axis=0, concat_axis=0, tiled=True),
        lax.all_to_all(to_rows(filter_vals), "seq", split_axis=0, concat_axis=0, tiled=True),
    )

    def inverted(operands):
        return products_inverted(block_len, operands)

    def paired(operands):
        return paired_rows(block_len, operands)

    freq_ids = jnp.arange(freq_count, dtype=jnp.int32)
    dev_ids = jnp.arange(seq_count, dtype=jnp.int32)
    local_m = seq_place * block_len + jnp.arange(block_len, dtype=jnp.int32)
    twid_cos, twid_sin = angle_table(freq_ids, local_m, padded_len)
    twid_cos = jnp.tile(twid_cos, (1, channels))
    twid_sin = jnp.tile(twid_sin, (1, channels))
    scale_term = 1.0 / padded_len
    alternate = jnp.where(dev_ids % 2 == 0, 1.0, -1.0).astype(jnp.float32)
    cos_half, sin_half = angle_table(dev_ids, dev_ids, freq_count)
    sin_half = jnp.where(dev_ids[:, None] == 0, -alternate[None, :], sin_half)
    twid_half_cos = twid_cos[:seq_count]
    twid_half_sin = twid_sin[:seq_count]
    spread = [
        first_section(piece, cos_half, sin_half, twid_half_cos, twid_half_sin) for piece in received
    ]
    exchanged = (
        lax.all_to_all(spread[0][0], "seq", split_axis=0, concat_axis=1, tiled=True),
        lax.all_to_all(spread[0][1], "seq", split_axis=0, concat_axis=1, tiled=True),
        lax.all_to_all(spread[1][0], "seq", split_axis=0, concat_axis=1, tiled=True),
        lax.all_to_all(spread[1][1], "seq", split_axis=0, concat_axis=1, tiled=True),
        lax.all_to_all(spread[2][0], "seq", split_axis=0, concat_axis=1, tiled=True),
        lax.all_to_all(spread[2][1], "seq", split_axis=0, concat_axis=1, tiled=True),
    )
    corr_real, corr_imag, lag_real, lag_imag = lax.cond(
        seq_place == 0, paired, inverted, tuple(exchanged)
    )
    corr_real, corr_imag, lag_real, lag_imag = (
        lax.all_to_all(corr_real, "seq", split_axis=1, concat_axis=0, tiled=True),
        lax.all_to_all(corr_imag, "seq", split_axis=1, concat_axis=0, tiled=True),
        lax.all_to_all(lag_real, "seq", split_axis=1, concat_axis=0, tiled=True),
        lax.all_to_all(lag_imag, "seq", split_axis=1, concat_axis=0, tiled=True),
    )
    corr_flat_real, corr_flat_imag = rotate_back(
        corr_real.reshape(seq_count, width_all),
        corr_imag.reshape(seq_count, width_all),
        twid_half_cos,
        twid_half_sin,
    )
    lag_flat_real, lag_flat_imag = rotate_back(
        lag_real.reshape(seq_count, width_all),
        lag_imag.reshape(seq_count, width_all),
        twid_half_cos,
        twid_half_sin,
    )
    cos_final, sin_final = angle_table(dev_ids, dev_ids, freq_count)
    cos_final = jnp.where(dev_ids[None, :] == 0, 1.0, 2.0 * cos_final)
    sin_final = jnp.where(dev_ids[None, :] == 0, -alternate[:, None], 2.0 * sin_final)
    conv_rows = (
        matmul_high(cos_final, corr_flat_real) - matmul_high(sin_final, corr_flat_imag)
    ) * scale_term
    lag_rows = (
        matmul_high(cos_final, lag_flat_real) - matmul_high(sin_final, lag_flat_imag)
    ) * scale_term
    conv_back, lag_back = (
        lax.all_to_all(conv_rows, "seq", split_axis=0, concat_axis=0, tiled=True),
        lax.all_to_all(lag_rows, "seq", split_axis=0, concat_axis=0, tiled=True),
    )

    def to_channels(values):
        return (
            values.reshape(seq_count, channels, block_len)
            .transpose(1, 0, 2)
            .reshape(channels, local_len)
        )

    conv_grad = to_channels(conv_back)
    filt_grad = to_channels(lag_back)
    in_grad = conv_grad + local_bias[:, None] * out_grad
    weighted = filt_grad * window
    regrouped = lax.all_to_all(weighted, "ch", split_axis=1, concat_axis=0, tiled=True)
    feat_grad = matmul_high(filter_weight, regrouped)
    return (in_grad, feat_grad)


lanes = 128
conv_joint = 2


def split_table(table):
    table = np.asarray(table, np.float32)
    high_part = table.astype(jnp.bfloat16)
    low_part = (table - high_part.astype(np.float32)).astype(jnp.bfloat16)
    return np.stack([high_part, low_part])


def make_tables(data_rows):
    freq_rows = 2 * data_rows
    padded_len = freq_rows * lanes
    odd_ids = 2 * np.arange(data_rows) + 1
    row_angle = (odd_ids[:, None] * np.arange(data_rows)[None, :] % (2 * freq_rows)) * (
        math.pi / freq_rows
    )
    row_table = np.concatenate([np.cos(row_angle), -np.sin(row_angle)], axis=0)
    lane_ids = np.arange(lanes)
    twist_angle = (odd_ids[:, None] * lane_ids[None, :]) * (math.pi / padded_len)
    twist = np.stack([np.cos(twist_angle), -np.sin(twist_angle)]).astype(np.float32)
    lane_angle = (lane_ids[:, None] * lane_ids[None, :] % lanes) * (2.0 * math.pi / lanes)
    lane_cos, lane_sin = np.cos(lane_angle), np.sin(lane_angle)
    lane_table = np.block([[lane_cos, -lane_sin], [lane_sin, lane_cos]])
    back_table = np.block([[lane_cos, lane_sin], [-lane_sin, lane_cos]]) * (2.0 / padded_len)
    return (
        split_table(row_table),
        split_table(row_table.T),
        split_table(lane_table),
        split_table(back_table),
        twist,
    )


def split_value(value):
    high_part = value.astype(jnp.bfloat16)
    return high_part, (value - high_part.astype(jnp.float32)).astype(jnp.bfloat16)


def dot_split(left, right):
    def product(first, second):
        return jnp.dot(first, second, preferred_element_type=jnp.float32)

    return product(left[0], right[0]) + (product(left[0], right[1]) + product(left[1], right[0]))


def whole_kernel(
    sizes,
    grad_hbm,
    input_hbm,
    feat_hbm,
    weight_ref,
    rate_ref,
    bias_ref,
    row_hbm,
    row_back_hbm,
    lane_hbm,
    lane_back_hbm,
    twist_hbm,
    in_grad_hbm,
    feat_grad_hbm,
    grad_ref,
    input_ref,
    feat_ref,
    row_ref,
    row_back_ref,
    lane_ref,
    lane_back_ref,
    twist_ref,
    load_sem,
    in_grad_ref,
    feat_grad_ref,
    send_buf,
    gather_buf,
    conv_send,
    lag_send,
    conv_recv,
    lag_recv,
    window_buf,
    rate_buf,
    bias_buf,
    weight_buf,
    fwd_recv_sem,
    conv_recv_sem,
    send_sem,
    lag_recv_sem,
    store_sem,
):
    seq_count, ch_count, channels, rows = sizes
    per = channels // seq_count
    joint = math.gcd(per, conv_joint)
    data_rows = rows * seq_count
    sub_rows = rows // ch_count
    all_channels = channels * ch_count
    total = seq_count * ch_count
    full_len = data_rows * lanes
    seq_place = lax.axis_index("seq")
    ch_place = lax.axis_index("ch")
    flat_place = seq_place * ch_count + ch_place

    loads = [
        pltpu.make_async_copy(source, target, load_sem.at[index])
        for index, (source, target) in enumerate(
            (
                (grad_hbm, grad_ref),
                (input_hbm, input_ref),
                (feat_hbm, feat_ref),
                (row_hbm, row_ref),
                (twist_hbm, twist_ref),
                (lane_hbm, lane_ref),
                (lane_back_hbm, lane_back_ref),
                (row_back_hbm, row_back_ref),
            )
        )
    ]
    barrier = pltpu.get_barrier_semaphore()

    def greet(step, carry):
        other = lax.rem(flat_place + step, total)
        pl.semaphore_signal(
            barrier,
            inc=1,
            device_id={"seq": other // ch_count, "ch": lax.rem(other, ch_count)},
            device_id_type=pl.DeviceIdType.MESH,
        )
        return carry

    lax.fori_loop(1, total, greet, 0)
    for load in loads:
        load.start()

    def each_other(place, count, visit):
        def one(step, carry):
            visit(lax.rem(place + step, count))
            return carry

        lax.fori_loop(1, count, one, 0)

    def remote(source, target, send, recv, device):
        return pltpu.make_async_remote_copy(
            src_ref=source,
            dst_ref=target,
            send_sem=send,
            recv_sem=recv,
            device_id=device,
            device_id_type=pl.DeviceIdType.MESH,
        )

    def fwd_copy(first, last, chan, target):
        return remote(
            send_buf.at[
                first:last, pl.ds(pl.multiple_of((target * per + chan) * rows, 8), rows)
            ],
            gather_buf.at[
                first:last, chan, pl.ds(pl.multiple_of(seq_place * rows, 8), rows)
            ],
            send_sem.at[0],
            fwd_recv_sem.at[chan],
            {"seq": target, "ch": ch_place},
        )

    def fwd_arrived(chan):
        part = gather_buf.at[:, chan, pl.ds(0, (seq_count - 1) * rows)]
        remote(
            part, part, send_sem.at[0], fwd_recv_sem.at[chan], {"seq": seq_place, "ch": ch_place}
        ).wait_recv()

    def conv_copy(group, target):
        return remote(
            conv_send.at[target, pl.ds(pl.multiple_of(group * joint * rows, 8), joint * rows)],
            conv_recv.at[
                pl.ds(
                    pl.multiple_of((seq_place * per + group * joint) * rows, 8), joint * rows
                )
            ],
            send_sem.at[1],
            conv_recv_sem.at[group],
            {"seq": target, "ch": ch_place},
        )

    def lag_row(flat):
        channel = lax.rem(flat, ch_count) * channels + (flat // ch_count) * per
        return pl.multiple_of(channel * sub_rows, 8)

    def lag_copy(target):
        return remote(
            lag_send.at[target],
            lag_recv.at[pl.ds(lag_row(flat_place), per * sub_rows)],
            send_sem.at[2],
            lag_recv_sem.at[0],
            {"seq": target // ch_count, "ch": lax.rem(target, ch_count)},
        )

    def to_rows(which, index, tile):
        send_buf[which, pl.ds(index, channels, stride=rows), :] = tile

    rate_buf[...] = jnp.broadcast_to(rate_ref[...], (lanes, all_channels)).T
    weight_buf[...] = weight_ref[...].T
    loads[0].wait()
    for index in range(rows):
        to_rows(0, index, grad_ref[:, index * lanes : (index + 1) * lanes])
    loads[1].wait()
    for index in range(rows):
        to_rows(1, index, input_ref[:, index * lanes : (index + 1) * lanes])

    pl.semaphore_wait(barrier, total - 1)

    def send_fwd(first, last, chan):
        each_other(
            seq_place, seq_count, lambda target: fwd_copy(first, last, chan, target).start()
        )

    send_fwd(0, 2, 0)

    first_chan = pl.multiple_of(ch_place * channels, 8)
    local_rates = rate_buf[pl.ds(first_chan, channels), :]
    local_weight = split_value(weight_buf[pl.ds(first_chan, channels), :])
    lane_ids = lax.broadcasted_iota(jnp.int32, (1, lanes), 1)

    def window_of(rates, first):
        steps_t = (first + lane_ids).astype(jnp.float32) / full_len
        return jnp.exp(-rates * steps_t) + shift_term

    bias_buf[...] = jnp.broadcast_to(bias_ref[...], (lanes, all_channels)).T
    loads[2].wait()
    chunk = math.gcd(rows, 4)
    for outer in range(rows // chunk):
        lo = outer * chunk * lanes
        block = split_value(feat_ref[:, lo : lo + chunk * lanes])
        values = dot_split(local_weight, block)
        for inner in range(chunk):
            index = outer * chunk + inner
            window = window_of(local_rates, (seq_place * rows + index) * lanes)
            to_rows(2, index, values[:, inner * lanes : (inner + 1) * lanes] * window)

    send_fwd(2, 3, 0)

    def send_rest(chan, carry):
        send_fwd(0, 3, chan)
        return carry

    lax.fori_loop(1, per, send_rest, 0)

    own_rows = pl.ds(pl.multiple_of(seq_place * rows, 8), rows)

    def keep_own(chan, carry):
        for which in range(3):
            gather_buf[which, chan, own_rows, :] = send_buf[
                which, pl.ds(pl.multiple_of((seq_place * per + chan) * rows, 8), rows), :
            ]
        return carry

    lax.fori_loop(0, per, keep_own, 0)

    for index in range(sub_rows):
        window_buf[index] = window_of(rate_buf[...], (flat_place * sub_rows + index) * lanes)

    for load in loads[3:]:
        load.wait()

    def work(chan, carry):
        fwd_arrived(chan)

        twist_cos, twist_sin = twist_ref[0], twist_ref[1]
        packed = jnp.concatenate([gather_buf[which, chan] for which in range(3)], axis=1)
        spread = dot_split((row_ref[0], row_ref[1]), split_value(packed))
        turned = []
        for which in range(3):
            re_part = spread[:data_rows, which * lanes : (which + 1) * lanes]
            im_part = spread[data_rows:, which * lanes : (which + 1) * lanes]
            turned.append(
                jnp.concatenate(
                    [
                        re_part * twist_cos - im_part * twist_sin,
                        re_part * twist_sin + im_part * twist_cos,
                    ],
                    axis=1,
                )
            )
        freqs = [
            dot_split(split_value(part), (lane_ref[0], lane_ref[1])) for part in turned
        ]
        grad_re, grad_im = freqs[0][:, :lanes], freqs[0][:, lanes:]

        def inverse(spectrum):
            re_part, im_part = spectrum[:, :lanes], spectrum[:, lanes:]
            product = jnp.concatenate(
                [
                    re_part * grad_re + im_part * grad_im,
                    re_part * grad_im - im_part * grad_re,
                ],
                axis=1,
            )
            back = dot_split(split_value(product), (lane_back_ref[0], lane_back_ref[1]))
            re_part, im_part = back[:, :lanes], back[:, lanes:]
            return jnp.concatenate(
                [
                    re_part * twist_cos + im_part * twist_sin,
                    im_part * twist_cos - re_part * twist_sin,
                ],
                axis=0,
            )

        both = jnp.concatenate([inverse(freqs[2]), inverse(freqs[1])], axis=1)
        final = dot_split((row_back_ref[0], row_back_ref[1]), split_value(both))
        conv_send[:, pl.ds(pl.multiple_of(chan * rows, 8), rows), :] = final[:, :lanes].reshape(
            seq_count, rows, lanes
        )
        lag_send[:, pl.ds(pl.multiple_of(chan * sub_rows, 8), sub_rows), :] = final[
            :, lanes:
        ].reshape(total, sub_rows, lanes)

        @pl.when(lax.rem(chan, joint) == joint - 1)
        def _():
            group = chan // joint
            each_other(seq_place, seq_count, lambda target: conv_copy(group, target).start())

        return carry

    lax.fori_loop(0, per, work, 0)
    each_other(flat_place, total, lambda target: lag_copy(target).start())
    conv_recv[pl.ds(pl.multiple_of(seq_place * per * rows, 8), per * rows), :] = conv_send[
        seq_place
    ]
    lag_recv[pl.ds(lag_row(flat_place), per * sub_rows), :] = lag_send[flat_place]

    here = {"seq": seq_place, "ch": ch_place}
    for group in range(per // joint):
        part = conv_recv.at[pl.ds(0, (seq_count - 1) * joint * rows)]
        remote(part, part, send_sem.at[1], conv_recv_sem.at[group], here).wait_recv()
    local_bias = bias_buf[pl.ds(first_chan, channels), :]
    for index in range(rows):
        span = slice(index * lanes, (index + 1) * lanes)
        in_grad_ref[:, span] = (
            conv_recv[pl.ds(index, channels, stride=rows), :] + local_bias * grad_ref[:, span]
        )
    in_grad_store = pltpu.make_async_copy(in_grad_ref, in_grad_hbm, store_sem.at[0])
    in_grad_store.start()

    part = send_buf.at[:, pl.ds(0, (seq_count - 1) * per * rows)]
    remote(part, part, send_sem.at[0], fwd_recv_sem.at[0], here).wait_send()
    part = conv_recv.at[pl.ds(0, (seq_count - 1) * per * rows)]
    remote(part, part, send_sem.at[1], conv_recv_sem.at[0], here).wait_send()
    part = lag_send.at[pl.ds(0, total - 1)]
    remote(part, part, send_sem.at[2], lag_recv_sem.at[0], here).wait_send()
    remote(part, part, send_sem.at[2], lag_recv_sem.at[0], here).wait_recv()
    weight = split_value(weight_ref[...])
    for index in range(sub_rows):
        tile = lag_recv[pl.ds(index, all_channels, stride=sub_rows), :] * window_buf[index]
        feat_grad_ref[:, index * lanes : (index + 1) * lanes] = dot_split(
            weight, split_value(tile)
        )
    feat_store = pltpu.make_async_copy(feat_grad_ref, feat_grad_hbm, store_sem.at[1])
    feat_store.start()
    in_grad_store.wait()
    feat_store.wait()


def local_whole(seq_count, ch_count, tables, *args):
    out_grad, gated_input, features, filter_weight, rates, skip_bias = args
    channels, local_len = out_grad.shape
    rows = local_len // lanes
    feats, all_channels = filter_weight.shape
    per = channels // seq_count
    data_rows = rows * seq_count
    sub_rows = rows // ch_count
    total = seq_count * ch_count
    sizes = (seq_count, ch_count, channels, rows)
    in_vmem = pl.BlockSpec(memory_space=pltpu.VMEM)
    anywhere = pl.BlockSpec(memory_space=pl.ANY)
    dma = pltpu.SemaphoreType.DMA
    f32 = jnp.float32
    return pl.pallas_call(
        functools.partial(whole_kernel, sizes),
        out_shape=(
            jax.ShapeDtypeStruct((channels, local_len), f32),
            jax.ShapeDtypeStruct((feats, sub_rows * lanes), f32),
        ),
        in_specs=[anywhere] * 3 + [in_vmem] * 3 + [anywhere] * 5,
        out_specs=(anywhere, anywhere),
        scratch_shapes=[
            pltpu.VMEM((channels, local_len), f32),
            pltpu.VMEM((channels, local_len), f32),
            pltpu.VMEM((feats, local_len), f32),
            *[pltpu.VMEM(table.shape, table.dtype) for table in tables],
            dma((8,)),
            pltpu.VMEM((channels, local_len), f32),
            pltpu.VMEM((feats, sub_rows * lanes), f32),
            pltpu.VMEM((3, channels * rows, lanes), f32),
            pltpu.VMEM((3, per, data_rows, lanes), f32),
            pltpu.VMEM((seq_count, per * rows, lanes), f32),
            pltpu.VMEM((total, per * sub_rows, lanes), f32),
            pltpu.VMEM((channels * rows, lanes), f32),
            pltpu.VMEM((all_channels * sub_rows, lanes), f32),
            pltpu.VMEM((sub_rows, all_channels, lanes), f32),
            pltpu.VMEM((all_channels, lanes), f32),
            pltpu.VMEM((all_channels, lanes), f32),
            pltpu.VMEM((all_channels, feats), f32),
            dma((per,)),
            dma((per // math.gcd(per, conv_joint),)),
            dma((3,)),
            dma((1,)),
            dma((2,)),
        ],
        compiler_params=pltpu.CompilerParams(collective_id=0, has_side_effects=True),
    )(
        out_grad,
        gated_input,
        features,
        filter_weight,
        rates.reshape(1, all_channels),
        skip_bias.reshape(1, all_channels),
        *[jnp.asarray(table) for table in tables],
    )


def solution(mesh):
    seq_count, ch_count = mesh.shape["seq"], mesh.shape["ch"]
    in_specs = (P("ch", "seq"), P("ch", "seq"), P(None, "seq"), P(), P(), P())
    out_specs = (P("ch", "seq"), P(None, ("seq", "ch")))

    def whole(*args):
        channels, full_len = args[0].shape
        channels = channels // ch_count
        local_len = full_len // seq_count
        fits = (
            seq_count % 2 == 0
            and channels % seq_count == 0
            and channels % 8 == 0
            and local_len % (8 * lanes * ch_count) == 0
            and full_len <= 512 * lanes
        )
        body = local
        if fits:
            tables = make_tables(full_len // lanes)
            body = functools.partial(local_whole, seq_count, ch_count, tables)
        return jax.shard_map(
            body, mesh=mesh, in_specs=in_specs, out_specs=out_specs, check_vma=False
        )(*args)

    return whole
```

```python
import functools
import math

import jax
import jax.numpy as jnp
import numpy as np
from jax import lax
from jax.experimental import pallas as pl
from jax.experimental.pallas import tpu as pltpu
from jax.sharding import PartitionSpec as P

shift_term = 0.05
highest = lax.Precision.HIGHEST


def matmul_high(operand, matrix):
    return jnp.dot(operand, matrix, precision=highest, preferred_element_type=jnp.float32)


def angle_table(first_ids, second_ids, period):
    product = first_ids[:, None] * second_ids[None, :] % period
    angles = product.astype(jnp.float32) * (2.0 * math.pi / period)
    return (jnp.cos(angles), jnp.sin(angles))


def contract(real_part, imag_part, cos_table, sin_table, einsum_form):

    def multiply_by(operand, matrix):
        return jnp.einsum(
            einsum_form, operand, matrix, precision=highest, preferred_element_type=jnp.float32
        )

    return (
        multiply_by(real_part, cos_table) - multiply_by(imag_part, sin_table),
        multiply_by(real_part, sin_table) + multiply_by(imag_part, cos_table),
    )


def group_width(channels, block_len):
    return math.gcd(channels, max(1, 128 // block_len)) * block_len


def group_table(width, block_len, sign_term):
    ids = jnp.arange(width, dtype=jnp.int32)
    same = ids[:, None] // block_len == ids[None, :] // block_len
    inner = ids % block_len
    product = inner[:, None] * inner[None, :] % block_len
    angles = product.astype(jnp.float32) * (2.0 * math.pi / block_len)
    return (
        jnp.where(same, jnp.cos(angles), 0.0).astype(jnp.float32),
        jnp.where(same, sign_term * jnp.sin(angles), 0.0).astype(jnp.float32),
    )


def local_transform(real_part, imag_part, block_len, inverse):
    rows, seq_count, width_all = real_part.shape
    channels = width_all // block_len
    local_len = seq_count * block_len
    width = group_width(channels, block_len)
    sign_term = 1.0 if inverse else -1.0
    seq_ids = jnp.arange(seq_count, dtype=jnp.int32)
    block_ids = jnp.arange(block_len, dtype=jnp.int32)
    cos_seq, sin_seq = angle_table(seq_ids, seq_ids, seq_count)
    sin_seq = sign_term * sin_seq
    cos_twist, sin_twist = angle_table(seq_ids, block_ids, local_len)
    cos_twist = jnp.tile(cos_twist, (1, channels))
    sin_twist = sign_term * jnp.tile(sin_twist, (1, channels))
    cos_group, sin_group = group_table(width, block_len, sign_term)
    grouped = (rows, seq_count, width_all // width, width)
    flat = (rows, seq_count, width_all)

    def twist(re_part, im_part):
        return (
            re_part * cos_twist - im_part * sin_twist,
            re_part * sin_twist + im_part * cos_twist,
        )

    def across_groups(re_part, im_part):
        re_part, im_part = contract(
            re_part.reshape(grouped),
            im_part.reshape(grouped),
            cos_group,
            sin_group,
            "rkgm,mq->rkgq",
        )
        return (re_part.reshape(flat), im_part.reshape(flat))

    if inverse:
        real_part, imag_part = across_groups(real_part, imag_part)
        real_part, imag_part = twist(real_part, imag_part)
        real_part, imag_part = contract(real_part, imag_part, cos_seq, sin_seq, "rsx,sk->rkx")
    else:
        real_part, imag_part = contract(real_part, imag_part, cos_seq, sin_seq, "rsx,sk->rkx")
        real_part, imag_part = twist(real_part, imag_part)
        real_part, imag_part = across_groups(real_part, imag_part)
    return (real_part, imag_part)


def first_section(row_block, cos_fwd, sin_fwd, twid_cos, twid_sin):
    real_part = matmul_high(cos_fwd, row_block)
    imag_part = -matmul_high(sin_fwd, row_block)
    real_out = real_part * twid_cos + imag_part * twid_sin
    imag_out = imag_part * twid_cos - real_part * twid_sin
    return (real_out[:, None, :], imag_out[:, None, :])


def rotate_back(real_part, imag_part, twid_cos, twid_sin):
    return (
        real_part * twid_cos - imag_part * twid_sin,
        real_part * twid_sin + imag_part * twid_cos,
    )


def forward_products(
    block_len, grad_real, grad_imag, input_real, input_imag, filter_real, filter_imag
):
    grad_real, grad_imag = local_transform(grad_real, grad_imag, block_len, False)
    input_real, input_imag = local_transform(input_real, input_imag, block_len, False)
    filter_real, filter_imag = local_transform(filter_real, filter_imag, block_len, False)
    corr_real = filter_real * grad_real + filter_imag * grad_imag
    corr_imag = filter_real * grad_imag - filter_imag * grad_real
    lag_real = input_real * grad_real + input_imag * grad_imag
    lag_imag = input_real * grad_imag - input_imag * grad_real
    return (corr_real, corr_imag, lag_real, lag_imag)


def products_inverted(block_len, operands):
    corr_real, corr_imag, lag_real, lag_imag = forward_products(block_len, *operands)
    corr_real, corr_imag = local_transform(corr_real, corr_imag, block_len, True)
    lag_real, lag_imag = local_transform(lag_real, lag_imag, block_len, True)
    return (corr_real, corr_imag, lag_real, lag_imag)


def paired_rows(block_len, operands):
    seq_count = operands[0].shape[1]
    channels = operands[0].shape[2] // block_len
    local_len = seq_count * block_len
    positions = (
        jnp.arange(seq_count, dtype=jnp.int32)[:, None] * block_len
        + jnp.arange(block_len, dtype=jnp.int32)[None, :]
    )
    angles = positions.astype(jnp.float32) * (math.pi / local_len)
    half_cos = jnp.tile(jnp.cos(angles), (1, channels))
    half_sin = jnp.tile(jnp.sin(angles), (1, channels))
    stacked = []
    for index in range(3):
        low_row = operands[2 * index]
        high_row = operands[2 * index + 1]
        stacked.append(jnp.concatenate([low_row, high_row * half_cos], axis=0))
        stacked.append(jnp.concatenate([jnp.zeros_like(low_row), -high_row * half_sin], axis=0))
    corr_real, corr_imag, lag_real, lag_imag = products_inverted(block_len, tuple(stacked))
    return (
        corr_real[0:1],
        corr_real[1:2] * half_cos - corr_imag[1:2] * half_sin,
        lag_real[0:1],
        lag_real[1:2] * half_cos - lag_imag[1:2] * half_sin,
    )


def local(out_grad, gated_input, features, filter_weight, rates, skip_bias):
    channels, local_len = out_grad.shape
    seq_count = lax.axis_size("seq")
    block_len = local_len // seq_count
    width_all = channels * block_len
    freq_count = 2 * seq_count
    full_len = local_len * seq_count
    padded_len = 2 * full_len
    seq_place = lax.axis_index("seq")
    first_chan = lax.axis_index("ch") * channels
    local_rates = lax.dynamic_slice_in_dim(rates, first_chan, channels)
    local_bias = lax.dynamic_slice_in_dim(skip_bias, first_chan, channels)
    local_weight = lax.dynamic_slice_in_dim(filter_weight, first_chan, channels, 1)
    position = seq_place * local_len + jnp.arange(local_len, dtype=jnp.int32)
    window = (
        jnp.exp(-local_rates[:, None] * (position.astype(jnp.float32) / full_len)[None, :])
        + shift_term
    )
    filter_vals = matmul_high(local_weight.T, features) * window

    def to_rows(values):
        return (
            values.reshape(channels, seq_count, block_len)
            .transpose(1, 0, 2)
            .reshape(seq_count, width_all)
        )

    received = (
        lax.all_to_all(to_rows(out_grad), "seq", split_axis=0, concat_axis=0, tiled=True),
        lax.all_to_all(to_rows(gated_input), "seq", split_axis=0, concat_axis=0, tiled=True),
        lax.all_to_all(to_rows(filter_vals), "seq", split_axis=0, concat_axis=0, tiled=True),
    )

    def inverted(operands):
        return products_inverted(block_len, operands)

    def paired(operands):
        return paired_rows(block_len, operands)

    freq_ids = jnp.arange(freq_count, dtype=jnp.int32)
    dev_ids = jnp.arange(seq_count, dtype=jnp.int32)
    local_m = seq_place * block_len + jnp.arange(block_len, dtype=jnp.int32)
    twid_cos, twid_sin = angle_table(freq_ids, local_m, padded_len)
    twid_cos = jnp.tile(twid_cos, (1, channels))
    twid_sin = jnp.tile(twid_sin, (1, channels))
    scale_term = 1.0 / padded_len
    alternate = jnp.where(dev_ids % 2 == 0, 1.0, -1.0).astype(jnp.float32)
    cos_half, sin_half = angle_table(dev_ids, dev_ids, freq_count)
    sin_half = jnp.where(dev_ids[:, None] == 0, -alternate[None, :], sin_half)
    twid_half_cos = twid_cos[:seq_count]
    twid_half_sin = twid_sin[:seq_count]
    spread = [
        first_section(piece, cos_half, sin_half, twid_half_cos, twid_half_sin) for piece in received
    ]
    exchanged = (
        lax.all_to_all(spread[0][0], "seq", split_axis=0, concat_axis=1, tiled=True),
        lax.all_to_all(spread[0][1], "seq", split_axis=0, concat_axis=1, tiled=True),
        lax.all_to_all(spread[1][0], "seq", split_axis=0, concat_axis=1, tiled=True),
        lax.all_to_all(spread[1][1], "seq", split_axis=0, concat_axis=1, tiled=True),
        lax.all_to_all(spread[2][0], "seq", split_axis=0, concat_axis=1, tiled=True),
        lax.all_to_all(spread[2][1], "seq", split_axis=0, concat_axis=1, tiled=True),
    )
    corr_real, corr_imag, lag_real, lag_imag = lax.cond(
        seq_place == 0, paired, inverted, tuple(exchanged)
    )
    corr_real, corr_imag, lag_real, lag_imag = (
        lax.all_to_all(corr_real, "seq", split_axis=1, concat_axis=0, tiled=True),
        lax.all_to_all(corr_imag, "seq", split_axis=1, concat_axis=0, tiled=True),
        lax.all_to_all(lag_real, "seq", split_axis=1, concat_axis=0, tiled=True),
        lax.all_to_all(lag_imag, "seq", split_axis=1, concat_axis=0, tiled=True),
    )
    corr_flat_real, corr_flat_imag = rotate_back(
        corr_real.reshape(seq_count, width_all),
        corr_imag.reshape(seq_count, width_all),
        twid_half_cos,
        twid_half_sin,
    )
    lag_flat_real, lag_flat_imag = rotate_back(
        lag_real.reshape(seq_count, width_all),
        lag_imag.reshape(seq_count, width_all),
        twid_half_cos,
        twid_half_sin,
    )
    cos_final, sin_final = angle_table(dev_ids, dev_ids, freq_count)
    cos_final = jnp.where(dev_ids[None, :] == 0, 1.0, 2.0 * cos_final)
    sin_final = jnp.where(dev_ids[None, :] == 0, -alternate[:, None], 2.0 * sin_final)
    conv_rows = (
        matmul_high(cos_final, corr_flat_real) - matmul_high(sin_final, corr_flat_imag)
    ) * scale_term
    lag_rows = (
        matmul_high(cos_final, lag_flat_real) - matmul_high(sin_final, lag_flat_imag)
    ) * scale_term
    conv_back, lag_back = (
        lax.all_to_all(conv_rows, "seq", split_axis=0, concat_axis=0, tiled=True),
        lax.all_to_all(lag_rows, "seq", split_axis=0, concat_axis=0, tiled=True),
    )

    def to_channels(values):
        return (
            values.reshape(seq_count, channels, block_len)
            .transpose(1, 0, 2)
            .reshape(channels, local_len)
        )

    conv_grad = to_channels(conv_back)
    filt_grad = to_channels(lag_back)
    in_grad = conv_grad + local_bias[:, None] * out_grad
    weighted = filt_grad * window
    regrouped = lax.all_to_all(weighted, "ch", split_axis=1, concat_axis=0, tiled=True)
    feat_grad = matmul_high(filter_weight, regrouped)
    return (in_grad, feat_grad)


lanes = 128


def split_table(table):
    table = np.asarray(table, np.float32)
    high_part = table.astype(jnp.bfloat16)
    low_part = (table - high_part.astype(np.float32)).astype(jnp.bfloat16)
    return np.stack([high_part, low_part])


def make_tables(data_rows):
    freq_rows = 2 * data_rows
    padded_len = freq_rows * lanes
    odd_ids = 2 * np.arange(data_rows) + 1
    row_angle = (odd_ids[:, None] * np.arange(data_rows)[None, :] % (2 * freq_rows)) * (
        math.pi / freq_rows
    )
    row_table = np.concatenate([np.cos(row_angle), -np.sin(row_angle)], axis=0)
    lane_ids = np.arange(lanes)
    twist_angle = (odd_ids[:, None] * lane_ids[None, :]) * (math.pi / padded_len)
    twist = np.stack([np.cos(twist_angle), -np.sin(twist_angle)]).astype(np.float32)
    lane_angle = (lane_ids[:, None] * lane_ids[None, :] % lanes) * (2.0 * math.pi / lanes)
    lane_cos, lane_sin = np.cos(lane_angle), np.sin(lane_angle)
    lane_table = np.block([[lane_cos, -lane_sin], [lane_sin, lane_cos]])
    back_table = np.block([[lane_cos, lane_sin], [-lane_sin, lane_cos]]) * (2.0 / padded_len)
    return (
        split_table(row_table),
        split_table(row_table.T),
        split_table(lane_table),
        split_table(back_table),
        twist,
    )


def split_value(value):
    high_part = value.astype(jnp.bfloat16)
    return high_part, (value - high_part.astype(jnp.float32)).astype(jnp.bfloat16)


def dot_split(left, right):
    def product(first, second):
        return jnp.dot(first, second, preferred_element_type=jnp.float32)

    return product(left[0], right[0]) + (product(left[0], right[1]) + product(left[1], right[0]))


def correlate(pieces, row_ref, row_back_ref, lane_ref, lane_back_ref, twist_ref):
    data_rows = pieces[0].shape[0]
    twist_cos, twist_sin = twist_ref[0], twist_ref[1]
    packed = jnp.concatenate(pieces, axis=1)
    spread = dot_split((row_ref[0], row_ref[1]), split_value(packed))
    freqs = []
    for which in range(3):
        re_part = spread[:data_rows, which * lanes : (which + 1) * lanes]
        im_part = spread[data_rows:, which * lanes : (which + 1) * lanes]
        turned = jnp.concatenate(
            [
                re_part * twist_cos - im_part * twist_sin,
                re_part * twist_sin + im_part * twist_cos,
            ],
            axis=1,
        )
        freqs.append(dot_split(split_value(turned), (lane_ref[0], lane_ref[1])))
    grad_re, grad_im = freqs[0][:, :lanes], freqs[0][:, lanes:]

    def inverse(spectrum):
        re_part, im_part = spectrum[:, :lanes], spectrum[:, lanes:]
        product = jnp.concatenate(
            [
                re_part * grad_re + im_part * grad_im,
                re_part * grad_im - im_part * grad_re,
            ],
            axis=1,
        )
        back = dot_split(split_value(product), (lane_back_ref[0], lane_back_ref[1]))
        re_part, im_part = back[:, :lanes], back[:, lanes:]
        return jnp.concatenate(
            [
                re_part * twist_cos + im_part * twist_sin,
                im_part * twist_cos - re_part * twist_sin,
            ],
            axis=0,
        )

    both = jnp.concatenate([inverse(freqs[2]), inverse(freqs[1])], axis=1)
    return dot_split((row_back_ref[0], row_back_ref[1]), split_value(both))


def plan(seq_count, channels):
    half = seq_count // 2
    mixed = channels // 8
    inner = half // 2
    return half, inner, mixed, mixed // max(inner, 1), (channels - mixed) // half


def whole_kernel(sizes, *refs):
    (
        grad_hbm,
        input_hbm,
        feat_hbm,
        weight_ref,
        rate_ref,
        bias_ref,
        row_hbm,
        row_back_hbm,
        lane_hbm,
        lane_back_hbm,
        twist_hbm,
        half_row_hbm,
        half_back_hbm,
        half_twist_hbm,
        in_grad_ref,
        feat_grad_ref,
        grad_ref,
        input_ref,
        feat_ref,
        row_ref,
        row_back_ref,
        lane_ref,
        lane_back_ref,
        twist_ref,
        half_row_ref,
        half_back_ref,
        half_twist_ref,
        load_sem,
        send_buf,
        gather_full,
        gather_half,
        conv_send,
        lag_send,
        conv_recv,
        lag_recv,
        window_buf,
        rate_buf,
        bias_buf,
        weight_buf,
        ruler,
        full_sem,
        half_sem,
        send_sem,
        back_sem,
    ) = refs
    seq_count, ch_count, channels, rows = sizes
    half, inner, mixed, mixed_per, per = plan(seq_count, channels)
    data_rows = rows * seq_count
    sub_rows = rows // ch_count
    all_channels = channels * ch_count
    total = seq_count * ch_count
    left_total = half * ch_count
    full_len = data_rows * lanes
    seq_place = lax.axis_index("seq")
    ch_place = lax.axis_index("ch")
    flat_place = seq_place * ch_count + ch_place
    on_right = seq_place >= half
    on_left = seq_place < half
    on_inner = jnp.logical_and(seq_place >= inner, on_left)
    on_outer = seq_place < inner
    side_place = lax.rem(seq_place, half)
    here = {"seq": seq_place, "ch": ch_place}

    loads = [
        pltpu.make_async_copy(source, target, load_sem.at[index])
        for index, (source, target) in enumerate(
            (
                (grad_hbm, grad_ref),
                (input_hbm, input_ref),
                (feat_hbm, feat_ref),
                (row_hbm, row_ref),
                (twist_hbm, twist_ref),
                (lane_hbm, lane_ref),
                (lane_back_hbm, lane_back_ref),
                (row_back_hbm, row_back_ref),
                (half_row_hbm, half_row_ref),
                (half_back_hbm, half_back_ref),
                (half_twist_hbm, half_twist_ref),
            )
        )
    ]
    barrier = pltpu.get_barrier_semaphore()

    def greet(step, carry):
        other = lax.rem(flat_place + step, total)
        pl.semaphore_signal(
            barrier,
            inc=1,
            device_id={"seq": other // ch_count, "ch": lax.rem(other, ch_count)},
            device_id_type=pl.DeviceIdType.MESH,
        )
        return carry

    lax.fori_loop(1, total, greet, 0)
    for load in loads:
        load.start()

    def each_other(place, count, visit, first=1):
        def one(step, carry):
            visit(lax.rem(place + step, count))
            return carry

        lax.fori_loop(first, count, one, 0)

    def remote(source, target, send, recv, device):
        return pltpu.make_async_remote_copy(
            src_ref=source,
            dst_ref=target,
            send_sem=send,
            recv_sem=recv,
            device_id=device,
            device_id_type=pl.DeviceIdType.MESH,
        )

    def counted(count, send, recv):
        part = ruler.at[pl.ds(0, count)]
        return remote(part, part, send, recv, here)

    def rows_of(channel):
        return pl.ds(pl.multiple_of(channel * rows, 8), rows)

    def split_channel(side, chan):
        return mixed + side * per + chan

    def full_copy(first, last, channel, slot, target, sem):
        return remote(
            send_buf.at[first:last, rows_of(channel)],
            gather_full.at[first:last, slot, rows_of(seq_place)],
            send_sem.at[sem],
            full_sem.at[slot],
            {"seq": target, "ch": ch_place},
        )

    def half_copy(first, last, channel, slot, target):
        return remote(
            send_buf.at[first:last, rows_of(channel)],
            gather_half.at[first:last, slot, rows_of(side_place)],
            send_sem.at[1],
            half_sem.at[slot],
            {"seq": target, "ch": ch_place},
        )

    def send_mixed(first, last):
        for side in range(inner):
            target = inner + side

            @pl.when(seq_place != target)
            def _():
                for slot in range(mixed_per):
                    channel = side * mixed_per + slot
                    full_copy(first, last, channel, slot, target, 2).start()

    def send_split(first, last, chan):
        @pl.when(on_left)
        def _():
            for step in range(half):
                side = step // 2 * 2 + lax.rem(step + seq_place, 2)
                full_copy(
                    max(first, 1), last, split_channel(side, chan), chan, half + side, 0
                ).start()
            each_other(
                side_place,
                half,
                lambda side: half_copy(
                    first, last, split_channel(side, chan), chan, side
                ).start(),
            )

        @pl.when(on_right)
        def _():
            each_other(
                side_place,
                half,
                lambda side: full_copy(
                    first, last, split_channel(side, chan), chan, half + side, 0
                ).start(),
            )

    def conv_copy(channel, slot, count, target):
        part = jnp.where(jnp.logical_and(on_right, target < half), channels, 0)
        return remote(
            conv_send.at[target, pl.ds(pl.multiple_of(slot * rows, 8), count * rows)],
            conv_recv.at[pl.ds(pl.multiple_of((part + channel) * rows, 8), count * rows)],
            send_sem.at[3],
            back_sem.at[0],
            {"seq": target, "ch": ch_place},
        )

    def lag_row(channel):
        return pl.multiple_of((ch_place * channels + channel) * sub_rows, 8)

    def lag_copy(channel, slot, count, target):
        part = jnp.where(jnp.logical_and(on_right, target < left_total), all_channels, 0)
        return remote(
            lag_send.at[target, pl.ds(pl.multiple_of(slot * sub_rows, 8), count * sub_rows)],
            lag_recv.at[
                pl.ds(
                    pl.multiple_of(part * sub_rows + lag_row(channel), 8), count * sub_rows
                )
            ],
            send_sem.at[4],
            back_sem.at[1],
            {"seq": target // ch_count, "ch": lax.rem(target, ch_count)},
        )

    def to_rows(which, index, tile):
        send_buf[which, pl.ds(index, channels, stride=rows), :] = tile

    rate_buf[...] = jnp.broadcast_to(rate_ref[...], (lanes, all_channels)).T
    weight_buf[...] = weight_ref[...].T
    loads[0].wait()
    for index in range(rows):
        to_rows(0, index, grad_ref[:, index * lanes : (index + 1) * lanes])
    loads[1].wait()
    for index in range(rows):
        to_rows(1, index, input_ref[:, index * lanes : (index + 1) * lanes])

    pl.semaphore_wait(barrier, total - 1)

    send_mixed(0, 2)
    send_split(0, 2, 0)

    first_chan = pl.multiple_of(ch_place * channels, 8)
    local_rates = rate_buf[pl.ds(first_chan, channels), :]
    local_weight = split_value(weight_buf[pl.ds(first_chan, channels), :])
    lane_ids = lax.broadcasted_iota(jnp.int32, (1, lanes), 1)

    def window_of(rates, first):
        steps_t = (first + lane_ids).astype(jnp.float32) / full_len
        return jnp.exp(-rates * steps_t) + shift_term

    bias_buf[...] = jnp.broadcast_to(bias_ref[...], (lanes, all_channels)).T
    loads[2].wait()
    chunk = math.gcd(rows, 4)
    for outer in range(rows // chunk):
        lo = outer * chunk * lanes
        block = split_value(feat_ref[:, lo : lo + chunk * lanes])
        values = dot_split(local_weight, block)
        for inside in range(chunk):
            index = outer * chunk + inside
            window = window_of(local_rates, (seq_place * rows + index) * lanes)
            to_rows(2, index, values[:, inside * lanes : (inside + 1) * lanes] * window)

    send_mixed(2, 3)
    send_split(2, 3, 0)

    def send_rest(chan, carry):
        send_split(0, 3, chan)
        return carry

    lax.fori_loop(1, jnp.where(on_right, 2, per), send_rest, 0)

    conv_recv[pl.ds(channels * rows, mixed * rows), :] = jnp.zeros(
        (mixed * rows, lanes), jnp.float32
    )
    for group in range(ch_count):
        lag_recv[pl.ds((all_channels + group * channels) * sub_rows, mixed * sub_rows), :] = (
            jnp.zeros((mixed * sub_rows, lanes), jnp.float32)
        )

    @pl.when(on_right)
    def _():
        conv_recv[pl.ds((channels + mixed) * rows, (channels - mixed) * rows), :] = jnp.zeros(
            ((channels - mixed) * rows, lanes), jnp.float32
        )
        for group in range(ch_count):
            lag_recv[
                pl.ds(
                    (all_channels + group * channels + mixed) * sub_rows,
                    (channels - mixed) * sub_rows,
                ),
                :,
            ] = jnp.zeros(((channels - mixed) * sub_rows, lanes), jnp.float32)

        def keep_own(chan, carry):
            gather_full[0, chan, pl.ds(0, half * rows), :] = jnp.zeros(
                (half * rows, lanes), jnp.float32
            )
            for which in range(3):
                gather_full[which, chan, rows_of(seq_place), :] = send_buf[
                    which, rows_of(split_channel(side_place, chan)), :
                ]
            return carry

        lax.fori_loop(0, per, keep_own, 0)

    @pl.when(on_left)
    def _():
        def keep_own(chan, carry):
            for which in range(3):
                gather_half[which, chan, rows_of(side_place), :] = send_buf[
                    which, rows_of(split_channel(side_place, chan)), :
                ]
            return carry

        lax.fori_loop(0, per, keep_own, 0)

    @pl.when(on_inner)
    def _():
        for slot in range(mixed_per):
            for which in range(3):
                gather_full[which, slot, rows_of(seq_place), :] = send_buf[
                    which, rows_of((seq_place - inner) * mixed_per + slot), :
                ]

    for index in range(sub_rows):
        window_buf[index] = window_of(rate_buf[...], (flat_place * sub_rows + index) * lanes)

    for load in loads[3:]:
        load.wait()

    def send_back(channel, slot, count, seq_targets, flat_targets):
        each_other(
            seq_place,
            seq_targets,
            lambda target: conv_copy(channel, slot, count, target).start(),
        )
        each_other(
            flat_place,
            flat_targets,
            lambda target: lag_copy(channel, slot, count, target).start(),
        )

    def work_full(chan, carry):
        @pl.when(on_right)
        def _():
            @pl.when(chan + 2 < per)
            def _():
                each_other(
                    side_place,
                    half,
                    lambda side: full_copy(
                        0, 3, split_channel(side, chan + 2), chan + 2, half + side, 0
                    ).start(),
                )

            counted((5 * half - 3) * rows, send_sem.at[0], full_sem.at[chan]).wait_recv()

        @pl.when(on_left)
        def _():
            counted(3 * (seq_count - 1) * rows, send_sem.at[0], full_sem.at[chan]).wait_recv()

        final = correlate(
            [gather_full[which, chan] for which in range(3)],
            row_ref,
            row_back_ref,
            lane_ref,
            lane_back_ref,
            twist_ref,
        )
        slot = jnp.where(on_right, chan, per + chan)
        channel = jnp.where(
            on_right,
            split_channel(side_place, chan),
            (seq_place - inner) * mixed_per + chan,
        )
        conv_send[:, pl.ds(pl.multiple_of(slot * rows, 8), rows), :] = final[:, :lanes].reshape(
            seq_count, rows, lanes
        )
        lag_send[:, pl.ds(pl.multiple_of(slot * sub_rows, 8), sub_rows), :] = final[
            :, lanes:
        ].reshape(total, sub_rows, lanes)

        alone = chan >= 0

        @pl.when(jnp.logical_and(on_right, alone))
        def _():
            send_back(channel, slot, 1, seq_count, total)

        @pl.when(
            jnp.logical_or(
                jnp.logical_and(
                    on_right, jnp.logical_and(lax.rem(chan, 2) == 0, jnp.logical_not(alone))
                ),
                jnp.logical_and(on_left, chan == 1),
            )
        )
        def _():
            send_back(channel - 1, slot - 1, 2, seq_count, total)

        return carry

    rounds = jnp.where(on_right, per, jnp.where(on_inner, mixed_per, 0))
    lax.fori_loop(0, rounds, work_full, 0)

    def work_half(chan, carry):
        counted(3 * (half - 1) * rows, send_sem.at[0], half_sem.at[chan]).wait_recv()
        final = correlate(
            [gather_half[which, chan] for which in range(3)],
            half_row_ref,
            half_back_ref,
            lane_ref,
            lane_back_ref,
            half_twist_ref,
        )
        channel = split_channel(side_place, chan)
        conv_send[:half, pl.ds(pl.multiple_of(chan * rows, 8), rows), :] = final[
            :, :lanes
        ].reshape(half, rows, lanes)
        lag_send[:left_total, pl.ds(pl.multiple_of(chan * sub_rows, 8), sub_rows), :] = final[
            :, lanes:
        ].reshape(left_total, sub_rows, lanes)

        @pl.when(lax.rem(chan, 2) == 1)
        def _():
            send_back(channel - 1, chan - 1, 2, half, left_total)

        @pl.when(chan == per - 1)
        def _():
            send_back(channel, chan, 1, half, left_total)

        return carry

    @pl.when(on_left)
    def _():
        lax.fori_loop(0, per, work_half, 0)

    def keep_back(channel, slot, count):
        conv_recv[pl.ds(pl.multiple_of(channel * rows, 8), count * rows), :] = conv_send[
            seq_place, pl.ds(pl.multiple_of(slot * rows, 8), count * rows), :
        ]
        lag_recv[pl.ds(lag_row(channel), count * sub_rows), :] = lag_send[
            flat_place, pl.ds(pl.multiple_of(slot * sub_rows, 8), count * sub_rows), :
        ]

    keep_back(split_channel(side_place, 0), 0, per)

    @pl.when(on_inner)
    def _():
        keep_back((seq_place - inner) * mixed_per, per, mixed_per)

    def expect(recv, unit, own_side, whole):
        for place, count in (
            (on_outer, own_side * per + whole * mixed_per + (own_side + 1) * per),
            (on_inner, own_side * per + (whole - 1) * mixed_per + (own_side + 1) * per),
            (on_right, own_side * per + whole * mixed_per),
        ):

            @pl.when(place)
            def _():
                counted(count * unit, send_sem.at[0], recv).wait_recv()

    def sent(index, outer_count, inner_count, right_count):
        for place, count in (
            (on_outer, outer_count),
            (on_inner, inner_count),
            (on_right, right_count),
        ):
            if count:

                @pl.when(place)
                def _():
                    counted(count, send_sem.at[index], back_sem.at[0]).wait_send()

    expect(back_sem.at[0], rows, half - 1, inner)
    local_bias = bias_buf[pl.ds(first_chan, channels), :]
    for index in range(rows):
        span = slice(index * lanes, (index + 1) * lanes)
        in_grad_ref[:, span] = (
            conv_recv[pl.ds(index, channels, stride=rows), :]
            + conv_recv[pl.ds(channels * rows + index, channels, stride=rows), :]
            + local_bias * grad_ref[:, span]
        )

    to_left = 2 * half * per * rows
    own_side = 3 * (half - 1) * per * rows
    to_inner = 3 * mixed * rows
    to_inner_own = 3 * (mixed - mixed_per) * rows
    sent(0, to_left, to_left, own_side)
    sent(1, own_side, own_side, 0)
    sent(2, to_inner, to_inner_own, to_inner)
    side_back = (half - 1) * per * rows
    sent(
        3,
        side_back,
        side_back + (seq_count - 1) * mixed_per * rows,
        (seq_count - 1) * per * rows,
    )
    side_lag = (left_total - 1) * per * sub_rows
    sent(
        4,
        side_lag,
        side_lag + (total - 1) * mixed_per * sub_rows,
        (total - 1) * per * sub_rows,
    )
    expect(back_sem.at[1], sub_rows, left_total - 1, inner * ch_count)
    weight = split_value(weight_ref[...])
    for index in range(sub_rows):
        tile = (
            lag_recv[pl.ds(index, all_channels, stride=sub_rows), :]
            + lag_recv[pl.ds(all_channels * sub_rows + index, all_channels, stride=sub_rows), :]
        ) * window_buf[index]
        feat_grad_ref[:, index * lanes : (index + 1) * lanes] = dot_split(
            weight, split_value(tile)
        )


def local_whole(seq_count, ch_count, tables, *args):
    out_grad, gated_input, features, filter_weight, rates, skip_bias = args
    channels, local_len = out_grad.shape
    rows = local_len // lanes
    feats, all_channels = filter_weight.shape
    half, inner, mixed, mixed_per, per = plan(seq_count, channels)
    slots = per + mixed_per
    data_rows = rows * seq_count
    sub_rows = rows // ch_count
    total = seq_count * ch_count
    sizes = (seq_count, ch_count, channels, rows)
    in_vmem = pl.BlockSpec(memory_space=pltpu.VMEM)
    anywhere = pl.BlockSpec(memory_space=pl.ANY)
    dma = pltpu.SemaphoreType.DMA
    f32 = jnp.float32
    longest = max(
        3 * channels * rows,
        2 * channels * rows,
        2 * all_channels * sub_rows,
        seq_count * slots * rows,
        total * slots * sub_rows,
    )
    held = pl.pallas_call(
        functools.partial(whole_kernel, sizes),
        out_shape=(
            pltpu.VMEM((channels, local_len), f32),
            pltpu.VMEM((feats, sub_rows * lanes), f32),
        ),
        in_specs=[anywhere] * 3 + [in_vmem] * 3 + [anywhere] * len(tables),
        out_specs=(in_vmem, in_vmem),
        scratch_shapes=[
            pltpu.VMEM((channels, local_len), f32),
            pltpu.VMEM((channels, local_len), f32),
            pltpu.VMEM((feats, local_len), f32),
            *[pltpu.VMEM(table.shape, table.dtype) for table in tables],
            dma((3 + len(tables),)),
            pltpu.VMEM((3, channels * rows, lanes), f32),
            pltpu.VMEM((3, per, data_rows, lanes), f32),
            pltpu.VMEM((3, per, half * rows, lanes), f32),
            pltpu.VMEM((seq_count, slots * rows, lanes), f32),
            pltpu.VMEM((total, slots * sub_rows, lanes), f32),
            pltpu.VMEM((2 * channels * rows, lanes), f32),
            pltpu.VMEM((2 * all_channels * sub_rows, lanes), f32),
            pltpu.VMEM((sub_rows, all_channels, lanes), f32),
            pltpu.VMEM((all_channels, lanes), f32),
            pltpu.VMEM((all_channels, lanes), f32),
            pltpu.VMEM((all_channels, feats), f32),
            pltpu.VMEM((longest, lanes), f32),
            dma((per,)),
            dma((per,)),
            dma((5,)),
            dma((2,)),
        ],
        compiler_params=pltpu.CompilerParams(collective_id=0, has_side_effects=True),
    )(
        out_grad,
        gated_input,
        features,
        filter_weight,
        rates.reshape(1, all_channels),
        skip_bias.reshape(1, all_channels),
        *[jnp.asarray(table) for table in tables],
    )
    held = [pltpu.with_memory_space_constraint(value, pltpu.VMEM) for value in held]
    return pl.pallas_call(
        store_kernel,
        out_shape=tuple(jax.ShapeDtypeStruct(value.shape, f32) for value in held),
        in_specs=[in_vmem] * 2,
        out_specs=(anywhere, anywhere),
        scratch_shapes=[dma((2,))],
    )(*held)


def store_kernel(first_ref, second_ref, first_hbm, second_hbm, sem):
    stores = [
        pltpu.make_async_copy(first_ref, first_hbm, sem.at[0]),
        pltpu.make_async_copy(second_ref, second_hbm, sem.at[1]),
    ]
    for store in stores:
        store.start()
    for store in stores:
        store.wait()


def solution(mesh):
    seq_count, ch_count = mesh.shape["seq"], mesh.shape["ch"]
    in_specs = (P("ch", "seq"), P("ch", "seq"), P(None, "seq"), P(), P(), P())
    out_specs = (P("ch", "seq"), P(None, ("seq", "ch")))

    def whole(*args):
        channels, full_len = args[0].shape
        channels = channels // ch_count
        local_len = full_len // seq_count
        half, inner, mixed, mixed_per, per = plan(seq_count, channels)
        fits = (
            seq_count % 4 == 0
            and channels % 8 == 0
            and mixed == inner * mixed_per
            and mixed_per == 2
            and mixed + half * per == channels
            and per % 2 == 1
            and per >= 5
            and local_len % (8 * lanes * ch_count) == 0
            and full_len <= 512 * lanes
        )
        body = local
        if fits:
            row, row_back, lane, lane_back, twist = make_tables(full_len // lanes)
            half_row, half_back, _, _, half_twist = make_tables(full_len // lanes // 2)
            tables = (row, row_back, lane, lane_back, twist, half_row, half_back * 2, half_twist)
            body = functools.partial(local_whole, seq_count, ch_count, tables)
        return jax.shard_map(
            body, mesh=mesh, in_specs=in_specs, out_specs=out_specs, check_vma=False
        )(*args)

    return whole
```

```python
import functools
import math

import jax
import jax.numpy as jnp
import numpy as np
from jax import lax
from jax.experimental import pallas as pl
from jax.experimental.pallas import tpu as pltpu
from jax.sharding import PartitionSpec as P

shift_term = 0.05
highest = lax.Precision.HIGHEST


def matmul_high(operand, matrix):
    return jnp.dot(operand, matrix, precision=highest, preferred_element_type=jnp.float32)


def angle_table(first_ids, second_ids, period):
    product = first_ids[:, None] * second_ids[None, :] % period
    angles = product.astype(jnp.float32) * (2.0 * math.pi / period)
    return (jnp.cos(angles), jnp.sin(angles))


def contract(real_part, imag_part, cos_table, sin_table, einsum_form):

    def multiply_by(operand, matrix):
        return jnp.einsum(
            einsum_form, operand, matrix, precision=highest, preferred_element_type=jnp.float32
        )

    return (
        multiply_by(real_part, cos_table) - multiply_by(imag_part, sin_table),
        multiply_by(real_part, sin_table) + multiply_by(imag_part, cos_table),
    )


def group_width(channels, block_len):
    return math.gcd(channels, max(1, 128 // block_len)) * block_len


def group_table(width, block_len, sign_term):
    ids = jnp.arange(width, dtype=jnp.int32)
    same = ids[:, None] // block_len == ids[None, :] // block_len
    inner = ids % block_len
    product = inner[:, None] * inner[None, :] % block_len
    angles = product.astype(jnp.float32) * (2.0 * math.pi / block_len)
    return (
        jnp.where(same, jnp.cos(angles), 0.0).astype(jnp.float32),
        jnp.where(same, sign_term * jnp.sin(angles), 0.0).astype(jnp.float32),
    )


def local_transform(real_part, imag_part, block_len, inverse):
    rows, seq_count, width_all = real_part.shape
    channels = width_all // block_len
    local_len = seq_count * block_len
    width = group_width(channels, block_len)
    sign_term = 1.0 if inverse else -1.0
    seq_ids = jnp.arange(seq_count, dtype=jnp.int32)
    block_ids = jnp.arange(block_len, dtype=jnp.int32)
    cos_seq, sin_seq = angle_table(seq_ids, seq_ids, seq_count)
    sin_seq = sign_term * sin_seq
    cos_twist, sin_twist = angle_table(seq_ids, block_ids, local_len)
    cos_twist = jnp.tile(cos_twist, (1, channels))
    sin_twist = sign_term * jnp.tile(sin_twist, (1, channels))
    cos_group, sin_group = group_table(width, block_len, sign_term)
    grouped = (rows, seq_count, width_all // width, width)
    flat = (rows, seq_count, width_all)

    def twist(re_part, im_part):
        return (
            re_part * cos_twist - im_part * sin_twist,
            re_part * sin_twist + im_part * cos_twist,
        )

    def across_groups(re_part, im_part):
        re_part, im_part = contract(
            re_part.reshape(grouped),
            im_part.reshape(grouped),
            cos_group,
            sin_group,
            "rkgm,mq->rkgq",
        )
        return (re_part.reshape(flat), im_part.reshape(flat))

    if inverse:
        real_part, imag_part = across_groups(real_part, imag_part)
        real_part, imag_part = twist(real_part, imag_part)
        real_part, imag_part = contract(real_part, imag_part, cos_seq, sin_seq, "rsx,sk->rkx")
    else:
        real_part, imag_part = contract(real_part, imag_part, cos_seq, sin_seq, "rsx,sk->rkx")
        real_part, imag_part = twist(real_part, imag_part)
        real_part, imag_part = across_groups(real_part, imag_part)
    return (real_part, imag_part)


def first_section(row_block, cos_fwd, sin_fwd, twid_cos, twid_sin):
    real_part = matmul_high(cos_fwd, row_block)
    imag_part = -matmul_high(sin_fwd, row_block)
    real_out = real_part * twid_cos + imag_part * twid_sin
    imag_out = imag_part * twid_cos - real_part * twid_sin
    return (real_out[:, None, :], imag_out[:, None, :])


def rotate_back(real_part, imag_part, twid_cos, twid_sin):
    return (
        real_part * twid_cos - imag_part * twid_sin,
        real_part * twid_sin + imag_part * twid_cos,
    )


def forward_products(
    block_len, grad_real, grad_imag, input_real, input_imag, filter_real, filter_imag
):
    grad_real, grad_imag = local_transform(grad_real, grad_imag, block_len, False)
    input_real, input_imag = local_transform(input_real, input_imag, block_len, False)
    filter_real, filter_imag = local_transform(filter_real, filter_imag, block_len, False)
    corr_real = filter_real * grad_real + filter_imag * grad_imag
    corr_imag = filter_real * grad_imag - filter_imag * grad_real
    lag_real = input_real * grad_real + input_imag * grad_imag
    lag_imag = input_real * grad_imag - input_imag * grad_real
    return (corr_real, corr_imag, lag_real, lag_imag)


def products_inverted(block_len, operands):
    corr_real, corr_imag, lag_real, lag_imag = forward_products(block_len, *operands)
    corr_real, corr_imag = local_transform(corr_real, corr_imag, block_len, True)
    lag_real, lag_imag = local_transform(lag_real, lag_imag, block_len, True)
    return (corr_real, corr_imag, lag_real, lag_imag)


def paired_rows(block_len, operands):
    seq_count = operands[0].shape[1]
    channels = operands[0].shape[2] // block_len
    local_len = seq_count * block_len
    positions = (
        jnp.arange(seq_count, dtype=jnp.int32)[:, None] * block_len
        + jnp.arange(block_len, dtype=jnp.int32)[None, :]
    )
    angles = positions.astype(jnp.float32) * (math.pi / local_len)
    half_cos = jnp.tile(jnp.cos(angles), (1, channels))
    half_sin = jnp.tile(jnp.sin(angles), (1, channels))
    stacked = []
    for index in range(3):
        low_row = operands[2 * index]
        high_row = operands[2 * index + 1]
        stacked.append(jnp.concatenate([low_row, high_row * half_cos], axis=0))
        stacked.append(jnp.concatenate([jnp.zeros_like(low_row), -high_row * half_sin], axis=0))
    corr_real, corr_imag, lag_real, lag_imag = products_inverted(block_len, tuple(stacked))
    return (
        corr_real[0:1],
        corr_real[1:2] * half_cos - corr_imag[1:2] * half_sin,
        lag_real[0:1],
        lag_real[1:2] * half_cos - lag_imag[1:2] * half_sin,
    )


def local(out_grad, gated_input, features, filter_weight, rates, skip_bias):
    channels, local_len = out_grad.shape
    seq_count = lax.axis_size("seq")
    block_len = local_len // seq_count
    width_all = channels * block_len
    freq_count = 2 * seq_count
    full_len = local_len * seq_count
    padded_len = 2 * full_len
    seq_place = lax.axis_index("seq")
    first_chan = lax.axis_index("ch") * channels
    local_rates = lax.dynamic_slice_in_dim(rates, first_chan, channels)
    local_bias = lax.dynamic_slice_in_dim(skip_bias, first_chan, channels)
    local_weight = lax.dynamic_slice_in_dim(filter_weight, first_chan, channels, 1)
    position = seq_place * local_len + jnp.arange(local_len, dtype=jnp.int32)
    window = (
        jnp.exp(-local_rates[:, None] * (position.astype(jnp.float32) / full_len)[None, :])
        + shift_term
    )
    filter_vals = matmul_high(local_weight.T, features) * window

    def to_rows(values):
        return (
            values.reshape(channels, seq_count, block_len)
            .transpose(1, 0, 2)
            .reshape(seq_count, width_all)
        )

    received = (
        lax.all_to_all(to_rows(out_grad), "seq", split_axis=0, concat_axis=0, tiled=True),
        lax.all_to_all(to_rows(gated_input), "seq", split_axis=0, concat_axis=0, tiled=True),
        lax.all_to_all(to_rows(filter_vals), "seq", split_axis=0, concat_axis=0, tiled=True),
    )

    def inverted(operands):
        return products_inverted(block_len, operands)

    def paired(operands):
        return paired_rows(block_len, operands)

    freq_ids = jnp.arange(freq_count, dtype=jnp.int32)
    dev_ids = jnp.arange(seq_count, dtype=jnp.int32)
    local_m = seq_place * block_len + jnp.arange(block_len, dtype=jnp.int32)
    twid_cos, twid_sin = angle_table(freq_ids, local_m, padded_len)
    twid_cos = jnp.tile(twid_cos, (1, channels))
    twid_sin = jnp.tile(twid_sin, (1, channels))
    scale_term = 1.0 / padded_len
    alternate = jnp.where(dev_ids % 2 == 0, 1.0, -1.0).astype(jnp.float32)
    cos_half, sin_half = angle_table(dev_ids, dev_ids, freq_count)
    sin_half = jnp.where(dev_ids[:, None] == 0, -alternate[None, :], sin_half)
    twid_half_cos = twid_cos[:seq_count]
    twid_half_sin = twid_sin[:seq_count]
    spread = [
        first_section(piece, cos_half, sin_half, twid_half_cos, twid_half_sin) for piece in received
    ]
    exchanged = (
        lax.all_to_all(spread[0][0], "seq", split_axis=0, concat_axis=1, tiled=True),
        lax.all_to_all(spread[0][1], "seq", split_axis=0, concat_axis=1, tiled=True),
        lax.all_to_all(spread[1][0], "seq", split_axis=0, concat_axis=1, tiled=True),
        lax.all_to_all(spread[1][1], "seq", split_axis=0, concat_axis=1, tiled=True),
        lax.all_to_all(spread[2][0], "seq", split_axis=0, concat_axis=1, tiled=True),
        lax.all_to_all(spread[2][1], "seq", split_axis=0, concat_axis=1, tiled=True),
    )
    corr_real, corr_imag, lag_real, lag_imag = lax.cond(
        seq_place == 0, paired, inverted, tuple(exchanged)
    )
    corr_real, corr_imag, lag_real, lag_imag = (
        lax.all_to_all(corr_real, "seq", split_axis=1, concat_axis=0, tiled=True),
        lax.all_to_all(corr_imag, "seq", split_axis=1, concat_axis=0, tiled=True),
        lax.all_to_all(lag_real, "seq", split_axis=1, concat_axis=0, tiled=True),
        lax.all_to_all(lag_imag, "seq", split_axis=1, concat_axis=0, tiled=True),
    )
    corr_flat_real, corr_flat_imag = rotate_back(
        corr_real.reshape(seq_count, width_all),
        corr_imag.reshape(seq_count, width_all),
        twid_half_cos,
        twid_half_sin,
    )
    lag_flat_real, lag_flat_imag = rotate_back(
        lag_real.reshape(seq_count, width_all),
        lag_imag.reshape(seq_count, width_all),
        twid_half_cos,
        twid_half_sin,
    )
    cos_final, sin_final = angle_table(dev_ids, dev_ids, freq_count)
    cos_final = jnp.where(dev_ids[None, :] == 0, 1.0, 2.0 * cos_final)
    sin_final = jnp.where(dev_ids[None, :] == 0, -alternate[:, None], 2.0 * sin_final)
    conv_rows = (
        matmul_high(cos_final, corr_flat_real) - matmul_high(sin_final, corr_flat_imag)
    ) * scale_term
    lag_rows = (
        matmul_high(cos_final, lag_flat_real) - matmul_high(sin_final, lag_flat_imag)
    ) * scale_term
    conv_back, lag_back = (
        lax.all_to_all(conv_rows, "seq", split_axis=0, concat_axis=0, tiled=True),
        lax.all_to_all(lag_rows, "seq", split_axis=0, concat_axis=0, tiled=True),
    )

    def to_channels(values):
        return (
            values.reshape(seq_count, channels, block_len)
            .transpose(1, 0, 2)
            .reshape(channels, local_len)
        )

    conv_grad = to_channels(conv_back)
    filt_grad = to_channels(lag_back)
    in_grad = conv_grad + local_bias[:, None] * out_grad
    weighted = filt_grad * window
    regrouped = lax.all_to_all(weighted, "ch", split_axis=1, concat_axis=0, tiled=True)
    feat_grad = matmul_high(filter_weight, regrouped)
    return (in_grad, feat_grad)


lanes = 128


def split_table(table):
    table = np.asarray(table, np.float32)
    high_part = table.astype(jnp.bfloat16)
    low_part = (table - high_part.astype(np.float32)).astype(jnp.bfloat16)
    return np.stack([high_part, low_part])


def make_tables(data_rows):
    freq_rows = 2 * data_rows
    padded_len = freq_rows * lanes
    odd_ids = 2 * np.arange(data_rows) + 1
    row_angle = (odd_ids[:, None] * np.arange(data_rows)[None, :] % (2 * freq_rows)) * (
        math.pi / freq_rows
    )
    row_table = np.concatenate([np.cos(row_angle), -np.sin(row_angle)], axis=0)
    lane_ids = np.arange(lanes)
    twist_angle = (odd_ids[:, None] * lane_ids[None, :]) * (math.pi / padded_len)
    twist = np.stack([np.cos(twist_angle), -np.sin(twist_angle)]).astype(np.float32)
    lane_angle = (lane_ids[:, None] * lane_ids[None, :] % lanes) * (2.0 * math.pi / lanes)
    lane_cos, lane_sin = np.cos(lane_angle), np.sin(lane_angle)
    lane_table = np.block([[lane_cos, -lane_sin], [lane_sin, lane_cos]])
    back_table = np.block([[lane_cos, lane_sin], [-lane_sin, lane_cos]]) * (2.0 / padded_len)
    return (
        split_table(row_table),
        split_table(row_table.T),
        split_table(lane_table),
        split_table(back_table),
        twist,
    )


def split_value(value):
    high_part = value.astype(jnp.bfloat16)
    return high_part, (value - high_part.astype(jnp.float32)).astype(jnp.bfloat16)


def dot_split(left, right):
    def product(first, second):
        return jnp.dot(first, second, preferred_element_type=jnp.float32)

    return product(left[0], right[0]) + (product(left[0], right[1]) + product(left[1], right[0]))


def spectra(pieces, tables):
    row_ref, lane_ref, twist_ref = tables[0], tables[2], tables[4]
    data_rows = pieces[0].shape[0]
    twist_cos, twist_sin = twist_ref[0], twist_ref[1]
    packed = pieces[0] if len(pieces) == 1 else jnp.concatenate(pieces, axis=1)
    spread = dot_split((row_ref[0], row_ref[1]), split_value(packed))
    freqs = []
    for which in range(len(pieces)):
        re_part = spread[:data_rows, which * lanes : (which + 1) * lanes]
        im_part = spread[data_rows:, which * lanes : (which + 1) * lanes]
        turned = jnp.concatenate(
            [
                re_part * twist_cos - im_part * twist_sin,
                re_part * twist_sin + im_part * twist_cos,
            ],
            axis=1,
        )
        freqs.append(dot_split(split_value(turned), (lane_ref[0], lane_ref[1])))
    return freqs


def correlated(grad_freqs, others, tables):
    row_back_ref, lane_back_ref, twist_ref = tables[1], tables[3], tables[4]
    twist_cos, twist_sin = twist_ref[0], twist_ref[1]
    grad_re, grad_im = grad_freqs[:, :lanes], grad_freqs[:, lanes:]
    turned = []
    for spectrum in others:
        re_part, im_part = spectrum[:, :lanes], spectrum[:, lanes:]
        product = jnp.concatenate(
            [
                re_part * grad_re + im_part * grad_im,
                re_part * grad_im - im_part * grad_re,
            ],
            axis=1,
        )
        back = dot_split(split_value(product), (lane_back_ref[0], lane_back_ref[1]))
        re_part, im_part = back[:, :lanes], back[:, lanes:]
        turned.append(
            jnp.concatenate(
                [
                    re_part * twist_cos + im_part * twist_sin,
                    im_part * twist_cos - re_part * twist_sin,
                ],
                axis=0,
            )
        )
    both = turned[0] if len(turned) == 1 else jnp.concatenate(turned, axis=1)
    return dot_split((row_back_ref[0], row_back_ref[1]), split_value(both))


def plan(seq_count, channels):
    half = seq_count // 2
    mixed = channels // 8
    inner = half // 2
    return half, inner, mixed, mixed // max(inner, 1), (channels - mixed) // half


def whole_kernel(sizes, *refs):
    (
        grad_hbm,
        input_hbm,
        feat_hbm,
        weight_ref,
        rate_ref,
        bias_ref,
        row_hbm,
        row_back_hbm,
        lane_hbm,
        lane_back_hbm,
        twist_hbm,
        half_row_hbm,
        half_back_hbm,
        half_twist_hbm,
        in_grad_ref,
        feat_grad_ref,
        grad_ref,
        input_ref,
        feat_ref,
        row_ref,
        row_back_ref,
        lane_ref,
        lane_back_ref,
        twist_ref,
        half_row_ref,
        half_back_ref,
        half_twist_ref,
        load_sem,
        send_buf,
        gather_full,
        gather_half,
        conv_send,
        lag_send,
        conv_recv,
        lag_recv,
        window_buf,
        rate_buf,
        bias_buf,
        weight_buf,
        ruler,
        grad_freqs,
        full_sem,
        filt_sem,
        half_sem,
        send_sem,
        back_sem,
        met_sem,
    ) = refs
    seq_count, ch_count, channels, rows = sizes
    half, inner, mixed, mixed_per, per = plan(seq_count, channels)
    data_rows = rows * seq_count
    sub_rows = rows // ch_count
    all_channels = channels * ch_count
    total = seq_count * ch_count
    left_total = half * ch_count
    full_len = data_rows * lanes
    seq_place = lax.axis_index("seq")
    ch_place = lax.axis_index("ch")
    flat_place = seq_place * ch_count + ch_place
    on_right = seq_place >= half
    on_left = seq_place < half
    on_inner = jnp.logical_and(seq_place >= inner, on_left)
    on_outer = seq_place < inner
    side_place = lax.rem(seq_place, half)
    here = {"seq": seq_place, "ch": ch_place}

    loads = [
        pltpu.make_async_copy(source, target, load_sem.at[index])
        for index, (source, target) in enumerate(
            (
                (grad_hbm, grad_ref),
                (input_hbm, input_ref),
                (feat_hbm, feat_ref),
                (row_hbm, row_ref),
                (twist_hbm, twist_ref),
                (lane_hbm, lane_ref),
                (lane_back_hbm, lane_back_ref),
                (row_back_hbm, row_back_ref),
                (half_row_hbm, half_row_ref),
                (half_back_hbm, half_back_ref),
                (half_twist_hbm, half_twist_ref),
            )
        )
    ]
    barrier = pltpu.get_barrier_semaphore()

    def signal(sem, seq, ch):
        pl.semaphore_signal(
            sem, inc=1, device_id={"seq": seq, "ch": ch}, device_id_type=pl.DeviceIdType.MESH
        )

    for step in range(1, seq_count):
        signal(barrier, lax.rem(seq_place + step, seq_count), ch_place)
    for step in range(1, ch_count):
        signal(barrier, seq_place, lax.rem(ch_place + step, ch_count))
    for load in loads:
        load.start()

    def each_other(place, count, visit, first=1):
        def one(step, carry):
            visit(lax.rem(place + step, count))
            return carry

        lax.fori_loop(first, count, one, 0)

    def remote(source, target, send, recv, device):
        return pltpu.make_async_remote_copy(
            src_ref=source,
            dst_ref=target,
            send_sem=send,
            recv_sem=recv,
            device_id=device,
            device_id_type=pl.DeviceIdType.MESH,
        )

    def counted(count, send, recv):
        part = ruler.at[pl.ds(0, count)]
        return remote(part, part, send, recv, here)

    def rows_of(channel):
        return pl.ds(pl.multiple_of(channel * rows, 8), rows)

    def split_channel(side, chan):
        return mixed + side * per + chan

    def full_copy(first, last, channel, slot, target, sem):
        return remote(
            send_buf.at[first:last, rows_of(channel)],
            gather_full.at[first:last, slot, rows_of(seq_place)],
            send_sem.at[sem],
            (filt_sem if first == 2 else full_sem).at[slot],
            {"seq": target, "ch": ch_place},
        )

    def half_copy(first, last, channel, slot, target):
        return remote(
            send_buf.at[first:last, rows_of(channel)],
            gather_half.at[first:last, slot, rows_of(side_place)],
            send_sem.at[1],
            half_sem.at[slot],
            {"seq": target, "ch": ch_place},
        )

    def send_mixed(first, last):
        for side in range(inner):
            target = inner + side

            @pl.when(seq_place != target)
            def _():
                for slot in range(mixed_per):
                    channel = side * mixed_per + slot
                    full_copy(first, last, channel, slot, target, 2).start()

    def to_right(first, last, chan):
        @pl.when(on_left)
        def _():
            for step in range(half):
                side = step // 2 * 2 + lax.rem(step + seq_place, 2)
                full_copy(
                    max(first, 1), last, split_channel(side, chan), chan, half + side, 0
                ).start()

        @pl.when(on_right)
        def _():
            each_other(
                side_place,
                half,
                lambda side: full_copy(
                    first, last, split_channel(side, chan), chan, half + side, 0
                ).start(),
            )

    def to_left(first, last, chan):
        @pl.when(on_left)
        def _():
            each_other(
                side_place,
                half,
                lambda side: half_copy(
                    first, last, split_channel(side, chan), chan, side
                ).start(),
            )

    def conv_copy(channel, slot, count, target):
        part = jnp.where(jnp.logical_and(on_right, target < half), channels, 0)
        return remote(
            conv_send.at[target, pl.ds(pl.multiple_of(slot * rows, 8), count * rows)],
            conv_recv.at[pl.ds(pl.multiple_of((part + channel) * rows, 8), count * rows)],
            send_sem.at[3],
            back_sem.at[0],
            {"seq": target, "ch": ch_place},
        )

    def lag_row(channel):
        return pl.multiple_of((ch_place * channels + channel) * sub_rows, 8)

    def lag_copy(channel, slot, count, target):
        part = jnp.where(jnp.logical_and(on_right, target < left_total), all_channels, 0)
        return remote(
            lag_send.at[target, pl.ds(pl.multiple_of(slot * sub_rows, 8), count * sub_rows)],
            lag_recv.at[
                pl.ds(
                    pl.multiple_of(part * sub_rows + lag_row(channel), 8), count * sub_rows
                )
            ],
            send_sem.at[4],
            back_sem.at[1],
            {"seq": target // ch_count, "ch": lax.rem(target, ch_count)},
        )

    def to_rows(which, index, tile):
        send_buf[which, pl.ds(index, channels, stride=rows), :] = tile

    rate_buf[...] = jnp.broadcast_to(rate_ref[...], (lanes, all_channels)).T
    weight_buf[...] = weight_ref[...].T
    loads[0].wait()
    for index in range(rows):
        to_rows(0, index, grad_ref[:, index * lanes : (index + 1) * lanes])
    loads[1].wait()
    for index in range(rows):
        to_rows(1, index, input_ref[:, index * lanes : (index + 1) * lanes])

    pl.semaphore_wait(barrier, seq_count + ch_count - 2)

    send_mixed(0, 2)
    to_right(0, 2, 0)
    to_left(0, 2, 0)

    for step in range(1, seq_count):
        signal(met_sem.at[0], lax.rem(seq_place + step, seq_count), ch_place)

    first_chan = pl.multiple_of(ch_place * channels, 8)
    local_rates = rate_buf[pl.ds(first_chan, channels), :]
    local_weight = split_value(weight_buf[pl.ds(first_chan, channels), :])
    lane_ids = lax.broadcasted_iota(jnp.int32, (1, lanes), 1)

    def window_of(rates, first):
        steps_t = (first + lane_ids).astype(jnp.float32) / full_len
        return jnp.exp(-rates * steps_t) + shift_term

    bias_buf[...] = jnp.broadcast_to(bias_ref[...], (lanes, all_channels)).T
    loads[2].wait()
    chunk = math.gcd(rows, 4)
    for outer in range(rows // chunk):
        lo = outer * chunk * lanes
        block = split_value(feat_ref[:, lo : lo + chunk * lanes])
        values = dot_split(local_weight, block)
        for inside in range(chunk):
            index = outer * chunk + inside
            window = window_of(local_rates, (seq_place * rows + index) * lanes)
            to_rows(2, index, values[:, inside * lanes : (inside + 1) * lanes] * window)

    send_mixed(2, 3)
    to_right(2, 3, 0)
    to_left(2, 3, 0)

    def send_rest(chan, carry):
        to_right(0, 2, chan)
        to_right(2, 3, chan)
        to_left(0, 3, chan)
        return carry

    lax.fori_loop(1, jnp.where(on_right, 2, per), send_rest, 0)

    conv_recv[pl.ds(channels * rows, mixed * rows), :] = jnp.zeros(
        (mixed * rows, lanes), jnp.float32
    )
    for group in range(ch_count):
        lag_recv[pl.ds((all_channels + group * channels) * sub_rows, mixed * sub_rows), :] = (
            jnp.zeros((mixed * sub_rows, lanes), jnp.float32)
        )

    @pl.when(on_right)
    def _():
        conv_recv[pl.ds((channels + mixed) * rows, (channels - mixed) * rows), :] = jnp.zeros(
            ((channels - mixed) * rows, lanes), jnp.float32
        )
        for group in range(ch_count):
            lag_recv[
                pl.ds(
                    (all_channels + group * channels + mixed) * sub_rows,
                    (channels - mixed) * sub_rows,
                ),
                :,
            ] = jnp.zeros(((channels - mixed) * sub_rows, lanes), jnp.float32)

        def keep_own(chan, carry):
            gather_full[0, chan, pl.ds(0, half * rows), :] = jnp.zeros(
                (half * rows, lanes), jnp.float32
            )
            for which in range(3):
                gather_full[which, chan, rows_of(seq_place), :] = send_buf[
                    which, rows_of(split_channel(side_place, chan)), :
                ]
            return carry

        lax.fori_loop(0, per, keep_own, 0)

    @pl.when(on_left)
    def _():
        def keep_own(chan, carry):
            for which in range(3):
                gather_half[which, chan, rows_of(side_place), :] = send_buf[
                    which, rows_of(split_channel(side_place, chan)), :
                ]
            return carry

        lax.fori_loop(0, per, keep_own, 0)

    @pl.when(on_inner)
    def _():
        for slot in range(mixed_per):
            for which in range(3):
                gather_full[which, slot, rows_of(seq_place), :] = send_buf[
                    which, rows_of((seq_place - inner) * mixed_per + slot), :
                ]

    for index in range(sub_rows):
        window_buf[index] = window_of(rate_buf[...], (flat_place * sub_rows + index) * lanes)

    for load in loads[3:]:
        load.wait()
    pl.semaphore_wait(met_sem.at[0], seq_count - 1)

    def send_conv(channel, slot, count, targets):
        each_other(
            seq_place,
            targets,
            lambda target: conv_copy(channel, slot, count, target).start(),
        )

    def send_lag(channel, slot, count, targets):
        each_other(
            flat_place,
            targets,
            lambda target: lag_copy(channel, slot, count, target).start(),
        )

    full_tables = (row_ref, row_back_ref, lane_ref, lane_back_ref, twist_ref)
    half_tables = (half_row_ref, half_back_ref, lane_ref, lane_back_ref, half_twist_ref)

    def work_full(chan, carry):
        slot = jnp.where(on_right, chan, per + chan)
        channel = jnp.where(
            on_right,
            split_channel(side_place, chan),
            (seq_place - inner) * mixed_per + chan,
        )

        @pl.when(on_right)
        def _():
            @pl.when(chan + 2 < per)
            def _():
                to_right(0, 2, chan + 2)
                to_right(2, 3, chan + 2)

            counted((3 * half - 2) * rows, send_sem.at[0], full_sem.at[chan]).wait_recv()

        @pl.when(on_left)
        def _():
            counted(2 * (seq_count - 1) * rows, send_sem.at[0], full_sem.at[chan]).wait_recv()

        first, second = spectra([gather_full[0, chan], gather_full[1, chan]], full_tables)
        grad_freqs[...] = first
        lag_send[:, pl.ds(pl.multiple_of(slot * sub_rows, 8), sub_rows), :] = correlated(
            first, [second], full_tables
        ).reshape(total, sub_rows, lanes)
        send_lag(channel, slot, 1, total)

        @pl.when(on_right)
        def _():
            counted((2 * half - 1) * rows, send_sem.at[0], filt_sem.at[chan]).wait_recv()

        @pl.when(on_left)
        def _():
            counted((seq_count - 1) * rows, send_sem.at[0], filt_sem.at[chan]).wait_recv()

        (third,) = spectra([gather_full[2, chan]], full_tables)
        conv_send[:, pl.ds(pl.multiple_of(slot * rows, 8), rows), :] = correlated(
            grad_freqs[...], [third], full_tables
        ).reshape(seq_count, rows, lanes)
        send_conv(channel, slot, 1, seq_count)
        return carry

    rounds = jnp.where(on_right, per, jnp.where(on_inner, mixed_per, 0))
    lax.fori_loop(0, rounds, work_full, 0)

    def work_half(chan, carry):
        counted(3 * (half - 1) * rows, send_sem.at[0], half_sem.at[chan]).wait_recv()
        first, second, third = spectra(
            [gather_half[which, chan] for which in range(3)], half_tables
        )
        final = correlated(first, [third, second], half_tables)
        channel = split_channel(side_place, chan)
        conv_send[:half, pl.ds(pl.multiple_of(chan * rows, 8), rows), :] = final[
            :, :lanes
        ].reshape(half, rows, lanes)
        lag_send[:left_total, pl.ds(pl.multiple_of(chan * sub_rows, 8), sub_rows), :] = final[
            :, lanes:
        ].reshape(left_total, sub_rows, lanes)

        @pl.when(lax.rem(chan, 2) == 1)
        def _():
            send_conv(channel - 1, chan - 1, 2, half)
            send_lag(channel - 1, chan - 1, 2, left_total)

        @pl.when(chan == per - 1)
        def _():
            send_conv(channel, chan, 1, half)
            send_lag(channel, chan, 1, left_total)

        return carry

    @pl.when(on_left)
    def _():
        lax.fori_loop(0, per, work_half, 0)

    def keep_back(channel, slot, count):
        conv_recv[pl.ds(pl.multiple_of(channel * rows, 8), count * rows), :] = conv_send[
            seq_place, pl.ds(pl.multiple_of(slot * rows, 8), count * rows), :
        ]
        lag_recv[pl.ds(lag_row(channel), count * sub_rows), :] = lag_send[
            flat_place, pl.ds(pl.multiple_of(slot * sub_rows, 8), count * sub_rows), :
        ]

    keep_back(split_channel(side_place, 0), 0, per)

    @pl.when(on_inner)
    def _():
        keep_back((seq_place - inner) * mixed_per, per, mixed_per)

    def expect(recv, unit, own_side, whole):
        for place, count in (
            (on_outer, own_side * per + whole * mixed_per + (own_side + 1) * per),
            (on_inner, own_side * per + (whole - 1) * mixed_per + (own_side + 1) * per),
            (on_right, own_side * per + whole * mixed_per),
        ):

            @pl.when(place)
            def _():
                counted(count * unit, send_sem.at[0], recv).wait_recv()

    def sent(index, outer_count, inner_count, right_count):
        for place, count in (
            (on_outer, outer_count),
            (on_inner, inner_count),
            (on_right, right_count),
        ):
            if count:

                @pl.when(place)
                def _():
                    counted(count, send_sem.at[index], back_sem.at[0]).wait_send()

    expect(back_sem.at[1], sub_rows, left_total - 1, inner * ch_count)
    weight = split_value(weight_ref[...])
    for index in range(sub_rows):
        tile = (
            lag_recv[pl.ds(index, all_channels, stride=sub_rows), :]
            + lag_recv[pl.ds(all_channels * sub_rows + index, all_channels, stride=sub_rows), :]
        ) * window_buf[index]
        feat_grad_ref[:, index * lanes : (index + 1) * lanes] = dot_split(
            weight, split_value(tile)
        )
    expect(back_sem.at[0], rows, half - 1, inner)
    local_bias = bias_buf[pl.ds(first_chan, channels), :]
    for index in range(rows):
        span = slice(index * lanes, (index + 1) * lanes)
        in_grad_ref[:, span] = (
            conv_recv[pl.ds(index, channels, stride=rows), :]
            + conv_recv[pl.ds(channels * rows + index, channels, stride=rows), :]
            + local_bias * grad_ref[:, span]
        )

    left_sent = 2 * half * per * rows
    own_side = 3 * (half - 1) * per * rows
    to_inner = 3 * mixed * rows
    to_inner_own = 3 * (mixed - mixed_per) * rows
    sent(0, left_sent, left_sent, own_side)
    sent(1, own_side, own_side, 0)
    sent(2, to_inner, to_inner_own, to_inner)
    side_back = (half - 1) * per * rows
    sent(
        3,
        side_back,
        side_back + (seq_count - 1) * mixed_per * rows,
        (seq_count - 1) * per * rows,
    )
    side_lag = (left_total - 1) * per * sub_rows
    sent(
        4,
        side_lag,
        side_lag + (total - 1) * mixed_per * sub_rows,
        (total - 1) * per * sub_rows,
    )


def local_whole(seq_count, ch_count, tables, *args):
    out_grad, gated_input, features, filter_weight, rates, skip_bias = args
    channels, local_len = out_grad.shape
    rows = local_len // lanes
    feats, all_channels = filter_weight.shape
    half, inner, mixed, mixed_per, per = plan(seq_count, channels)
    slots = per + mixed_per
    data_rows = rows * seq_count
    sub_rows = rows // ch_count
    total = seq_count * ch_count
    sizes = (seq_count, ch_count, channels, rows)
    in_vmem = pl.BlockSpec(memory_space=pltpu.VMEM)
    anywhere = pl.BlockSpec(memory_space=pl.ANY)
    dma = pltpu.SemaphoreType.DMA
    f32 = jnp.float32
    longest = max(
        3 * channels * rows,
        2 * channels * rows,
        2 * all_channels * sub_rows,
        seq_count * slots * rows,
        total * slots * sub_rows,
    )
    held = pl.pallas_call(
        functools.partial(whole_kernel, sizes),
        out_shape=(
            pltpu.VMEM((channels, local_len), f32),
            pltpu.VMEM((feats, sub_rows * lanes), f32),
        ),
        in_specs=[anywhere] * 3 + [in_vmem] * 3 + [anywhere] * len(tables),
        out_specs=(in_vmem, in_vmem),
        scratch_shapes=[
            pltpu.VMEM((channels, local_len), f32),
            pltpu.VMEM((channels, local_len), f32),
            pltpu.VMEM((feats, local_len), f32),
            *[pltpu.VMEM(table.shape, table.dtype) for table in tables],
            dma((3 + len(tables),)),
            pltpu.VMEM((3, channels * rows, lanes), f32),
            pltpu.VMEM((3, per, data_rows, lanes), f32),
            pltpu.VMEM((3, per, half * rows, lanes), f32),
            pltpu.VMEM((seq_count, slots * rows, lanes), f32),
            pltpu.VMEM((total, slots * sub_rows, lanes), f32),
            pltpu.VMEM((2 * channels * rows, lanes), f32),
            pltpu.VMEM((2 * all_channels * sub_rows, lanes), f32),
            pltpu.VMEM((sub_rows, all_channels, lanes), f32),
            pltpu.VMEM((all_channels, lanes), f32),
            pltpu.VMEM((all_channels, lanes), f32),
            pltpu.VMEM((all_channels, feats), f32),
            pltpu.VMEM((longest, lanes), f32),
            pltpu.VMEM((data_rows, 2 * lanes), f32),
            dma((per,)),
            dma((per,)),
            dma((per,)),
            dma((5,)),
            dma((2,)),
            pltpu.SemaphoreType.REGULAR((1,)),
        ],
        compiler_params=pltpu.CompilerParams(collective_id=0, has_side_effects=True),
    )(
        out_grad,
        gated_input,
        features,
        filter_weight,
        rates.reshape(1, all_channels),
        skip_bias.reshape(1, all_channels),
        *[jnp.asarray(table) for table in tables],
    )
    held = [pltpu.with_memory_space_constraint(value, pltpu.VMEM) for value in held]
    return pl.pallas_call(
        store_kernel,
        out_shape=tuple(jax.ShapeDtypeStruct(value.shape, f32) for value in held),
        in_specs=[in_vmem] * 2,
        out_specs=(anywhere, anywhere),
        scratch_shapes=[dma((2,))],
    )(*held)


def store_kernel(first_ref, second_ref, first_hbm, second_hbm, sem):
    stores = [
        pltpu.make_async_copy(first_ref, first_hbm, sem.at[0]),
        pltpu.make_async_copy(second_ref, second_hbm, sem.at[1]),
    ]
    for store in stores:
        store.start()
    for store in stores:
        store.wait()


def solution(mesh):
    seq_count, ch_count = mesh.shape["seq"], mesh.shape["ch"]
    in_specs = (P("ch", "seq"), P("ch", "seq"), P(None, "seq"), P(), P(), P())
    out_specs = (P("ch", "seq"), P(None, ("seq", "ch")))

    def whole(*args):
        channels, full_len = args[0].shape
        channels = channels // ch_count
        local_len = full_len // seq_count
        half, inner, mixed, mixed_per, per = plan(seq_count, channels)
        fits = (
            seq_count % 4 == 0
            and channels % 8 == 0
            and mixed == inner * mixed_per
            and mixed_per == 2
            and mixed + half * per == channels
            and per % 2 == 1
            and per >= 5
            and local_len % (8 * lanes * ch_count) == 0
            and full_len <= 512 * lanes
        )
        body = local
        if fits:
            row, row_back, lane, lane_back, twist = make_tables(full_len // lanes)
            half_row, half_back, _, _, half_twist = make_tables(full_len // lanes // 2)
            tables = (row, row_back, lane, lane_back, twist, half_row, half_back * 2, half_twist)
            body = functools.partial(local_whole, seq_count, ch_count, tables)
        return jax.shard_map(
            body, mesh=mesh, in_specs=in_specs, out_specs=out_specs, check_vma=False
        )(*args)

    return whole
```

```python
import functools
import math

import jax
import jax.numpy as jnp
import numpy as np
from jax import lax
from jax.experimental import pallas as pl
from jax.experimental.pallas import tpu as pltpu
from jax.sharding import PartitionSpec as P

shift_term = 0.05
highest = lax.Precision.HIGHEST


def matmul_high(operand, matrix):
    return jnp.dot(operand, matrix, precision=highest, preferred_element_type=jnp.float32)


def angle_table(first_ids, second_ids, period):
    product = first_ids[:, None] * second_ids[None, :] % period
    angles = product.astype(jnp.float32) * (2.0 * math.pi / period)
    return (jnp.cos(angles), jnp.sin(angles))


def contract(real_part, imag_part, cos_table, sin_table, einsum_form):

    def multiply_by(operand, matrix):
        return jnp.einsum(
            einsum_form, operand, matrix, precision=highest, preferred_element_type=jnp.float32
        )

    return (
        multiply_by(real_part, cos_table) - multiply_by(imag_part, sin_table),
        multiply_by(real_part, sin_table) + multiply_by(imag_part, cos_table),
    )


def group_width(channels, block_len):
    return math.gcd(channels, max(1, 128 // block_len)) * block_len


def group_table(width, block_len, sign_term):
    ids = jnp.arange(width, dtype=jnp.int32)
    same = ids[:, None] // block_len == ids[None, :] // block_len
    inner = ids % block_len
    product = inner[:, None] * inner[None, :] % block_len
    angles = product.astype(jnp.float32) * (2.0 * math.pi / block_len)
    return (
        jnp.where(same, jnp.cos(angles), 0.0).astype(jnp.float32),
        jnp.where(same, sign_term * jnp.sin(angles), 0.0).astype(jnp.float32),
    )


def local_transform(real_part, imag_part, block_len, inverse):
    rows, seq_count, width_all = real_part.shape
    channels = width_all // block_len
    local_len = seq_count * block_len
    width = group_width(channels, block_len)
    sign_term = 1.0 if inverse else -1.0
    seq_ids = jnp.arange(seq_count, dtype=jnp.int32)
    block_ids = jnp.arange(block_len, dtype=jnp.int32)
    cos_seq, sin_seq = angle_table(seq_ids, seq_ids, seq_count)
    sin_seq = sign_term * sin_seq
    cos_twist, sin_twist = angle_table(seq_ids, block_ids, local_len)
    cos_twist = jnp.tile(cos_twist, (1, channels))
    sin_twist = sign_term * jnp.tile(sin_twist, (1, channels))
    cos_group, sin_group = group_table(width, block_len, sign_term)
    grouped = (rows, seq_count, width_all // width, width)
    flat = (rows, seq_count, width_all)

    def twist(re_part, im_part):
        return (
            re_part * cos_twist - im_part * sin_twist,
            re_part * sin_twist + im_part * cos_twist,
        )

    def across_groups(re_part, im_part):
        re_part, im_part = contract(
            re_part.reshape(grouped),
            im_part.reshape(grouped),
            cos_group,
            sin_group,
            "rkgm,mq->rkgq",
        )
        return (re_part.reshape(flat), im_part.reshape(flat))

    if inverse:
        real_part, imag_part = across_groups(real_part, imag_part)
        real_part, imag_part = twist(real_part, imag_part)
        real_part, imag_part = contract(real_part, imag_part, cos_seq, sin_seq, "rsx,sk->rkx")
    else:
        real_part, imag_part = contract(real_part, imag_part, cos_seq, sin_seq, "rsx,sk->rkx")
        real_part, imag_part = twist(real_part, imag_part)
        real_part, imag_part = across_groups(real_part, imag_part)
    return (real_part, imag_part)


def first_section(row_block, cos_fwd, sin_fwd, twid_cos, twid_sin):
    real_part = matmul_high(cos_fwd, row_block)
    imag_part = -matmul_high(sin_fwd, row_block)
    real_out = real_part * twid_cos + imag_part * twid_sin
    imag_out = imag_part * twid_cos - real_part * twid_sin
    return (real_out[:, None, :], imag_out[:, None, :])


def rotate_back(real_part, imag_part, twid_cos, twid_sin):
    return (
        real_part * twid_cos - imag_part * twid_sin,
        real_part * twid_sin + imag_part * twid_cos,
    )


def forward_products(
    block_len, grad_real, grad_imag, input_real, input_imag, filter_real, filter_imag
):
    grad_real, grad_imag = local_transform(grad_real, grad_imag, block_len, False)
    input_real, input_imag = local_transform(input_real, input_imag, block_len, False)
    filter_real, filter_imag = local_transform(filter_real, filter_imag, block_len, False)
    corr_real = filter_real * grad_real + filter_imag * grad_imag
    corr_imag = filter_real * grad_imag - filter_imag * grad_real
    lag_real = input_real * grad_real + input_imag * grad_imag
    lag_imag = input_real * grad_imag - input_imag * grad_real
    return (corr_real, corr_imag, lag_real, lag_imag)


def products_inverted(block_len, operands):
    corr_real, corr_imag, lag_real, lag_imag = forward_products(block_len, *operands)
    corr_real, corr_imag = local_transform(corr_real, corr_imag, block_len, True)
    lag_real, lag_imag = local_transform(lag_real, lag_imag, block_len, True)
    return (corr_real, corr_imag, lag_real, lag_imag)


def paired_rows(block_len, operands):
    seq_count = operands[0].shape[1]
    channels = operands[0].shape[2] // block_len
    local_len = seq_count * block_len
    positions = (
        jnp.arange(seq_count, dtype=jnp.int32)[:, None] * block_len
        + jnp.arange(block_len, dtype=jnp.int32)[None, :]
    )
    angles = positions.astype(jnp.float32) * (math.pi / local_len)
    half_cos = jnp.tile(jnp.cos(angles), (1, channels))
    half_sin = jnp.tile(jnp.sin(angles), (1, channels))
    stacked = []
    for index in range(3):
        low_row = operands[2 * index]
        high_row = operands[2 * index + 1]
        stacked.append(jnp.concatenate([low_row, high_row * half_cos], axis=0))
        stacked.append(jnp.concatenate([jnp.zeros_like(low_row), -high_row * half_sin], axis=0))
    corr_real, corr_imag, lag_real, lag_imag = products_inverted(block_len, tuple(stacked))
    return (
        corr_real[0:1],
        corr_real[1:2] * half_cos - corr_imag[1:2] * half_sin,
        lag_real[0:1],
        lag_real[1:2] * half_cos - lag_imag[1:2] * half_sin,
    )


def local(out_grad, gated_input, features, filter_weight, rates, skip_bias):
    channels, local_len = out_grad.shape
    seq_count = lax.axis_size("seq")
    block_len = local_len // seq_count
    width_all = channels * block_len
    freq_count = 2 * seq_count
    full_len = local_len * seq_count
    padded_len = 2 * full_len
    seq_place = lax.axis_index("seq")
    first_chan = lax.axis_index("ch") * channels
    local_rates = lax.dynamic_slice_in_dim(rates, first_chan, channels)
    local_bias = lax.dynamic_slice_in_dim(skip_bias, first_chan, channels)
    local_weight = lax.dynamic_slice_in_dim(filter_weight, first_chan, channels, 1)
    position = seq_place * local_len + jnp.arange(local_len, dtype=jnp.int32)
    window = (
        jnp.exp(-local_rates[:, None] * (position.astype(jnp.float32) / full_len)[None, :])
        + shift_term
    )
    filter_vals = matmul_high(local_weight.T, features) * window

    def to_rows(values):
        return (
            values.reshape(channels, seq_count, block_len)
            .transpose(1, 0, 2)
            .reshape(seq_count, width_all)
        )

    received = (
        lax.all_to_all(to_rows(out_grad), "seq", split_axis=0, concat_axis=0, tiled=True),
        lax.all_to_all(to_rows(gated_input), "seq", split_axis=0, concat_axis=0, tiled=True),
        lax.all_to_all(to_rows(filter_vals), "seq", split_axis=0, concat_axis=0, tiled=True),
    )

    def inverted(operands):
        return products_inverted(block_len, operands)

    def paired(operands):
        return paired_rows(block_len, operands)

    freq_ids = jnp.arange(freq_count, dtype=jnp.int32)
    dev_ids = jnp.arange(seq_count, dtype=jnp.int32)
    local_m = seq_place * block_len + jnp.arange(block_len, dtype=jnp.int32)
    twid_cos, twid_sin = angle_table(freq_ids, local_m, padded_len)
    twid_cos = jnp.tile(twid_cos, (1, channels))
    twid_sin = jnp.tile(twid_sin, (1, channels))
    scale_term = 1.0 / padded_len
    alternate = jnp.where(dev_ids % 2 == 0, 1.0, -1.0).astype(jnp.float32)
    cos_half, sin_half = angle_table(dev_ids, dev_ids, freq_count)
    sin_half = jnp.where(dev_ids[:, None] == 0, -alternate[None, :], sin_half)
    twid_half_cos = twid_cos[:seq_count]
    twid_half_sin = twid_sin[:seq_count]
    spread = [
        first_section(piece, cos_half, sin_half, twid_half_cos, twid_half_sin) for piece in received
    ]
    exchanged = (
        lax.all_to_all(spread[0][0], "seq", split_axis=0, concat_axis=1, tiled=True),
        lax.all_to_all(spread[0][1], "seq", split_axis=0, concat_axis=1, tiled=True),
        lax.all_to_all(spread[1][0], "seq", split_axis=0, concat_axis=1, tiled=True),
        lax.all_to_all(spread[1][1], "seq", split_axis=0, concat_axis=1, tiled=True),
        lax.all_to_all(spread[2][0], "seq", split_axis=0, concat_axis=1, tiled=True),
        lax.all_to_all(spread[2][1], "seq", split_axis=0, concat_axis=1, tiled=True),
    )
    corr_real, corr_imag, lag_real, lag_imag = lax.cond(
        seq_place == 0, paired, inverted, tuple(exchanged)
    )
    corr_real, corr_imag, lag_real, lag_imag = (
        lax.all_to_all(corr_real, "seq", split_axis=1, concat_axis=0, tiled=True),
        lax.all_to_all(corr_imag, "seq", split_axis=1, concat_axis=0, tiled=True),
        lax.all_to_all(lag_real, "seq", split_axis=1, concat_axis=0, tiled=True),
        lax.all_to_all(lag_imag, "seq", split_axis=1, concat_axis=0, tiled=True),
    )
    corr_flat_real, corr_flat_imag = rotate_back(
        corr_real.reshape(seq_count, width_all),
        corr_imag.reshape(seq_count, width_all),
        twid_half_cos,
        twid_half_sin,
    )
    lag_flat_real, lag_flat_imag = rotate_back(
        lag_real.reshape(seq_count, width_all),
        lag_imag.reshape(seq_count, width_all),
        twid_half_cos,
        twid_half_sin,
    )
    cos_final, sin_final = angle_table(dev_ids, dev_ids, freq_count)
    cos_final = jnp.where(dev_ids[None, :] == 0, 1.0, 2.0 * cos_final)
    sin_final = jnp.where(dev_ids[None, :] == 0, -alternate[:, None], 2.0 * sin_final)
    conv_rows = (
        matmul_high(cos_final, corr_flat_real) - matmul_high(sin_final, corr_flat_imag)
    ) * scale_term
    lag_rows = (
        matmul_high(cos_final, lag_flat_real) - matmul_high(sin_final, lag_flat_imag)
    ) * scale_term
    conv_back, lag_back = (
        lax.all_to_all(conv_rows, "seq", split_axis=0, concat_axis=0, tiled=True),
        lax.all_to_all(lag_rows, "seq", split_axis=0, concat_axis=0, tiled=True),
    )

    def to_channels(values):
        return (
            values.reshape(seq_count, channels, block_len)
            .transpose(1, 0, 2)
            .reshape(channels, local_len)
        )

    conv_grad = to_channels(conv_back)
    filt_grad = to_channels(lag_back)
    in_grad = conv_grad + local_bias[:, None] * out_grad
    weighted = filt_grad * window
    regrouped = lax.all_to_all(weighted, "ch", split_axis=1, concat_axis=0, tiled=True)
    feat_grad = matmul_high(filter_weight, regrouped)
    return (in_grad, feat_grad)


lanes = 128


def split_table(table):
    table = np.asarray(table, np.float32)
    high_part = table.astype(jnp.bfloat16)
    low_part = (table - high_part.astype(np.float32)).astype(jnp.bfloat16)
    return np.stack([high_part, low_part])


def make_tables(data_rows):
    freq_rows = 2 * data_rows
    padded_len = freq_rows * lanes
    odd_ids = 2 * np.arange(data_rows) + 1
    row_angle = (odd_ids[:, None] * np.arange(data_rows)[None, :] % (2 * freq_rows)) * (
        math.pi / freq_rows
    )
    row_table = np.concatenate([np.cos(row_angle), -np.sin(row_angle)], axis=0)
    lane_ids = np.arange(lanes)
    twist_angle = (odd_ids[:, None] * lane_ids[None, :]) * (math.pi / padded_len)
    twist = np.stack([np.cos(twist_angle), -np.sin(twist_angle)]).astype(np.float32)
    lane_angle = (lane_ids[:, None] * lane_ids[None, :] % lanes) * (2.0 * math.pi / lanes)
    lane_cos, lane_sin = np.cos(lane_angle), np.sin(lane_angle)
    lane_table = np.block([[lane_cos, -lane_sin], [lane_sin, lane_cos]])
    back_table = np.block([[lane_cos, lane_sin], [-lane_sin, lane_cos]]) * (2.0 / padded_len)
    return (
        split_table(row_table),
        split_table(row_table.T),
        split_table(lane_table),
        split_table(back_table),
        twist,
    )


def split_value(value):
    high_part = value.astype(jnp.bfloat16)
    return high_part, (value - high_part.astype(jnp.float32)).astype(jnp.bfloat16)


def dot_split(left, right):
    def product(first, second):
        return jnp.dot(first, second, preferred_element_type=jnp.float32)

    return product(left[0], right[0]) + (product(left[0], right[1]) + product(left[1], right[0]))


def spectra(pieces, tables):
    row_ref, lane_ref, twist_ref = tables[0], tables[2], tables[4]
    data_rows = pieces[0].shape[0]
    twist_cos, twist_sin = twist_ref[0], twist_ref[1]
    packed = pieces[0] if len(pieces) == 1 else jnp.concatenate(pieces, axis=1)
    spread = dot_split((row_ref[0], row_ref[1]), split_value(packed))
    freqs = []
    for which in range(len(pieces)):
        re_part = spread[:data_rows, which * lanes : (which + 1) * lanes]
        im_part = spread[data_rows:, which * lanes : (which + 1) * lanes]
        turned = jnp.concatenate(
            [
                re_part * twist_cos - im_part * twist_sin,
                re_part * twist_sin + im_part * twist_cos,
            ],
            axis=1,
        )
        freqs.append(dot_split(split_value(turned), (lane_ref[0], lane_ref[1])))
    return freqs


def correlated(grad_freqs, others, tables):
    row_back_ref, lane_back_ref, twist_ref = tables[1], tables[3], tables[4]
    twist_cos, twist_sin = twist_ref[0], twist_ref[1]
    grad_re, grad_im = grad_freqs[:, :lanes], grad_freqs[:, lanes:]
    turned = []
    for spectrum in others:
        re_part, im_part = spectrum[:, :lanes], spectrum[:, lanes:]
        product = jnp.concatenate(
            [
                re_part * grad_re + im_part * grad_im,
                re_part * grad_im - im_part * grad_re,
            ],
            axis=1,
        )
        back = dot_split(split_value(product), (lane_back_ref[0], lane_back_ref[1]))
        re_part, im_part = back[:, :lanes], back[:, lanes:]
        turned.append(
            jnp.concatenate(
                [
                    re_part * twist_cos + im_part * twist_sin,
                    im_part * twist_cos - re_part * twist_sin,
                ],
                axis=0,
            )
        )
    both = turned[0] if len(turned) == 1 else jnp.concatenate(turned, axis=1)
    return dot_split((row_back_ref[0], row_back_ref[1]), split_value(both))


def plan(seq_count, channels):
    half = seq_count // 2
    mixed = channels // 8
    inner = half // 2
    return half, inner, mixed, mixed // max(inner, 1), (channels - mixed) // half


def whole_kernel(sizes, *refs):
    (
        grad_hbm,
        input_hbm,
        feat_hbm,
        weight_hbm,
        rate_hbm,
        bias_hbm,
        row_hbm,
        row_back_hbm,
        lane_hbm,
        lane_back_hbm,
        twist_hbm,
        half_row_hbm,
        half_back_hbm,
        half_twist_hbm,
        in_grad_ref,
        feat_grad_ref,
        grad_ref,
        input_ref,
        feat_ref,
        row_ref,
        row_back_ref,
        lane_ref,
        lane_back_ref,
        twist_ref,
        half_row_ref,
        half_back_ref,
        half_twist_ref,
        weight_ref,
        rate_ref,
        bias_ref,
        load_sem,
        send_buf,
        gather_full,
        gather_half,
        conv_send,
        lag_send,
        conv_recv,
        lag_recv,
        window_buf,
        rate_buf,
        bias_buf,
        weight_buf,
        ruler,
        grad_freqs,
        full_sem,
        filt_sem,
        half_sem,
        send_sem,
        back_sem,
        met_sem,
    ) = refs
    seq_count, ch_count, channels, rows = sizes
    half, inner, mixed, mixed_per, per = plan(seq_count, channels)
    data_rows = rows * seq_count
    sub_rows = rows // ch_count
    all_channels = channels * ch_count
    total = seq_count * ch_count
    left_total = half * ch_count
    full_len = data_rows * lanes
    seq_place = lax.axis_index("seq")
    ch_place = lax.axis_index("ch")
    flat_place = seq_place * ch_count + ch_place
    on_right = seq_place >= half
    on_left = seq_place < half
    on_inner = jnp.logical_and(seq_place >= inner, on_left)
    on_outer = seq_place < inner
    side_place = lax.rem(seq_place, half)
    here = {"seq": seq_place, "ch": ch_place}

    loads = [
        pltpu.make_async_copy(source, target, load_sem.at[index])
        for index, (source, target) in enumerate(
            (
                (grad_hbm, grad_ref),
                (input_hbm, input_ref),
                (weight_hbm, weight_ref),
                (rate_hbm, rate_ref),
                (bias_hbm, bias_ref),
                (feat_hbm, feat_ref),
                (row_hbm, row_ref),
                (twist_hbm, twist_ref),
                (lane_hbm, lane_ref),
                (lane_back_hbm, lane_back_ref),
                (row_back_hbm, row_back_ref),
                (half_row_hbm, half_row_ref),
                (half_back_hbm, half_back_ref),
                (half_twist_hbm, half_twist_ref),
            )
        )
    ]
    barrier = pltpu.get_barrier_semaphore()

    def signal(sem, seq, ch):
        pl.semaphore_signal(
            sem, inc=1, device_id={"seq": seq, "ch": ch}, device_id_type=pl.DeviceIdType.MESH
        )

    for step in range(1, seq_count):
        signal(barrier, lax.rem(seq_place + step, seq_count), ch_place)
    for step in range(1, ch_count):
        signal(barrier, seq_place, lax.rem(ch_place + step, ch_count))
    for load in loads:
        load.start()

    def each_other(place, count, visit, first=1):
        def one(step, carry):
            visit(lax.rem(place + step, count))
            return carry

        lax.fori_loop(first, count, one, 0)

    def remote(source, target, send, recv, device):
        return pltpu.make_async_remote_copy(
            src_ref=source,
            dst_ref=target,
            send_sem=send,
            recv_sem=recv,
            device_id=device,
            device_id_type=pl.DeviceIdType.MESH,
        )

    def counted(count, send, recv):
        part = ruler.at[pl.ds(0, count)]
        return remote(part, part, send, recv, here)

    def rows_of(channel):
        return pl.ds(pl.multiple_of(channel * rows, 8), rows)

    def split_channel(side, chan):
        return mixed + side * per + chan

    def full_copy(first, last, channel, slot, target, sem):
        return remote(
            send_buf.at[first:last, rows_of(channel)],
            gather_full.at[first:last, slot, rows_of(seq_place)],
            send_sem.at[sem],
            (filt_sem if first == 2 else full_sem).at[slot],
            {"seq": target, "ch": ch_place},
        )

    def half_copy(first, last, channel, slot, target):
        return remote(
            send_buf.at[first:last, rows_of(channel)],
            gather_half.at[first:last, slot, rows_of(side_place)],
            send_sem.at[1],
            half_sem.at[slot],
            {"seq": target, "ch": ch_place},
        )

    def send_mixed(first, last):
        for side in range(inner):
            target = inner + side

            @pl.when(seq_place != target)
            def _():
                for slot in range(mixed_per):
                    channel = side * mixed_per + slot
                    full_copy(first, last, channel, slot, target, 2).start()

    def to_right(first, last, chan):
        @pl.when(on_left)
        def _():
            for step in range(half):
                side = step // 2 * 2 + lax.rem(step + seq_place, 2)
                full_copy(
                    max(first, 1), last, split_channel(side, chan), chan, half + side, 0
                ).start()

        @pl.when(on_right)
        def _():
            each_other(
                side_place,
                half,
                lambda side: full_copy(
                    first, last, split_channel(side, chan), chan, half + side, 0
                ).start(),
            )

    def to_left(first, last, chan):
        @pl.when(on_left)
        def _():
            each_other(
                side_place,
                half,
                lambda side: half_copy(
                    first, last, split_channel(side, chan), chan, side
                ).start(),
            )

    def conv_copy(channel, slot, count, target):
        part = jnp.where(jnp.logical_and(on_right, target < half), channels, 0)
        return remote(
            conv_send.at[target, pl.ds(pl.multiple_of(slot * rows, 8), count * rows)],
            conv_recv.at[pl.ds(pl.multiple_of((part + channel) * rows, 8), count * rows)],
            send_sem.at[3],
            back_sem.at[0],
            {"seq": target, "ch": ch_place},
        )

    def lag_row(channel):
        return pl.multiple_of((ch_place * channels + channel) * sub_rows, 8)

    def lag_copy(channel, slot, count, target):
        part = jnp.where(jnp.logical_and(on_right, target < left_total), all_channels, 0)
        return remote(
            lag_send.at[target, pl.ds(pl.multiple_of(slot * sub_rows, 8), count * sub_rows)],
            lag_recv.at[
                pl.ds(
                    pl.multiple_of(part * sub_rows + lag_row(channel), 8), count * sub_rows
                )
            ],
            send_sem.at[4],
            back_sem.at[1],
            {"seq": target // ch_count, "ch": lax.rem(target, ch_count)},
        )

    def to_rows(which, index, tile):
        send_buf[which, pl.ds(index, channels, stride=rows), :] = tile

    loads[0].wait()
    for index in range(rows):
        to_rows(0, index, grad_ref[:, index * lanes : (index + 1) * lanes])
    loads[1].wait()
    for index in range(rows):
        to_rows(1, index, input_ref[:, index * lanes : (index + 1) * lanes])

    for load in loads[2:5]:
        load.wait()
    rate_buf[...] = jnp.broadcast_to(rate_ref[...], (lanes, all_channels)).T
    weight_buf[...] = weight_ref[...].T
    bias_buf[...] = jnp.broadcast_to(bias_ref[...], (lanes, all_channels)).T

    pl.semaphore_wait(barrier, seq_count + ch_count - 2)

    @pl.when(on_right)
    def _():
        send_mixed(0, 2)

    to_right(0, 2, 0)
    to_left(0, 2, 0)

    @pl.when(on_left)
    def _():
        send_mixed(0, 2)


    for step in range(1, seq_count):
        signal(met_sem.at[0], lax.rem(seq_place + step, seq_count), ch_place)

    first_chan = pl.multiple_of(ch_place * channels, 8)
    local_rates = rate_buf[pl.ds(first_chan, channels), :]
    local_weight = split_value(weight_buf[pl.ds(first_chan, channels), :])
    lane_ids = lax.broadcasted_iota(jnp.int32, (1, lanes), 1)

    def window_of(rates, first):
        steps_t = (first + lane_ids).astype(jnp.float32) / full_len
        return jnp.exp(-rates * steps_t) + shift_term

    loads[5].wait()
    chunk = math.gcd(rows, 4)
    for outer in range(rows // chunk):
        lo = outer * chunk * lanes
        block = split_value(feat_ref[:, lo : lo + chunk * lanes])
        values = dot_split(local_weight, block)
        for inside in range(chunk):
            index = outer * chunk + inside
            window = window_of(local_rates, (seq_place * rows + index) * lanes)
            to_rows(2, index, values[:, inside * lanes : (inside + 1) * lanes] * window)

    send_mixed(2, 3)
    to_right(2, 3, 0)
    to_left(2, 3, 0)

    def send_rest(chan, carry):
        to_right(0, 2, chan)
        to_left(0, 3, chan)
        to_right(2, 3, chan)
        return carry

    lax.fori_loop(1, jnp.where(on_right, 2, per), send_rest, 0)

    conv_recv[pl.ds(channels * rows, mixed * rows), :] = jnp.zeros(
        (mixed * rows, lanes), jnp.float32
    )
    for group in range(ch_count):
        lag_recv[pl.ds((all_channels + group * channels) * sub_rows, mixed * sub_rows), :] = (
            jnp.zeros((mixed * sub_rows, lanes), jnp.float32)
        )

    @pl.when(on_right)
    def _():
        conv_recv[pl.ds((channels + mixed) * rows, (channels - mixed) * rows), :] = jnp.zeros(
            ((channels - mixed) * rows, lanes), jnp.float32
        )
        for group in range(ch_count):
            lag_recv[
                pl.ds(
                    (all_channels + group * channels + mixed) * sub_rows,
                    (channels - mixed) * sub_rows,
                ),
                :,
            ] = jnp.zeros(((channels - mixed) * sub_rows, lanes), jnp.float32)

        def keep_own(chan, carry):
            gather_full[0, chan, pl.ds(0, half * rows), :] = jnp.zeros(
                (half * rows, lanes), jnp.float32
            )
            for which in range(3):
                gather_full[which, chan, rows_of(seq_place), :] = send_buf[
                    which, rows_of(split_channel(side_place, chan)), :
                ]
            return carry

        lax.fori_loop(0, per, keep_own, 0)

    @pl.when(on_left)
    def _():
        def keep_own(chan, carry):
            for which in range(3):
                gather_half[which, chan, rows_of(side_place), :] = send_buf[
                    which, rows_of(split_channel(side_place, chan)), :
                ]
            return carry

        lax.fori_loop(0, per, keep_own, 0)

    @pl.when(on_inner)
    def _():
        for slot in range(mixed_per):
            for which in range(3):
                gather_full[which, slot, rows_of(seq_place), :] = send_buf[
                    which, rows_of((seq_place - inner) * mixed_per + slot), :
                ]

    for index in range(sub_rows):
        window_buf[index] = window_of(rate_buf[...], (flat_place * sub_rows + index) * lanes)

    for load in loads[6:]:
        load.wait()
    pl.semaphore_wait(met_sem.at[0], seq_count - 1)

    def send_conv(channel, slot, count, targets):
        each_other(
            seq_place,
            targets,
            lambda target: conv_copy(channel, slot, count, target).start(),
        )

    def send_lag(channel, slot, count, targets):
        each_other(
            flat_place,
            targets,
            lambda target: lag_copy(channel, slot, count, target).start(),
        )

    full_tables = (row_ref, row_back_ref, lane_ref, lane_back_ref, twist_ref)
    half_tables = (half_row_ref, half_back_ref, lane_ref, lane_back_ref, half_twist_ref)

    def work_full(chan, carry):
        slot = jnp.where(on_right, chan, per + chan)
        channel = jnp.where(
            on_right,
            split_channel(side_place, chan),
            (seq_place - inner) * mixed_per + chan,
        )

        @pl.when(on_right)
        def _():
            @pl.when(chan + 2 < per)
            def _():
                to_right(0, 2, chan + 2)
                to_right(2, 3, chan + 2)

            counted((3 * half - 2) * rows, send_sem.at[0], full_sem.at[chan]).wait_recv()

        @pl.when(on_left)
        def _():
            counted(2 * (seq_count - 1) * rows, send_sem.at[0], full_sem.at[chan]).wait_recv()

        first, second = spectra([gather_full[0, chan], gather_full[1, chan]], full_tables)
        grad_freqs[...] = first
        lag_send[:, pl.ds(pl.multiple_of(slot * sub_rows, 8), sub_rows), :] = correlated(
            first, [second], full_tables
        ).reshape(total, sub_rows, lanes)

        @pl.when(on_right)
        def _():
            send_lag(channel, slot, 1, total)

        @pl.when(jnp.logical_and(on_left, chan == 1))
        def _():
            send_lag(channel - 1, slot - 1, 2, total)

        @pl.when(on_right)
        def _():
            counted((2 * half - 1) * rows, send_sem.at[0], filt_sem.at[chan]).wait_recv()

        @pl.when(on_left)
        def _():
            counted((seq_count - 1) * rows, send_sem.at[0], filt_sem.at[chan]).wait_recv()

        (third,) = spectra([gather_full[2, chan]], full_tables)
        conv_send[:, pl.ds(pl.multiple_of(slot * rows, 8), rows), :] = correlated(
            grad_freqs[...], [third], full_tables
        ).reshape(seq_count, rows, lanes)
        send_conv(channel, slot, 1, seq_count)
        return carry

    rounds = jnp.where(on_right, per, jnp.where(on_inner, mixed_per, 0))
    lax.fori_loop(0, rounds, work_full, 0)

    def work_half(chan, carry):
        counted(3 * (half - 1) * rows, send_sem.at[0], half_sem.at[chan]).wait_recv()
        first, second, third = spectra(
            [gather_half[which, chan] for which in range(3)], half_tables
        )
        final = correlated(first, [third, second], half_tables)
        channel = split_channel(side_place, chan)
        conv_send[:half, pl.ds(pl.multiple_of(chan * rows, 8), rows), :] = final[
            :, :lanes
        ].reshape(half, rows, lanes)
        lag_send[:left_total, pl.ds(pl.multiple_of(chan * sub_rows, 8), sub_rows), :] = final[
            :, lanes:
        ].reshape(left_total, sub_rows, lanes)

        @pl.when(lax.rem(chan, 2) == 1)
        def _():
            send_conv(channel - 1, chan - 1, 2, half)
            send_lag(channel - 1, chan - 1, 2, left_total)

        @pl.when(chan == per - 1)
        def _():
            send_conv(channel, chan, 1, half)
            send_lag(channel, chan, 1, left_total)

        return carry

    @pl.when(on_left)
    def _():
        lax.fori_loop(0, per, work_half, 0)

    def keep_back(channel, slot, count):
        conv_recv[pl.ds(pl.multiple_of(channel * rows, 8), count * rows), :] = conv_send[
            seq_place, pl.ds(pl.multiple_of(slot * rows, 8), count * rows), :
        ]
        lag_recv[pl.ds(lag_row(channel), count * sub_rows), :] = lag_send[
            flat_place, pl.ds(pl.multiple_of(slot * sub_rows, 8), count * sub_rows), :
        ]

    keep_back(split_channel(side_place, 0), 0, per)

    @pl.when(on_inner)
    def _():
        keep_back((seq_place - inner) * mixed_per, per, mixed_per)

    def expect(recv, unit, own_side, whole):
        for place, count in (
            (on_outer, own_side * per + whole * mixed_per + (own_side + 1) * per),
            (on_inner, own_side * per + (whole - 1) * mixed_per + (own_side + 1) * per),
            (on_right, own_side * per + whole * mixed_per),
        ):

            @pl.when(place)
            def _():
                counted(count * unit, send_sem.at[0], recv).wait_recv()

    def sent(index, outer_count, inner_count, right_count):
        for place, count in (
            (on_outer, outer_count),
            (on_inner, inner_count),
            (on_right, right_count),
        ):
            if count:

                @pl.when(place)
                def _():
                    counted(count, send_sem.at[index], back_sem.at[0]).wait_send()

    expect(back_sem.at[1], sub_rows, left_total - 1, inner * ch_count)
    weight = split_value(weight_ref[...])
    for index in range(sub_rows):
        tile = (
            lag_recv[pl.ds(index, all_channels, stride=sub_rows), :]
            + lag_recv[pl.ds(all_channels * sub_rows + index, all_channels, stride=sub_rows), :]
        ) * window_buf[index]
        feat_grad_ref[:, index * lanes : (index + 1) * lanes] = dot_split(
            weight, split_value(tile)
        )
    expect(back_sem.at[0], rows, half - 1, inner)
    local_bias = bias_buf[pl.ds(first_chan, channels), :]
    for index in range(rows):
        span = slice(index * lanes, (index + 1) * lanes)
        in_grad_ref[:, span] = (
            conv_recv[pl.ds(index, channels, stride=rows), :]
            + conv_recv[pl.ds(channels * rows + index, channels, stride=rows), :]
            + local_bias * grad_ref[:, span]
        )

    left_sent = 2 * half * per * rows
    own_side = 3 * (half - 1) * per * rows
    to_inner = 3 * mixed * rows
    to_inner_own = 3 * (mixed - mixed_per) * rows
    sent(0, left_sent, left_sent, own_side)
    sent(1, own_side, own_side, 0)
    sent(2, to_inner, to_inner_own, to_inner)
    side_back = (half - 1) * per * rows
    sent(
        3,
        side_back,
        side_back + (seq_count - 1) * mixed_per * rows,
        (seq_count - 1) * per * rows,
    )
    side_lag = (left_total - 1) * per * sub_rows
    sent(
        4,
        side_lag,
        side_lag + (total - 1) * mixed_per * sub_rows,
        (total - 1) * per * sub_rows,
    )


def local_whole(seq_count, ch_count, tables, *args):
    out_grad, gated_input, features, filter_weight, rates, skip_bias = args
    channels, local_len = out_grad.shape
    rows = local_len // lanes
    feats, all_channels = filter_weight.shape
    half, inner, mixed, mixed_per, per = plan(seq_count, channels)
    slots = per + mixed_per
    data_rows = rows * seq_count
    sub_rows = rows // ch_count
    total = seq_count * ch_count
    sizes = (seq_count, ch_count, channels, rows)
    in_vmem = pl.BlockSpec(memory_space=pltpu.VMEM)
    anywhere = pl.BlockSpec(memory_space=pl.ANY)
    dma = pltpu.SemaphoreType.DMA
    f32 = jnp.float32
    longest = max(
        3 * channels * rows,
        2 * channels * rows,
        2 * all_channels * sub_rows,
        seq_count * slots * rows,
        total * slots * sub_rows,
    )
    held = pl.pallas_call(
        functools.partial(whole_kernel, sizes),
        out_shape=(
            pltpu.VMEM((channels, local_len), f32),
            pltpu.VMEM((feats, sub_rows * lanes), f32),
        ),
        in_specs=[anywhere] * (6 + len(tables)),
        out_specs=(in_vmem, in_vmem),
        scratch_shapes=[
            pltpu.VMEM((channels, local_len), f32),
            pltpu.VMEM((channels, local_len), f32),
            pltpu.VMEM((feats, local_len), f32),
            *[pltpu.VMEM(table.shape, table.dtype) for table in tables],
            pltpu.VMEM((feats, all_channels), f32),
            pltpu.VMEM((1, all_channels), f32),
            pltpu.VMEM((1, all_channels), f32),
            dma((6 + len(tables),)),
            pltpu.VMEM((3, channels * rows, lanes), f32),
            pltpu.VMEM((3, per, data_rows, lanes), f32),
            pltpu.VMEM((3, per, half * rows, lanes), f32),
            pltpu.VMEM((seq_count, slots * rows, lanes), f32),
            pltpu.VMEM((total, slots * sub_rows, lanes), f32),
            pltpu.VMEM((2 * channels * rows, lanes), f32),
            pltpu.VMEM((2 * all_channels * sub_rows, lanes), f32),
            pltpu.VMEM((sub_rows, all_channels, lanes), f32),
            pltpu.VMEM((all_channels, lanes), f32),
            pltpu.VMEM((all_channels, lanes), f32),
            pltpu.VMEM((all_channels, feats), f32),
            pltpu.VMEM((longest, lanes), f32),
            pltpu.VMEM((data_rows, 2 * lanes), f32),
            dma((per,)),
            dma((per,)),
            dma((per,)),
            dma((5,)),
            dma((2,)),
            pltpu.SemaphoreType.REGULAR((1,)),
        ],
        compiler_params=pltpu.CompilerParams(collective_id=0, has_side_effects=True),
    )(
        out_grad,
        gated_input,
        features,
        filter_weight,
        rates.reshape(1, all_channels),
        skip_bias.reshape(1, all_channels),
        *[jnp.asarray(table) for table in tables],
    )
    held = [pltpu.with_memory_space_constraint(value, pltpu.VMEM) for value in held]
    return pl.pallas_call(
        store_kernel,
        out_shape=tuple(jax.ShapeDtypeStruct(value.shape, f32) for value in held),
        in_specs=[in_vmem] * 2,
        out_specs=(anywhere, anywhere),
        scratch_shapes=[dma((2,))],
    )(*held)


def store_kernel(first_ref, second_ref, first_hbm, second_hbm, sem):
    stores = [
        pltpu.make_async_copy(first_ref, first_hbm, sem.at[0]),
        pltpu.make_async_copy(second_ref, second_hbm, sem.at[1]),
    ]
    for store in stores:
        store.start()
    for store in stores:
        store.wait()


def solution(mesh):
    seq_count, ch_count = mesh.shape["seq"], mesh.shape["ch"]
    in_specs = (P("ch", "seq"), P("ch", "seq"), P(None, "seq"), P(), P(), P())
    out_specs = (P("ch", "seq"), P(None, ("seq", "ch")))

    def whole(*args):
        channels, full_len = args[0].shape
        channels = channels // ch_count
        local_len = full_len // seq_count
        half, inner, mixed, mixed_per, per = plan(seq_count, channels)
        fits = (
            seq_count % 4 == 0
            and channels % 8 == 0
            and mixed == inner * mixed_per
            and mixed_per == 2
            and mixed + half * per == channels
            and per % 2 == 1
            and per >= 5
            and local_len % (8 * lanes * ch_count) == 0
            and full_len <= 512 * lanes
        )
        body = local
        if fits:
            row, row_back, lane, lane_back, twist = make_tables(full_len // lanes)
            half_row, half_back, _, _, half_twist = make_tables(full_len // lanes // 2)
            tables = (row, row_back, lane, lane_back, twist, half_row, half_back * 2, half_twist)
            body = functools.partial(local_whole, seq_count, ch_count, tables)
        return jax.shard_map(
            body, mesh=mesh, in_specs=in_specs, out_specs=out_specs, check_vma=False
        )(*args)

    return whole
```

```python
import functools
import math

import jax
import jax.numpy as jnp
import numpy as np
from jax import lax
from jax.experimental import pallas as pl
from jax.experimental.pallas import tpu as pltpu
from jax.sharding import PartitionSpec as P

shift_term = 0.05
highest = lax.Precision.HIGHEST


def matmul_high(operand, matrix):
    return jnp.dot(operand, matrix, precision=highest, preferred_element_type=jnp.float32)


def angle_table(first_ids, second_ids, period):
    product = first_ids[:, None] * second_ids[None, :] % period
    angles = product.astype(jnp.float32) * (2.0 * math.pi / period)
    return (jnp.cos(angles), jnp.sin(angles))


def contract(real_part, imag_part, cos_table, sin_table, einsum_form):

    def multiply_by(operand, matrix):
        return jnp.einsum(
            einsum_form, operand, matrix, precision=highest, preferred_element_type=jnp.float32
        )

    return (
        multiply_by(real_part, cos_table) - multiply_by(imag_part, sin_table),
        multiply_by(real_part, sin_table) + multiply_by(imag_part, cos_table),
    )


def group_width(channels, block_len):
    return math.gcd(channels, max(1, 128 // block_len)) * block_len


def group_table(width, block_len, sign_term):
    ids = jnp.arange(width, dtype=jnp.int32)
    same = ids[:, None] // block_len == ids[None, :] // block_len
    inner = ids % block_len
    product = inner[:, None] * inner[None, :] % block_len
    angles = product.astype(jnp.float32) * (2.0 * math.pi / block_len)
    return (
        jnp.where(same, jnp.cos(angles), 0.0).astype(jnp.float32),
        jnp.where(same, sign_term * jnp.sin(angles), 0.0).astype(jnp.float32),
    )


def local_transform(real_part, imag_part, block_len, inverse):
    rows, seq_count, width_all = real_part.shape
    channels = width_all // block_len
    local_len = seq_count * block_len
    width = group_width(channels, block_len)
    sign_term = 1.0 if inverse else -1.0
    seq_ids = jnp.arange(seq_count, dtype=jnp.int32)
    block_ids = jnp.arange(block_len, dtype=jnp.int32)
    cos_seq, sin_seq = angle_table(seq_ids, seq_ids, seq_count)
    sin_seq = sign_term * sin_seq
    cos_twist, sin_twist = angle_table(seq_ids, block_ids, local_len)
    cos_twist = jnp.tile(cos_twist, (1, channels))
    sin_twist = sign_term * jnp.tile(sin_twist, (1, channels))
    cos_group, sin_group = group_table(width, block_len, sign_term)
    grouped = (rows, seq_count, width_all // width, width)
    flat = (rows, seq_count, width_all)

    def twist(re_part, im_part):
        return (
            re_part * cos_twist - im_part * sin_twist,
            re_part * sin_twist + im_part * cos_twist,
        )

    def across_groups(re_part, im_part):
        re_part, im_part = contract(
            re_part.reshape(grouped),
            im_part.reshape(grouped),
            cos_group,
            sin_group,
            "rkgm,mq->rkgq",
        )
        return (re_part.reshape(flat), im_part.reshape(flat))

    if inverse:
        real_part, imag_part = across_groups(real_part, imag_part)
        real_part, imag_part = twist(real_part, imag_part)
        real_part, imag_part = contract(real_part, imag_part, cos_seq, sin_seq, "rsx,sk->rkx")
    else:
        real_part, imag_part = contract(real_part, imag_part, cos_seq, sin_seq, "rsx,sk->rkx")
        real_part, imag_part = twist(real_part, imag_part)
        real_part, imag_part = across_groups(real_part, imag_part)
    return (real_part, imag_part)


def first_section(row_block, cos_fwd, sin_fwd, twid_cos, twid_sin):
    real_part = matmul_high(cos_fwd, row_block)
    imag_part = -matmul_high(sin_fwd, row_block)
    real_out = real_part * twid_cos + imag_part * twid_sin
    imag_out = imag_part * twid_cos - real_part * twid_sin
    return (real_out[:, None, :], imag_out[:, None, :])


def rotate_back(real_part, imag_part, twid_cos, twid_sin):
    return (
        real_part * twid_cos - imag_part * twid_sin,
        real_part * twid_sin + imag_part * twid_cos,
    )


def forward_products(
    block_len, grad_real, grad_imag, input_real, input_imag, filter_real, filter_imag
):
    grad_real, grad_imag = local_transform(grad_real, grad_imag, block_len, False)
    input_real, input_imag = local_transform(input_real, input_imag, block_len, False)
    filter_real, filter_imag = local_transform(filter_real, filter_imag, block_len, False)
    corr_real = filter_real * grad_real + filter_imag * grad_imag
    corr_imag = filter_real * grad_imag - filter_imag * grad_real
    lag_real = input_real * grad_real + input_imag * grad_imag
    lag_imag = input_real * grad_imag - input_imag * grad_real
    return (corr_real, corr_imag, lag_real, lag_imag)


def products_inverted(block_len, operands):
    corr_real, corr_imag, lag_real, lag_imag = forward_products(block_len, *operands)
    corr_real, corr_imag = local_transform(corr_real, corr_imag, block_len, True)
    lag_real, lag_imag = local_transform(lag_real, lag_imag, block_len, True)
    return (corr_real, corr_imag, lag_real, lag_imag)


def paired_rows(block_len, operands):
    seq_count = operands[0].shape[1]
    channels = operands[0].shape[2] // block_len
    local_len = seq_count * block_len
    positions = (
        jnp.arange(seq_count, dtype=jnp.int32)[:, None] * block_len
        + jnp.arange(block_len, dtype=jnp.int32)[None, :]
    )
    angles = positions.astype(jnp.float32) * (math.pi / local_len)
    half_cos = jnp.tile(jnp.cos(angles), (1, channels))
    half_sin = jnp.tile(jnp.sin(angles), (1, channels))
    stacked = []
    for index in range(3):
        low_row = operands[2 * index]
        high_row = operands[2 * index + 1]
        stacked.append(jnp.concatenate([low_row, high_row * half_cos], axis=0))
        stacked.append(jnp.concatenate([jnp.zeros_like(low_row), -high_row * half_sin], axis=0))
    corr_real, corr_imag, lag_real, lag_imag = products_inverted(block_len, tuple(stacked))
    return (
        corr_real[0:1],
        corr_real[1:2] * half_cos - corr_imag[1:2] * half_sin,
        lag_real[0:1],
        lag_real[1:2] * half_cos - lag_imag[1:2] * half_sin,
    )


def local(out_grad, gated_input, features, filter_weight, rates, skip_bias):
    channels, local_len = out_grad.shape
    seq_count = lax.axis_size("seq")
    block_len = local_len // seq_count
    width_all = channels * block_len
    freq_count = 2 * seq_count
    full_len = local_len * seq_count
    padded_len = 2 * full_len
    seq_place = lax.axis_index("seq")
    first_chan = lax.axis_index("ch") * channels
    local_rates = lax.dynamic_slice_in_dim(rates, first_chan, channels)
    local_bias = lax.dynamic_slice_in_dim(skip_bias, first_chan, channels)
    local_weight = lax.dynamic_slice_in_dim(filter_weight, first_chan, channels, 1)
    position = seq_place * local_len + jnp.arange(local_len, dtype=jnp.int32)
    window = (
        jnp.exp(-local_rates[:, None] * (position.astype(jnp.float32) / full_len)[None, :])
        + shift_term
    )
    filter_vals = matmul_high(local_weight.T, features) * window

    def to_rows(values):
        return (
            values.reshape(channels, seq_count, block_len)
            .transpose(1, 0, 2)
            .reshape(seq_count, width_all)
        )

    received = (
        lax.all_to_all(to_rows(out_grad), "seq", split_axis=0, concat_axis=0, tiled=True),
        lax.all_to_all(to_rows(gated_input), "seq", split_axis=0, concat_axis=0, tiled=True),
        lax.all_to_all(to_rows(filter_vals), "seq", split_axis=0, concat_axis=0, tiled=True),
    )

    def inverted(operands):
        return products_inverted(block_len, operands)

    def paired(operands):
        return paired_rows(block_len, operands)

    freq_ids = jnp.arange(freq_count, dtype=jnp.int32)
    dev_ids = jnp.arange(seq_count, dtype=jnp.int32)
    local_m = seq_place * block_len + jnp.arange(block_len, dtype=jnp.int32)
    twid_cos, twid_sin = angle_table(freq_ids, local_m, padded_len)
    twid_cos = jnp.tile(twid_cos, (1, channels))
    twid_sin = jnp.tile(twid_sin, (1, channels))
    scale_term = 1.0 / padded_len
    alternate = jnp.where(dev_ids % 2 == 0, 1.0, -1.0).astype(jnp.float32)
    cos_half, sin_half = angle_table(dev_ids, dev_ids, freq_count)
    sin_half = jnp.where(dev_ids[:, None] == 0, -alternate[None, :], sin_half)
    twid_half_cos = twid_cos[:seq_count]
    twid_half_sin = twid_sin[:seq_count]
    spread = [
        first_section(piece, cos_half, sin_half, twid_half_cos, twid_half_sin) for piece in received
    ]
    exchanged = (
        lax.all_to_all(spread[0][0], "seq", split_axis=0, concat_axis=1, tiled=True),
        lax.all_to_all(spread[0][1], "seq", split_axis=0, concat_axis=1, tiled=True),
        lax.all_to_all(spread[1][0], "seq", split_axis=0, concat_axis=1, tiled=True),
        lax.all_to_all(spread[1][1], "seq", split_axis=0, concat_axis=1, tiled=True),
        lax.all_to_all(spread[2][0], "seq", split_axis=0, concat_axis=1, tiled=True),
        lax.all_to_all(spread[2][1], "seq", split_axis=0, concat_axis=1, tiled=True),
    )
    corr_real, corr_imag, lag_real, lag_imag = lax.cond(
        seq_place == 0, paired, inverted, tuple(exchanged)
    )
    corr_real, corr_imag, lag_real, lag_imag = (
        lax.all_to_all(corr_real, "seq", split_axis=1, concat_axis=0, tiled=True),
        lax.all_to_all(corr_imag, "seq", split_axis=1, concat_axis=0, tiled=True),
        lax.all_to_all(lag_real, "seq", split_axis=1, concat_axis=0, tiled=True),
        lax.all_to_all(lag_imag, "seq", split_axis=1, concat_axis=0, tiled=True),
    )
    corr_flat_real, corr_flat_imag = rotate_back(
        corr_real.reshape(seq_count, width_all),
        corr_imag.reshape(seq_count, width_all),
        twid_half_cos,
        twid_half_sin,
    )
    lag_flat_real, lag_flat_imag = rotate_back(
        lag_real.reshape(seq_count, width_all),
        lag_imag.reshape(seq_count, width_all),
        twid_half_cos,
        twid_half_sin,
    )
    cos_final, sin_final = angle_table(dev_ids, dev_ids, freq_count)
    cos_final = jnp.where(dev_ids[None, :] == 0, 1.0, 2.0 * cos_final)
    sin_final = jnp.where(dev_ids[None, :] == 0, -alternate[:, None], 2.0 * sin_final)
    conv_rows = (
        matmul_high(cos_final, corr_flat_real) - matmul_high(sin_final, corr_flat_imag)
    ) * scale_term
    lag_rows = (
        matmul_high(cos_final, lag_flat_real) - matmul_high(sin_final, lag_flat_imag)
    ) * scale_term
    conv_back, lag_back = (
        lax.all_to_all(conv_rows, "seq", split_axis=0, concat_axis=0, tiled=True),
        lax.all_to_all(lag_rows, "seq", split_axis=0, concat_axis=0, tiled=True),
    )

    def to_channels(values):
        return (
            values.reshape(seq_count, channels, block_len)
            .transpose(1, 0, 2)
            .reshape(channels, local_len)
        )

    conv_grad = to_channels(conv_back)
    filt_grad = to_channels(lag_back)
    in_grad = conv_grad + local_bias[:, None] * out_grad
    weighted = filt_grad * window
    regrouped = lax.all_to_all(weighted, "ch", split_axis=1, concat_axis=0, tiled=True)
    feat_grad = matmul_high(filter_weight, regrouped)
    return (in_grad, feat_grad)


lanes = 128


def split_table(table):
    table = np.asarray(table, np.float32)
    high_part = table.astype(jnp.bfloat16)
    low_part = (table - high_part.astype(np.float32)).astype(jnp.bfloat16)
    return np.stack([high_part, low_part])


def make_tables(data_rows):
    freq_rows = 2 * data_rows
    padded_len = freq_rows * lanes
    odd_ids = 2 * np.arange(data_rows) + 1
    row_angle = (odd_ids[:, None] * np.arange(data_rows)[None, :] % (2 * freq_rows)) * (
        math.pi / freq_rows
    )
    row_table = np.concatenate([np.cos(row_angle), -np.sin(row_angle)], axis=0)
    lane_ids = np.arange(lanes)
    twist_angle = (odd_ids[:, None] * lane_ids[None, :]) * (math.pi / padded_len)
    twist = np.stack([np.cos(twist_angle), -np.sin(twist_angle)]).astype(np.float32)
    lane_angle = (lane_ids[:, None] * lane_ids[None, :] % lanes) * (2.0 * math.pi / lanes)
    lane_cos, lane_sin = np.cos(lane_angle), np.sin(lane_angle)
    lane_table = np.block([[lane_cos, -lane_sin], [lane_sin, lane_cos]])
    back_table = np.block([[lane_cos, lane_sin], [-lane_sin, lane_cos]]) * (2.0 / padded_len)
    return (
        split_table(row_table),
        split_table(row_table.T),
        split_table(lane_table),
        split_table(back_table),
        twist,
    )


def split_value(value):
    high_part = value.astype(jnp.bfloat16)
    return high_part, (value - high_part.astype(jnp.float32)).astype(jnp.bfloat16)


def dot_split(left, right):
    def product(first, second):
        return jnp.dot(first, second, preferred_element_type=jnp.float32)

    return product(left[0], right[0]) + (product(left[0], right[1]) + product(left[1], right[0]))


def spectra(pieces, tables):
    row_ref, lane_ref, twist_ref = tables[0], tables[2], tables[4]
    data_rows = pieces[0].shape[0]
    twist_cos, twist_sin = twist_ref[0], twist_ref[1]
    packed = pieces[0] if len(pieces) == 1 else jnp.concatenate(pieces, axis=1)
    spread = dot_split((row_ref[0], row_ref[1]), split_value(packed))
    freqs = []
    for which in range(len(pieces)):
        re_part = spread[:data_rows, which * lanes : (which + 1) * lanes]
        im_part = spread[data_rows:, which * lanes : (which + 1) * lanes]
        turned = jnp.concatenate(
            [
                re_part * twist_cos - im_part * twist_sin,
                re_part * twist_sin + im_part * twist_cos,
            ],
            axis=1,
        )
        freqs.append(dot_split(split_value(turned), (lane_ref[0], lane_ref[1])))
    return freqs


def correlated(grad_freqs, others, tables):
    row_back_ref, lane_back_ref, twist_ref = tables[1], tables[3], tables[4]
    twist_cos, twist_sin = twist_ref[0], twist_ref[1]
    grad_re, grad_im = grad_freqs[:, :lanes], grad_freqs[:, lanes:]
    turned = []
    for spectrum in others:
        re_part, im_part = spectrum[:, :lanes], spectrum[:, lanes:]
        product = jnp.concatenate(
            [
                re_part * grad_re + im_part * grad_im,
                re_part * grad_im - im_part * grad_re,
            ],
            axis=1,
        )
        back = dot_split(split_value(product), (lane_back_ref[0], lane_back_ref[1]))
        re_part, im_part = back[:, :lanes], back[:, lanes:]
        turned.append(
            jnp.concatenate(
                [
                    re_part * twist_cos + im_part * twist_sin,
                    im_part * twist_cos - re_part * twist_sin,
                ],
                axis=0,
            )
        )
    both = turned[0] if len(turned) == 1 else jnp.concatenate(turned, axis=1)
    return dot_split((row_back_ref[0], row_back_ref[1]), split_value(both))


def plan(seq_count, channels):
    half = seq_count // 2
    mixed = channels // 8
    inner = half // 2
    return half, inner, mixed, mixed // max(inner, 1), (channels - mixed) // half


def whole_kernel(sizes, *refs):
    (
        grad_hbm,
        input_hbm,
        feat_hbm,
        weight_hbm,
        rate_hbm,
        bias_hbm,
        row_hbm,
        row_back_hbm,
        lane_hbm,
        lane_back_hbm,
        twist_hbm,
        half_row_hbm,
        half_back_hbm,
        half_twist_hbm,
        in_grad_ref,
        feat_grad_ref,
        grad_ref,
        input_ref,
        feat_ref,
        row_ref,
        row_back_ref,
        lane_ref,
        lane_back_ref,
        twist_ref,
        half_row_ref,
        half_back_ref,
        half_twist_ref,
        weight_ref,
        rate_ref,
        bias_ref,
        load_sem,
        send_buf,
        gather_full,
        gather_half,
        conv_send,
        lag_send,
        conv_recv,
        lag_recv,
        window_buf,
        rate_buf,
        bias_buf,
        weight_buf,
        ruler,
        grad_freqs,
        full_sem,
        filt_sem,
        half_sem,
        send_sem,
        back_sem,
        met_sem,
    ) = refs
    seq_count, ch_count, channels, rows = sizes
    half, inner, mixed, mixed_per, per = plan(seq_count, channels)
    data_rows = rows * seq_count
    sub_rows = rows // ch_count
    all_channels = channels * ch_count
    total = seq_count * ch_count
    left_total = half * ch_count
    full_len = data_rows * lanes
    seq_place = lax.axis_index("seq")
    ch_place = lax.axis_index("ch")
    flat_place = seq_place * ch_count + ch_place
    on_right = seq_place >= half
    on_left = seq_place < half
    on_inner = jnp.logical_and(seq_place >= inner, on_left)
    on_outer = seq_place < inner
    side_place = lax.rem(seq_place, half)
    here = {"seq": seq_place, "ch": ch_place}

    loads = [
        pltpu.make_async_copy(source, target, load_sem.at[index])
        for index, (source, target) in enumerate(
            (
                (grad_hbm, grad_ref),
                (input_hbm, input_ref),
                (weight_hbm, weight_ref),
                (rate_hbm, rate_ref),
                (bias_hbm, bias_ref),
                (feat_hbm, feat_ref),
                (row_hbm, row_ref),
                (twist_hbm, twist_ref),
                (lane_hbm, lane_ref),
                (lane_back_hbm, lane_back_ref),
                (row_back_hbm, row_back_ref),
                (half_row_hbm, half_row_ref),
                (half_back_hbm, half_back_ref),
                (half_twist_hbm, half_twist_ref),
            )
        )
    ]
    barrier = pltpu.get_barrier_semaphore()

    def signal(sem, seq, ch):
        pl.semaphore_signal(
            sem, inc=1, device_id={"seq": seq, "ch": ch}, device_id_type=pl.DeviceIdType.MESH
        )

    for step in range(1, seq_count):
        signal(barrier, lax.rem(seq_place + step, seq_count), ch_place)
    for step in range(1, ch_count):
        signal(barrier, seq_place, lax.rem(ch_place + step, ch_count))
    for load in loads:
        load.start()

    def each_other(place, count, visit, first=1):
        def one(step, carry):
            visit(lax.rem(place + step, count))
            return carry

        lax.fori_loop(first, count, one, 0)

    def remote(source, target, send, recv, device):
        return pltpu.make_async_remote_copy(
            src_ref=source,
            dst_ref=target,
            send_sem=send,
            recv_sem=recv,
            device_id=device,
            device_id_type=pl.DeviceIdType.MESH,
        )

    def counted(count, send, recv):
        part = ruler.at[pl.ds(0, count)]
        return remote(part, part, send, recv, here)

    def rows_of(channel):
        return pl.ds(pl.multiple_of(channel * rows, 8), rows)

    def split_channel(side, chan):
        return mixed + side * per + chan

    def full_copy(first, last, channel, slot, target, sem):
        return remote(
            send_buf.at[first:last, rows_of(channel)],
            gather_full.at[first:last, slot, rows_of(seq_place)],
            send_sem.at[sem],
            (filt_sem if first == 2 else full_sem).at[slot],
            {"seq": target, "ch": ch_place},
        )

    def half_copy(first, last, channel, slot, target):
        return remote(
            send_buf.at[first:last, rows_of(channel)],
            gather_half.at[first:last, slot, rows_of(side_place)],
            send_sem.at[1],
            half_sem.at[slot],
            {"seq": target, "ch": ch_place},
        )

    def send_mixed(first, last):
        for side in range(inner):
            target = inner + side

            @pl.when(seq_place != target)
            def _():
                for slot in range(mixed_per):
                    channel = side * mixed_per + slot
                    full_copy(first, last, channel, slot, target, 2).start()

    def to_right(first, last, chan):
        @pl.when(on_left)
        def _():
            for step in range(half):
                side = step // 2 * 2 + lax.rem(step + seq_place, 2)
                full_copy(
                    max(first, 1), last, split_channel(side, chan), chan, half + side, 0
                ).start()

        @pl.when(on_right)
        def _():
            each_other(
                side_place,
                half,
                lambda side: full_copy(
                    first, last, split_channel(side, chan), chan, half + side, 0
                ).start(),
            )

    def to_left(first, last, chan):
        @pl.when(on_left)
        def _():
            each_other(
                side_place,
                half,
                lambda side: half_copy(
                    first, last, split_channel(side, chan), chan, side
                ).start(),
            )

    def conv_copy(channel, slot, count, target):
        part = jnp.where(jnp.logical_and(on_right, target < half), channels, 0)
        return remote(
            conv_send.at[target, pl.ds(pl.multiple_of(slot * rows, 8), count * rows)],
            conv_recv.at[pl.ds(pl.multiple_of((part + channel) * rows, 8), count * rows)],
            send_sem.at[3],
            back_sem.at[0],
            {"seq": target, "ch": ch_place},
        )

    def lag_row(channel):
        return pl.multiple_of((ch_place * channels + channel) * sub_rows, 8)

    def lag_copy(channel, slot, count, target):
        part = jnp.where(jnp.logical_and(on_right, target < left_total), all_channels, 0)
        return remote(
            lag_send.at[target, pl.ds(pl.multiple_of(slot * sub_rows, 8), count * sub_rows)],
            lag_recv.at[
                pl.ds(
                    pl.multiple_of(part * sub_rows + lag_row(channel), 8), count * sub_rows
                )
            ],
            send_sem.at[4],
            back_sem.at[1],
            {"seq": target // ch_count, "ch": lax.rem(target, ch_count)},
        )

    def to_rows(which, index, tile):
        send_buf[which, pl.ds(index, channels, stride=rows), :] = tile

    loads[0].wait()
    for index in range(rows):
        to_rows(0, index, grad_ref[:, index * lanes : (index + 1) * lanes])
    loads[1].wait()
    for index in range(rows):
        to_rows(1, index, input_ref[:, index * lanes : (index + 1) * lanes])

    for load in loads[2:5]:
        load.wait()
    rate_buf[...] = jnp.broadcast_to(rate_ref[...], (lanes, all_channels)).T
    weight_buf[...] = weight_ref[...].T
    bias_buf[...] = jnp.broadcast_to(bias_ref[...], (lanes, all_channels)).T

    pl.semaphore_wait(barrier, seq_count + ch_count - 2)

    @pl.when(on_right)
    def _():
        send_mixed(0, 2)

    to_right(0, 2, 0)
    to_left(0, 2, 0)

    @pl.when(on_left)
    def _():
        send_mixed(0, 2)


    for step in range(1, seq_count):
        signal(met_sem.at[0], lax.rem(seq_place + step, seq_count), ch_place)

    first_chan = pl.multiple_of(ch_place * channels, 8)
    local_rates = rate_buf[pl.ds(first_chan, channels), :]
    local_weight = split_value(weight_buf[pl.ds(first_chan, channels), :])
    lane_ids = lax.broadcasted_iota(jnp.int32, (1, lanes), 1)

    def window_of(rates, first):
        steps_t = (first + lane_ids).astype(jnp.float32) / full_len
        return jnp.exp(-rates * steps_t) + shift_term

    loads[5].wait()
    chunk = math.gcd(rows, 4)
    for outer in range(rows // chunk):
        lo = outer * chunk * lanes
        block = split_value(feat_ref[:, lo : lo + chunk * lanes])
        values = dot_split(local_weight, block)
        for inside in range(chunk):
            index = outer * chunk + inside
            window = window_of(local_rates, (seq_place * rows + index) * lanes)
            to_rows(2, index, values[:, inside * lanes : (inside + 1) * lanes] * window)

    send_mixed(2, 3)
    to_right(2, 3, 0)
    to_left(2, 3, 0)

    def send_rest(chan, carry):
        to_right(0, 2, chan)
        to_left(0, 3, chan)
        to_right(2, 3, chan)
        return carry

    lax.fori_loop(1, jnp.where(on_right, 2, per), send_rest, 0)

    conv_recv[pl.ds(channels * rows, mixed * rows), :] = jnp.zeros(
        (mixed * rows, lanes), jnp.float32
    )
    for group in range(ch_count):
        lag_recv[pl.ds((all_channels + group * channels) * sub_rows, mixed * sub_rows), :] = (
            jnp.zeros((mixed * sub_rows, lanes), jnp.float32)
        )

    @pl.when(on_right)
    def _():
        conv_recv[pl.ds((channels + mixed) * rows, (channels - mixed) * rows), :] = jnp.zeros(
            ((channels - mixed) * rows, lanes), jnp.float32
        )
        for group in range(ch_count):
            lag_recv[
                pl.ds(
                    (all_channels + group * channels + mixed) * sub_rows,
                    (channels - mixed) * sub_rows,
                ),
                :,
            ] = jnp.zeros(((channels - mixed) * sub_rows, lanes), jnp.float32)

        def keep_own(chan, carry):
            gather_full[0, chan, pl.ds(0, half * rows), :] = jnp.zeros(
                (half * rows, lanes), jnp.float32
            )
            for which in range(3):
                gather_full[which, chan, rows_of(seq_place), :] = send_buf[
                    which, rows_of(split_channel(side_place, chan)), :
                ]
            return carry

        lax.fori_loop(0, per, keep_own, 0)

    @pl.when(on_left)
    def _():
        def keep_own(chan, carry):
            for which in range(3):
                gather_half[which, chan, rows_of(side_place), :] = send_buf[
                    which, rows_of(split_channel(side_place, chan)), :
                ]
            return carry

        lax.fori_loop(0, per, keep_own, 0)

    @pl.when(on_inner)
    def _():
        for slot in range(mixed_per):
            for which in range(3):
                gather_full[which, slot, rows_of(seq_place), :] = send_buf[
                    which, rows_of((seq_place - inner) * mixed_per + slot), :
                ]

    for index in range(sub_rows):
        window_buf[index] = window_of(rate_buf[...], (flat_place * sub_rows + index) * lanes)

    for load in loads[6:]:
        load.wait()
    pl.semaphore_wait(met_sem.at[0], seq_count - 1)

    def send_conv(channel, slot, count, targets):
        each_other(
            seq_place,
            targets,
            lambda target: conv_copy(channel, slot, count, target).start(),
        )

    def send_lag(channel, slot, count, targets):
        each_other(
            flat_place,
            targets,
            lambda target: lag_copy(channel, slot, count, target).start(),
        )

    full_tables = (row_ref, row_back_ref, lane_ref, lane_back_ref, twist_ref)
    half_tables = (half_row_ref, half_back_ref, lane_ref, lane_back_ref, half_twist_ref)

    def work_full(chan, carry):
        slot = jnp.where(on_right, chan, per + chan)
        channel = jnp.where(
            on_right,
            split_channel(side_place, chan),
            (seq_place - inner) * mixed_per + chan,
        )

        @pl.when(on_right)
        def _():
            @pl.when(chan + 2 < per)
            def _():
                to_right(0, 2, chan + 2)

            counted((3 * half - 2) * rows, send_sem.at[0], full_sem.at[chan]).wait_recv()

        @pl.when(on_left)
        def _():
            counted(2 * (seq_count - 1) * rows, send_sem.at[0], full_sem.at[chan]).wait_recv()

        first, second = spectra([gather_full[0, chan], gather_full[1, chan]], full_tables)
        grad_freqs[...] = first
        lag_send[:, pl.ds(pl.multiple_of(slot * sub_rows, 8), sub_rows), :] = correlated(
            first, [second], full_tables
        ).reshape(total, sub_rows, lanes)

        @pl.when(on_right)
        def _():
            send_lag(channel, slot, 1, total)

        @pl.when(jnp.logical_and(on_right, chan + 2 < per))
        def _():
            to_right(2, 3, chan + 2)

        @pl.when(jnp.logical_and(on_left, chan == 1))
        def _():
            send_lag(channel - 1, slot - 1, 2, total)

        @pl.when(on_right)
        def _():
            counted((2 * half - 1) * rows, send_sem.at[0], filt_sem.at[chan]).wait_recv()

        @pl.when(on_left)
        def _():
            counted((seq_count - 1) * rows, send_sem.at[0], filt_sem.at[chan]).wait_recv()

        (third,) = spectra([gather_full[2, chan]], full_tables)
        conv_send[:, pl.ds(pl.multiple_of(slot * rows, 8), rows), :] = correlated(
            grad_freqs[...], [third], full_tables
        ).reshape(seq_count, rows, lanes)
        send_conv(channel, slot, 1, seq_count)
        return carry

    rounds = jnp.where(on_right, per, jnp.where(on_inner, mixed_per, 0))
    lax.fori_loop(0, rounds, work_full, 0)

    def work_half(chan, carry):
        counted(3 * (half - 1) * rows, send_sem.at[0], half_sem.at[chan]).wait_recv()
        first, second, third = spectra(
            [gather_half[which, chan] for which in range(3)], half_tables
        )
        final = correlated(first, [third, second], half_tables)
        channel = split_channel(side_place, chan)
        conv_send[:half, pl.ds(pl.multiple_of(chan * rows, 8), rows), :] = final[
            :, :lanes
        ].reshape(half, rows, lanes)
        lag_send[:left_total, pl.ds(pl.multiple_of(chan * sub_rows, 8), sub_rows), :] = final[
            :, lanes:
        ].reshape(left_total, sub_rows, lanes)

        @pl.when(lax.rem(chan, 2) == 1)
        def _():
            send_conv(channel - 1, chan - 1, 2, half)
            send_lag(channel - 1, chan - 1, 2, left_total)

        @pl.when(chan == per - 1)
        def _():
            send_conv(channel, chan, 1, half)
            send_lag(channel, chan, 1, left_total)

        return carry

    @pl.when(on_left)
    def _():
        lax.fori_loop(0, per, work_half, 0)

    def keep_back(channel, slot, count):
        conv_recv[pl.ds(pl.multiple_of(channel * rows, 8), count * rows), :] = conv_send[
            seq_place, pl.ds(pl.multiple_of(slot * rows, 8), count * rows), :
        ]
        lag_recv[pl.ds(lag_row(channel), count * sub_rows), :] = lag_send[
            flat_place, pl.ds(pl.multiple_of(slot * sub_rows, 8), count * sub_rows), :
        ]

    keep_back(split_channel(side_place, 0), 0, per)

    @pl.when(on_inner)
    def _():
        keep_back((seq_place - inner) * mixed_per, per, mixed_per)

    def expect(recv, unit, own_side, whole):
        for place, count in (
            (on_outer, own_side * per + whole * mixed_per + (own_side + 1) * per),
            (on_inner, own_side * per + (whole - 1) * mixed_per + (own_side + 1) * per),
            (on_right, own_side * per + whole * mixed_per),
        ):

            @pl.when(place)
            def _():
                counted(count * unit, send_sem.at[0], recv).wait_recv()

    def sent(index, outer_count, inner_count, right_count):
        for place, count in (
            (on_outer, outer_count),
            (on_inner, inner_count),
            (on_right, right_count),
        ):
            if count:

                @pl.when(place)
                def _():
                    counted(count, send_sem.at[index], back_sem.at[0]).wait_send()

    expect(back_sem.at[1], sub_rows, left_total - 1, inner * ch_count)
    weight = split_value(weight_ref[...])
    for index in range(sub_rows):
        tile = (
            lag_recv[pl.ds(index, all_channels, stride=sub_rows), :]
            + lag_recv[pl.ds(all_channels * sub_rows + index, all_channels, stride=sub_rows), :]
        ) * window_buf[index]
        feat_grad_ref[:, index * lanes : (index + 1) * lanes] = dot_split(
            weight, split_value(tile)
        )
    expect(back_sem.at[0], rows, half - 1, inner)
    local_bias = bias_buf[pl.ds(first_chan, channels), :]
    for index in range(rows):
        span = slice(index * lanes, (index + 1) * lanes)
        in_grad_ref[:, span] = (
            conv_recv[pl.ds(index, channels, stride=rows), :]
            + conv_recv[pl.ds(channels * rows + index, channels, stride=rows), :]
            + local_bias * grad_ref[:, span]
        )

    left_sent = 2 * half * per * rows
    own_side = 3 * (half - 1) * per * rows
    to_inner = 3 * mixed * rows
    to_inner_own = 3 * (mixed - mixed_per) * rows
    sent(0, left_sent, left_sent, own_side)
    sent(1, own_side, own_side, 0)
    sent(2, to_inner, to_inner_own, to_inner)
    side_back = (half - 1) * per * rows
    sent(
        3,
        side_back,
        side_back + (seq_count - 1) * mixed_per * rows,
        (seq_count - 1) * per * rows,
    )
    side_lag = (left_total - 1) * per * sub_rows
    sent(
        4,
        side_lag,
        side_lag + (total - 1) * mixed_per * sub_rows,
        (total - 1) * per * sub_rows,
    )


def local_whole(seq_count, ch_count, tables, *args):
    out_grad, gated_input, features, filter_weight, rates, skip_bias = args
    channels, local_len = out_grad.shape
    rows = local_len // lanes
    feats, all_channels = filter_weight.shape
    half, inner, mixed, mixed_per, per = plan(seq_count, channels)
    slots = per + mixed_per
    data_rows = rows * seq_count
    sub_rows = rows // ch_count
    total = seq_count * ch_count
    sizes = (seq_count, ch_count, channels, rows)
    in_vmem = pl.BlockSpec(memory_space=pltpu.VMEM)
    anywhere = pl.BlockSpec(memory_space=pl.ANY)
    dma = pltpu.SemaphoreType.DMA
    f32 = jnp.float32
    longest = max(
        3 * channels * rows,
        2 * channels * rows,
        2 * all_channels * sub_rows,
        seq_count * slots * rows,
        total * slots * sub_rows,
    )
    held = pl.pallas_call(
        functools.partial(whole_kernel, sizes),
        out_shape=(
            pltpu.VMEM((channels, local_len), f32),
            pltpu.VMEM((feats, sub_rows * lanes), f32),
        ),
        in_specs=[anywhere] * (6 + len(tables)),
        out_specs=(in_vmem, in_vmem),
        scratch_shapes=[
            pltpu.VMEM((channels, local_len), f32),
            pltpu.VMEM((channels, local_len), f32),
            pltpu.VMEM((feats, local_len), f32),
            *[pltpu.VMEM(table.shape, table.dtype) for table in tables],
            pltpu.VMEM((feats, all_channels), f32),
            pltpu.VMEM((1, all_channels), f32),
            pltpu.VMEM((1, all_channels), f32),
            dma((6 + len(tables),)),
            pltpu.VMEM((3, channels * rows, lanes), f32),
            pltpu.VMEM((3, per, data_rows, lanes), f32),
            pltpu.VMEM((3, per, half * rows, lanes), f32),
            pltpu.VMEM((seq_count, slots * rows, lanes), f32),
            pltpu.VMEM((total, slots * sub_rows, lanes), f32),
            pltpu.VMEM((2 * channels * rows, lanes), f32),
            pltpu.VMEM((2 * all_channels * sub_rows, lanes), f32),
            pltpu.VMEM((sub_rows, all_channels, lanes), f32),
            pltpu.VMEM((all_channels, lanes), f32),
            pltpu.VMEM((all_channels, lanes), f32),
            pltpu.VMEM((all_channels, feats), f32),
            pltpu.VMEM((longest, lanes), f32),
            pltpu.VMEM((data_rows, 2 * lanes), f32),
            dma((per,)),
            dma((per,)),
            dma((per,)),
            dma((5,)),
            dma((2,)),
            pltpu.SemaphoreType.REGULAR((1,)),
        ],
        compiler_params=pltpu.CompilerParams(collective_id=0, has_side_effects=True),
    )(
        out_grad,
        gated_input,
        features,
        filter_weight,
        rates.reshape(1, all_channels),
        skip_bias.reshape(1, all_channels),
        *[jnp.asarray(table) for table in tables],
    )
    held = [pltpu.with_memory_space_constraint(value, pltpu.VMEM) for value in held]
    return pl.pallas_call(
        store_kernel,
        out_shape=tuple(jax.ShapeDtypeStruct(value.shape, f32) for value in held),
        in_specs=[in_vmem] * 2,
        out_specs=(anywhere, anywhere),
        scratch_shapes=[dma((2,))],
    )(*held)


def store_kernel(first_ref, second_ref, first_hbm, second_hbm, sem):
    stores = [
        pltpu.make_async_copy(first_ref, first_hbm, sem.at[0]),
        pltpu.make_async_copy(second_ref, second_hbm, sem.at[1]),
    ]
    for store in stores:
        store.start()
    for store in stores:
        store.wait()


def solution(mesh):
    seq_count, ch_count = mesh.shape["seq"], mesh.shape["ch"]
    in_specs = (P("ch", "seq"), P("ch", "seq"), P(None, "seq"), P(), P(), P())
    out_specs = (P("ch", "seq"), P(None, ("seq", "ch")))

    def whole(*args):
        channels, full_len = args[0].shape
        channels = channels // ch_count
        local_len = full_len // seq_count
        half, inner, mixed, mixed_per, per = plan(seq_count, channels)
        fits = (
            seq_count % 4 == 0
            and channels % 8 == 0
            and mixed == inner * mixed_per
            and mixed_per == 2
            and mixed + half * per == channels
            and per % 2 == 1
            and per >= 5
            and local_len % (8 * lanes * ch_count) == 0
            and full_len <= 512 * lanes
        )
        body = local
        if fits:
            row, row_back, lane, lane_back, twist = make_tables(full_len // lanes)
            half_row, half_back, _, _, half_twist = make_tables(full_len // lanes // 2)
            tables = (row, row_back, lane, lane_back, twist, half_row, half_back * 2, half_twist)
            body = functools.partial(local_whole, seq_count, ch_count, tables)
        return jax.shard_map(
            body, mesh=mesh, in_specs=in_specs, out_specs=out_specs, check_vma=False
        )(*args)

    return whole
```

```python
import functools
import math

import jax
import jax.numpy as jnp
import numpy as np
from jax import lax
from jax.experimental import pallas as pl
from jax.experimental.pallas import tpu as pltpu
from jax.sharding import PartitionSpec as P

shift_term = 0.05
highest = lax.Precision.HIGHEST


def matmul_high(operand, matrix):
    return jnp.dot(operand, matrix, precision=highest, preferred_element_type=jnp.float32)


def angle_table(first_ids, second_ids, period):
    product = first_ids[:, None] * second_ids[None, :] % period
    angles = product.astype(jnp.float32) * (2.0 * math.pi / period)
    return (jnp.cos(angles), jnp.sin(angles))


def contract(real_part, imag_part, cos_table, sin_table, einsum_form):

    def multiply_by(operand, matrix):
        return jnp.einsum(
            einsum_form, operand, matrix, precision=highest, preferred_element_type=jnp.float32
        )

    return (
        multiply_by(real_part, cos_table) - multiply_by(imag_part, sin_table),
        multiply_by(real_part, sin_table) + multiply_by(imag_part, cos_table),
    )


def group_width(channels, block_len):
    return math.gcd(channels, max(1, 128 // block_len)) * block_len


def group_table(width, block_len, sign_term):
    ids = jnp.arange(width, dtype=jnp.int32)
    same = ids[:, None] // block_len == ids[None, :] // block_len
    inner = ids % block_len
    product = inner[:, None] * inner[None, :] % block_len
    angles = product.astype(jnp.float32) * (2.0 * math.pi / block_len)
    return (
        jnp.where(same, jnp.cos(angles), 0.0).astype(jnp.float32),
        jnp.where(same, sign_term * jnp.sin(angles), 0.0).astype(jnp.float32),
    )


def local_transform(real_part, imag_part, block_len, inverse):
    rows, seq_count, width_all = real_part.shape
    channels = width_all // block_len
    local_len = seq_count * block_len
    width = group_width(channels, block_len)
    sign_term = 1.0 if inverse else -1.0
    seq_ids = jnp.arange(seq_count, dtype=jnp.int32)
    block_ids = jnp.arange(block_len, dtype=jnp.int32)
    cos_seq, sin_seq = angle_table(seq_ids, seq_ids, seq_count)
    sin_seq = sign_term * sin_seq
    cos_twist, sin_twist = angle_table(seq_ids, block_ids, local_len)
    cos_twist = jnp.tile(cos_twist, (1, channels))
    sin_twist = sign_term * jnp.tile(sin_twist, (1, channels))
    cos_group, sin_group = group_table(width, block_len, sign_term)
    grouped = (rows, seq_count, width_all // width, width)
    flat = (rows, seq_count, width_all)

    def twist(re_part, im_part):
        return (
            re_part * cos_twist - im_part * sin_twist,
            re_part * sin_twist + im_part * cos_twist,
        )

    def across_groups(re_part, im_part):
        re_part, im_part = contract(
            re_part.reshape(grouped),
            im_part.reshape(grouped),
            cos_group,
            sin_group,
            "rkgm,mq->rkgq",
        )
        return (re_part.reshape(flat), im_part.reshape(flat))

    if inverse:
        real_part, imag_part = across_groups(real_part, imag_part)
        real_part, imag_part = twist(real_part, imag_part)
        real_part, imag_part = contract(real_part, imag_part, cos_seq, sin_seq, "rsx,sk->rkx")
    else:
        real_part, imag_part = contract(real_part, imag_part, cos_seq, sin_seq, "rsx,sk->rkx")
        real_part, imag_part = twist(real_part, imag_part)
        real_part, imag_part = across_groups(real_part, imag_part)
    return (real_part, imag_part)


def first_section(row_block, cos_fwd, sin_fwd, twid_cos, twid_sin):
    real_part = matmul_high(cos_fwd, row_block)
    imag_part = -matmul_high(sin_fwd, row_block)
    real_out = real_part * twid_cos + imag_part * twid_sin
    imag_out = imag_part * twid_cos - real_part * twid_sin
    return (real_out[:, None, :], imag_out[:, None, :])


def rotate_back(real_part, imag_part, twid_cos, twid_sin):
    return (
        real_part * twid_cos - imag_part * twid_sin,
        real_part * twid_sin + imag_part * twid_cos,
    )


def forward_products(
    block_len, grad_real, grad_imag, input_real, input_imag, filter_real, filter_imag
):
    grad_real, grad_imag = local_transform(grad_real, grad_imag, block_len, False)
    input_real, input_imag = local_transform(input_real, input_imag, block_len, False)
    filter_real, filter_imag = local_transform(filter_real, filter_imag, block_len, False)
    corr_real = filter_real * grad_real + filter_imag * grad_imag
    corr_imag = filter_real * grad_imag - filter_imag * grad_real
    lag_real = input_real * grad_real + input_imag * grad_imag
    lag_imag = input_real * grad_imag - input_imag * grad_real
    return (corr_real, corr_imag, lag_real, lag_imag)


def products_inverted(block_len, operands):
    corr_real, corr_imag, lag_real, lag_imag = forward_products(block_len, *operands)
    corr_real, corr_imag = local_transform(corr_real, corr_imag, block_len, True)
    lag_real, lag_imag = local_transform(lag_real, lag_imag, block_len, True)
    return (corr_real, corr_imag, lag_real, lag_imag)


def paired_rows(block_len, operands):
    seq_count = operands[0].shape[1]
    channels = operands[0].shape[2] // block_len
    local_len = seq_count * block_len
    positions = (
        jnp.arange(seq_count, dtype=jnp.int32)[:, None] * block_len
        + jnp.arange(block_len, dtype=jnp.int32)[None, :]
    )
    angles = positions.astype(jnp.float32) * (math.pi / local_len)
    half_cos = jnp.tile(jnp.cos(angles), (1, channels))
    half_sin = jnp.tile(jnp.sin(angles), (1, channels))
    stacked = []
    for index in range(3):
        low_row = operands[2 * index]
        high_row = operands[2 * index + 1]
        stacked.append(jnp.concatenate([low_row, high_row * half_cos], axis=0))
        stacked.append(jnp.concatenate([jnp.zeros_like(low_row), -high_row * half_sin], axis=0))
    corr_real, corr_imag, lag_real, lag_imag = products_inverted(block_len, tuple(stacked))
    return (
        corr_real[0:1],
        corr_real[1:2] * half_cos - corr_imag[1:2] * half_sin,
        lag_real[0:1],
        lag_real[1:2] * half_cos - lag_imag[1:2] * half_sin,
    )


def local(out_grad, gated_input, features, filter_weight, rates, skip_bias):
    channels, local_len = out_grad.shape
    seq_count = lax.axis_size("seq")
    block_len = local_len // seq_count
    width_all = channels * block_len
    freq_count = 2 * seq_count
    full_len = local_len * seq_count
    padded_len = 2 * full_len
    seq_place = lax.axis_index("seq")
    first_chan = lax.axis_index("ch") * channels
    local_rates = lax.dynamic_slice_in_dim(rates, first_chan, channels)
    local_bias = lax.dynamic_slice_in_dim(skip_bias, first_chan, channels)
    local_weight = lax.dynamic_slice_in_dim(filter_weight, first_chan, channels, 1)
    position = seq_place * local_len + jnp.arange(local_len, dtype=jnp.int32)
    window = (
        jnp.exp(-local_rates[:, None] * (position.astype(jnp.float32) / full_len)[None, :])
        + shift_term
    )
    filter_vals = matmul_high(local_weight.T, features) * window

    def to_rows(values):
        return (
            values.reshape(channels, seq_count, block_len)
            .transpose(1, 0, 2)
            .reshape(seq_count, width_all)
        )

    received = (
        lax.all_to_all(to_rows(out_grad), "seq", split_axis=0, concat_axis=0, tiled=True),
        lax.all_to_all(to_rows(gated_input), "seq", split_axis=0, concat_axis=0, tiled=True),
        lax.all_to_all(to_rows(filter_vals), "seq", split_axis=0, concat_axis=0, tiled=True),
    )

    def inverted(operands):
        return products_inverted(block_len, operands)

    def paired(operands):
        return paired_rows(block_len, operands)

    freq_ids = jnp.arange(freq_count, dtype=jnp.int32)
    dev_ids = jnp.arange(seq_count, dtype=jnp.int32)
    local_m = seq_place * block_len + jnp.arange(block_len, dtype=jnp.int32)
    twid_cos, twid_sin = angle_table(freq_ids, local_m, padded_len)
    twid_cos = jnp.tile(twid_cos, (1, channels))
    twid_sin = jnp.tile(twid_sin, (1, channels))
    scale_term = 1.0 / padded_len
    alternate = jnp.where(dev_ids % 2 == 0, 1.0, -1.0).astype(jnp.float32)
    cos_half, sin_half = angle_table(dev_ids, dev_ids, freq_count)
    sin_half = jnp.where(dev_ids[:, None] == 0, -alternate[None, :], sin_half)
    twid_half_cos = twid_cos[:seq_count]
    twid_half_sin = twid_sin[:seq_count]
    spread = [
        first_section(piece, cos_half, sin_half, twid_half_cos, twid_half_sin) for piece in received
    ]
    exchanged = (
        lax.all_to_all(spread[0][0], "seq", split_axis=0, concat_axis=1, tiled=True),
        lax.all_to_all(spread[0][1], "seq", split_axis=0, concat_axis=1, tiled=True),
        lax.all_to_all(spread[1][0], "seq", split_axis=0, concat_axis=1, tiled=True),
        lax.all_to_all(spread[1][1], "seq", split_axis=0, concat_axis=1, tiled=True),
        lax.all_to_all(spread[2][0], "seq", split_axis=0, concat_axis=1, tiled=True),
        lax.all_to_all(spread[2][1], "seq", split_axis=0, concat_axis=1, tiled=True),
    )
    corr_real, corr_imag, lag_real, lag_imag = lax.cond(
        seq_place == 0, paired, inverted, tuple(exchanged)
    )
    corr_real, corr_imag, lag_real, lag_imag = (
        lax.all_to_all(corr_real, "seq", split_axis=1, concat_axis=0, tiled=True),
        lax.all_to_all(corr_imag, "seq", split_axis=1, concat_axis=0, tiled=True),
        lax.all_to_all(lag_real, "seq", split_axis=1, concat_axis=0, tiled=True),
        lax.all_to_all(lag_imag, "seq", split_axis=1, concat_axis=0, tiled=True),
    )
    corr_flat_real, corr_flat_imag = rotate_back(
        corr_real.reshape(seq_count, width_all),
        corr_imag.reshape(seq_count, width_all),
        twid_half_cos,
        twid_half_sin,
    )
    lag_flat_real, lag_flat_imag = rotate_back(
        lag_real.reshape(seq_count, width_all),
        lag_imag.reshape(seq_count, width_all),
        twid_half_cos,
        twid_half_sin,
    )
    cos_final, sin_final = angle_table(dev_ids, dev_ids, freq_count)
    cos_final = jnp.where(dev_ids[None, :] == 0, 1.0, 2.0 * cos_final)
    sin_final = jnp.where(dev_ids[None, :] == 0, -alternate[:, None], 2.0 * sin_final)
    conv_rows = (
        matmul_high(cos_final, corr_flat_real) - matmul_high(sin_final, corr_flat_imag)
    ) * scale_term
    lag_rows = (
        matmul_high(cos_final, lag_flat_real) - matmul_high(sin_final, lag_flat_imag)
    ) * scale_term
    conv_back, lag_back = (
        lax.all_to_all(conv_rows, "seq", split_axis=0, concat_axis=0, tiled=True),
        lax.all_to_all(lag_rows, "seq", split_axis=0, concat_axis=0, tiled=True),
    )

    def to_channels(values):
        return (
            values.reshape(seq_count, channels, block_len)
            .transpose(1, 0, 2)
            .reshape(channels, local_len)
        )

    conv_grad = to_channels(conv_back)
    filt_grad = to_channels(lag_back)
    in_grad = conv_grad + local_bias[:, None] * out_grad
    weighted = filt_grad * window
    regrouped = lax.all_to_all(weighted, "ch", split_axis=1, concat_axis=0, tiled=True)
    feat_grad = matmul_high(filter_weight, regrouped)
    return (in_grad, feat_grad)


lanes = 128


def split_table(table):
    table = np.asarray(table, np.float32)
    high_part = table.astype(jnp.bfloat16)
    low_part = (table - high_part.astype(np.float32)).astype(jnp.bfloat16)
    return np.stack([high_part, low_part])


def make_tables(data_rows):
    freq_rows = 2 * data_rows
    padded_len = freq_rows * lanes
    odd_ids = 2 * np.arange(data_rows) + 1
    row_angle = (odd_ids[:, None] * np.arange(data_rows)[None, :] % (2 * freq_rows)) * (
        math.pi / freq_rows
    )
    row_table = np.concatenate([np.cos(row_angle), -np.sin(row_angle)], axis=0)
    lane_ids = np.arange(lanes)
    twist_angle = (odd_ids[:, None] * lane_ids[None, :]) * (math.pi / padded_len)
    twist = np.stack([np.cos(twist_angle), -np.sin(twist_angle)]).astype(np.float32)
    lane_angle = (lane_ids[:, None] * lane_ids[None, :] % lanes) * (2.0 * math.pi / lanes)
    lane_cos, lane_sin = np.cos(lane_angle), np.sin(lane_angle)
    lane_table = np.block([[lane_cos, -lane_sin], [lane_sin, lane_cos]])
    back_table = np.block([[lane_cos, lane_sin], [-lane_sin, lane_cos]]) * (2.0 / padded_len)
    return (
        split_table(row_table),
        split_table(row_table.T),
        split_table(lane_table),
        split_table(back_table),
        twist,
    )


def split_value(value):
    high_part = value.astype(jnp.bfloat16)
    return high_part, (value - high_part.astype(jnp.float32)).astype(jnp.bfloat16)


def dot_split(left, right):
    def product(first, second):
        return jnp.dot(first, second, preferred_element_type=jnp.float32)

    return product(left[0], right[0]) + (product(left[0], right[1]) + product(left[1], right[0]))


def spectra(pieces, tables):
    row_ref, lane_ref, twist_ref = tables[0], tables[2], tables[4]
    data_rows = pieces[0].shape[0]
    twist_cos, twist_sin = twist_ref[0], twist_ref[1]
    packed = pieces[0] if len(pieces) == 1 else jnp.concatenate(pieces, axis=1)
    spread = dot_split((row_ref[0], row_ref[1]), split_value(packed))
    freqs = []
    for which in range(len(pieces)):
        re_part = spread[:data_rows, which * lanes : (which + 1) * lanes]
        im_part = spread[data_rows:, which * lanes : (which + 1) * lanes]
        turned = jnp.concatenate(
            [
                re_part * twist_cos - im_part * twist_sin,
                re_part * twist_sin + im_part * twist_cos,
            ],
            axis=1,
        )
        freqs.append(dot_split(split_value(turned), (lane_ref[0], lane_ref[1])))
    return freqs


def correlated(grad_freqs, others, tables):
    row_back_ref, lane_back_ref, twist_ref = tables[1], tables[3], tables[4]
    twist_cos, twist_sin = twist_ref[0], twist_ref[1]
    grad_re, grad_im = grad_freqs[:, :lanes], grad_freqs[:, lanes:]
    turned = []
    for spectrum in others:
        re_part, im_part = spectrum[:, :lanes], spectrum[:, lanes:]
        product = jnp.concatenate(
            [
                re_part * grad_re + im_part * grad_im,
                re_part * grad_im - im_part * grad_re,
            ],
            axis=1,
        )
        back = dot_split(split_value(product), (lane_back_ref[0], lane_back_ref[1]))
        re_part, im_part = back[:, :lanes], back[:, lanes:]
        turned.append(
            jnp.concatenate(
                [
                    re_part * twist_cos + im_part * twist_sin,
                    im_part * twist_cos - re_part * twist_sin,
                ],
                axis=0,
            )
        )
    both = turned[0] if len(turned) == 1 else jnp.concatenate(turned, axis=1)
    return dot_split((row_back_ref[0], row_back_ref[1]), split_value(both))


def plan(seq_count, channels):
    half = seq_count // 2
    mixed = channels // 8
    inner = half // 2
    return half, inner, mixed, mixed // max(inner, 1), (channels - mixed) // half


def whole_kernel(sizes, *refs):
    (
        grad_hbm,
        input_hbm,
        feat_hbm,
        weight_hbm,
        rate_hbm,
        bias_hbm,
        row_hbm,
        row_back_hbm,
        lane_hbm,
        lane_back_hbm,
        twist_hbm,
        half_row_hbm,
        half_back_hbm,
        half_twist_hbm,
        in_grad_ref,
        feat_grad_ref,
        grad_ref,
        input_ref,
        feat_ref,
        row_ref,
        row_back_ref,
        lane_ref,
        lane_back_ref,
        twist_ref,
        half_row_ref,
        half_back_ref,
        half_twist_ref,
        weight_ref,
        rate_ref,
        bias_ref,
        load_sem,
        send_buf,
        gather_full,
        gather_half,
        conv_send,
        lag_send,
        conv_recv,
        lag_recv,
        window_buf,
        rate_buf,
        bias_buf,
        weight_buf,
        ruler,
        grad_freqs,
        full_sem,
        filt_sem,
        half_sem,
        send_sem,
        back_sem,
        met_sem,
    ) = refs
    seq_count, ch_count, channels, rows = sizes
    half, inner, mixed, mixed_per, per = plan(seq_count, channels)
    data_rows = rows * seq_count
    sub_rows = rows // ch_count
    all_channels = channels * ch_count
    total = seq_count * ch_count
    left_total = half * ch_count
    full_len = data_rows * lanes
    seq_place = lax.axis_index("seq")
    ch_place = lax.axis_index("ch")
    flat_place = seq_place * ch_count + ch_place
    on_right = seq_place >= half
    on_left = seq_place < half
    on_inner = jnp.logical_and(seq_place >= inner, on_left)
    on_outer = seq_place < inner
    side_place = lax.rem(seq_place, half)
    here = {"seq": seq_place, "ch": ch_place}

    loads = [
        pltpu.make_async_copy(source, target, load_sem.at[index])
        for index, (source, target) in enumerate(
            (
                (grad_hbm, grad_ref),
                (input_hbm, input_ref),
                (weight_hbm, weight_ref),
                (rate_hbm, rate_ref),
                (bias_hbm, bias_ref),
                (feat_hbm, feat_ref),
                (row_hbm, row_ref),
                (twist_hbm, twist_ref),
                (lane_hbm, lane_ref),
                (lane_back_hbm, lane_back_ref),
                (row_back_hbm, row_back_ref),
                (half_row_hbm, half_row_ref),
                (half_back_hbm, half_back_ref),
                (half_twist_hbm, half_twist_ref),
            )
        )
    ]
    barrier = pltpu.get_barrier_semaphore()

    def signal(sem, seq, ch):
        pl.semaphore_signal(
            sem, inc=1, device_id={"seq": seq, "ch": ch}, device_id_type=pl.DeviceIdType.MESH
        )

    for step in range(1, seq_count):
        signal(barrier, lax.rem(seq_place + step, seq_count), ch_place)
    for step in range(1, ch_count):
        signal(barrier, seq_place, lax.rem(ch_place + step, ch_count))
    for load in loads:
        load.start()

    def each_other(place, count, visit, first=1):
        def one(step, carry):
            visit(lax.rem(place + step, count))
            return carry

        lax.fori_loop(first, count, one, 0)

    def remote(source, target, send, recv, device):
        return pltpu.make_async_remote_copy(
            src_ref=source,
            dst_ref=target,
            send_sem=send,
            recv_sem=recv,
            device_id=device,
            device_id_type=pl.DeviceIdType.MESH,
        )

    def counted(count, send, recv):
        part = ruler.at[pl.ds(0, count)]
        return remote(part, part, send, recv, here)

    def rows_of(channel):
        return pl.ds(pl.multiple_of(channel * rows, 8), rows)

    def split_channel(side, chan):
        return mixed + side * per + chan

    def full_copy(first, last, channel, slot, target, sem):
        return remote(
            send_buf.at[first:last, rows_of(channel)],
            gather_full.at[first:last, slot, rows_of(seq_place)],
            send_sem.at[sem],
            (filt_sem if first == 2 else full_sem).at[slot],
            {"seq": target, "ch": ch_place},
        )

    def half_copy(first, last, channel, slot, target):
        return remote(
            send_buf.at[first:last, rows_of(channel)],
            gather_half.at[first:last, slot, rows_of(side_place)],
            send_sem.at[1],
            half_sem.at[slot],
            {"seq": target, "ch": ch_place},
        )

    def send_mixed(first, last):
        for side in range(inner):
            target = inner + side

            @pl.when(seq_place != target)
            def _():
                for slot in range(mixed_per):
                    channel = side * mixed_per + slot
                    full_copy(first, last, channel, slot, target, 2).start()

    def to_right(first, last, chan):
        @pl.when(on_left)
        def _():
            for step in range(half):
                side = step // 2 * 2 + lax.rem(step + seq_place, 2)
                full_copy(
                    max(first, 1), last, split_channel(side, chan), chan, half + side, 0
                ).start()

        @pl.when(on_right)
        def _():
            each_other(
                side_place,
                half,
                lambda side: full_copy(
                    first, last, split_channel(side, chan), chan, half + side, 0
                ).start(),
            )

    def to_left(first, last, chan):
        @pl.when(on_left)
        def _():
            each_other(
                side_place,
                half,
                lambda side: half_copy(
                    first, last, split_channel(side, chan), chan, side
                ).start(),
            )

    def conv_copy(channel, slot, count, target):
        part = jnp.where(jnp.logical_and(on_right, target < half), channels, 0)
        return remote(
            conv_send.at[target, pl.ds(pl.multiple_of(slot * rows, 8), count * rows)],
            conv_recv.at[pl.ds(pl.multiple_of((part + channel) * rows, 8), count * rows)],
            send_sem.at[3],
            back_sem.at[jnp.where(part > 0, 2, 0)],
            {"seq": target, "ch": ch_place},
        )

    def lag_row(channel):
        return pl.multiple_of((ch_place * channels + channel) * sub_rows, 8)

    def lag_copy(channel, slot, count, target):
        part = jnp.where(jnp.logical_and(on_right, target < left_total), all_channels, 0)
        return remote(
            lag_send.at[target, pl.ds(pl.multiple_of(slot * sub_rows, 8), count * sub_rows)],
            lag_recv.at[
                pl.ds(
                    pl.multiple_of(part * sub_rows + lag_row(channel), 8), count * sub_rows
                )
            ],
            send_sem.at[4],
            back_sem.at[1],
            {"seq": target // ch_count, "ch": lax.rem(target, ch_count)},
        )

    def to_rows(which, index, tile):
        send_buf[which, pl.ds(index, channels, stride=rows), :] = tile

    loads[0].wait()
    for index in range(rows):
        to_rows(0, index, grad_ref[:, index * lanes : (index + 1) * lanes])
    loads[1].wait()
    for index in range(rows):
        to_rows(1, index, input_ref[:, index * lanes : (index + 1) * lanes])

    for load in loads[2:5]:
        load.wait()
    rate_buf[...] = jnp.broadcast_to(rate_ref[...], (lanes, all_channels)).T
    weight_buf[...] = weight_ref[...].T
    bias_buf[...] = jnp.broadcast_to(bias_ref[...], (lanes, all_channels)).T

    pl.semaphore_wait(barrier, seq_count + ch_count - 2)

    @pl.when(on_right)
    def _():
        send_mixed(0, 2)

    to_right(0, 2, 0)
    to_left(0, 2, 0)

    @pl.when(on_left)
    def _():
        send_mixed(0, 2)


    for step in range(1, seq_count):
        signal(met_sem.at[0], lax.rem(seq_place + step, seq_count), ch_place)

    first_chan = pl.multiple_of(ch_place * channels, 8)
    local_rates = rate_buf[pl.ds(first_chan, channels), :]
    local_weight = split_value(weight_buf[pl.ds(first_chan, channels), :])
    lane_ids = lax.broadcasted_iota(jnp.int32, (1, lanes), 1)

    def window_of(rates, first):
        steps_t = (first + lane_ids).astype(jnp.float32) / full_len
        return jnp.exp(-rates * steps_t) + shift_term

    loads[5].wait()
    chunk = math.gcd(rows, 4)
    for outer in range(rows // chunk):
        lo = outer * chunk * lanes
        block = split_value(feat_ref[:, lo : lo + chunk * lanes])
        values = dot_split(local_weight, block)
        for inside in range(chunk):
            index = outer * chunk + inside
            window = window_of(local_rates, (seq_place * rows + index) * lanes)
            to_rows(2, index, values[:, inside * lanes : (inside + 1) * lanes] * window)

    send_mixed(2, 3)
    to_right(2, 3, 0)
    to_left(2, 3, 0)

    def send_rest(chan, carry):
        to_right(0, 2, chan)
        to_left(0, 3, chan)
        to_right(2, 3, chan)
        return carry

    lax.fori_loop(1, jnp.where(on_right, 2, per), send_rest, 0)

    conv_recv[pl.ds(channels * rows, mixed * rows), :] = jnp.zeros(
        (mixed * rows, lanes), jnp.float32
    )
    for group in range(ch_count):
        lag_recv[pl.ds((all_channels + group * channels) * sub_rows, mixed * sub_rows), :] = (
            jnp.zeros((mixed * sub_rows, lanes), jnp.float32)
        )

    @pl.when(on_right)
    def _():
        conv_recv[pl.ds((channels + mixed) * rows, (channels - mixed) * rows), :] = jnp.zeros(
            ((channels - mixed) * rows, lanes), jnp.float32
        )
        for group in range(ch_count):
            lag_recv[
                pl.ds(
                    (all_channels + group * channels + mixed) * sub_rows,
                    (channels - mixed) * sub_rows,
                ),
                :,
            ] = jnp.zeros(((channels - mixed) * sub_rows, lanes), jnp.float32)

        def keep_own(chan, carry):
            gather_full[0, chan, pl.ds(0, half * rows), :] = jnp.zeros(
                (half * rows, lanes), jnp.float32
            )
            for which in range(3):
                gather_full[which, chan, rows_of(seq_place), :] = send_buf[
                    which, rows_of(split_channel(side_place, chan)), :
                ]
            return carry

        lax.fori_loop(0, per, keep_own, 0)

    @pl.when(on_left)
    def _():
        def keep_own(chan, carry):
            for which in range(3):
                gather_half[which, chan, rows_of(side_place), :] = send_buf[
                    which, rows_of(split_channel(side_place, chan)), :
                ]
            return carry

        lax.fori_loop(0, per, keep_own, 0)

    @pl.when(on_inner)
    def _():
        for slot in range(mixed_per):
            for which in range(3):
                gather_full[which, slot, rows_of(seq_place), :] = send_buf[
                    which, rows_of((seq_place - inner) * mixed_per + slot), :
                ]

    for index in range(sub_rows):
        window_buf[index] = window_of(rate_buf[...], (flat_place * sub_rows + index) * lanes)

    for load in loads[6:]:
        load.wait()
    pl.semaphore_wait(met_sem.at[0], seq_count - 1)

    def send_conv(channel, slot, count, targets):
        each_other(
            seq_place,
            targets,
            lambda target: conv_copy(channel, slot, count, target).start(),
        )

    def send_lag(channel, slot, count, targets):
        each_other(
            flat_place,
            targets,
            lambda target: lag_copy(channel, slot, count, target).start(),
        )

    full_tables = (row_ref, row_back_ref, lane_ref, lane_back_ref, twist_ref)
    half_tables = (half_row_ref, half_back_ref, lane_ref, lane_back_ref, half_twist_ref)

    def work_full(chan, carry):
        slot = jnp.where(on_right, chan, per + chan)
        channel = jnp.where(
            on_right,
            split_channel(side_place, chan),
            (seq_place - inner) * mixed_per + chan,
        )

        @pl.when(on_right)
        def _():
            @pl.when(chan + 2 < per)
            def _():
                to_right(0, 2, chan + 2)

            counted((3 * half - 2) * rows, send_sem.at[0], full_sem.at[chan]).wait_recv()

        @pl.when(on_left)
        def _():
            counted(2 * (seq_count - 1) * rows, send_sem.at[0], full_sem.at[chan]).wait_recv()

        first, second = spectra([gather_full[0, chan], gather_full[1, chan]], full_tables)
        grad_freqs[...] = first
        lag_send[:, pl.ds(pl.multiple_of(slot * sub_rows, 8), sub_rows), :] = correlated(
            first, [second], full_tables
        ).reshape(total, sub_rows, lanes)

        @pl.when(on_right)
        def _():
            send_lag(channel, slot, 1, total)

        @pl.when(jnp.logical_and(on_right, chan + 2 < per))
        def _():
            to_right(2, 3, chan + 2)

        @pl.when(jnp.logical_and(on_left, chan == 1))
        def _():
            send_lag(channel - 1, slot - 1, 2, total)

        @pl.when(on_right)
        def _():
            counted((2 * half - 1) * rows, send_sem.at[0], filt_sem.at[chan]).wait_recv()

        @pl.when(on_left)
        def _():
            counted((seq_count - 1) * rows, send_sem.at[0], filt_sem.at[chan]).wait_recv()

        (third,) = spectra([gather_full[2, chan]], full_tables)
        conv_send[:, pl.ds(pl.multiple_of(slot * rows, 8), rows), :] = correlated(
            grad_freqs[...], [third], full_tables
        ).reshape(seq_count, rows, lanes)
        send_conv(channel, slot, 1, seq_count)
        return carry

    rounds = jnp.where(on_right, per, jnp.where(on_inner, mixed_per, 0))
    lax.fori_loop(0, rounds, work_full, 0)

    def work_half(chan, carry):
        counted(3 * (half - 1) * rows, send_sem.at[0], half_sem.at[chan]).wait_recv()
        first, second, third = spectra(
            [gather_half[which, chan] for which in range(3)], half_tables
        )
        final = correlated(first, [third, second], half_tables)
        channel = split_channel(side_place, chan)
        conv_send[:half, pl.ds(pl.multiple_of(chan * rows, 8), rows), :] = final[
            :, :lanes
        ].reshape(half, rows, lanes)
        lag_send[:left_total, pl.ds(pl.multiple_of(chan * sub_rows, 8), sub_rows), :] = final[
            :, lanes:
        ].reshape(left_total, sub_rows, lanes)

        @pl.when(lax.rem(chan, 2) == 1)
        def _():
            send_conv(channel - 1, chan - 1, 2, half)
            send_lag(channel - 1, chan - 1, 2, left_total)

        @pl.when(chan == per - 1)
        def _():
            send_conv(channel, chan, 1, half)
            send_lag(channel, chan, 1, left_total)

        return carry

    @pl.when(on_left)
    def _():
        lax.fori_loop(0, per, work_half, 0)

    def keep_back(channel, slot, count):
        conv_recv[pl.ds(pl.multiple_of(channel * rows, 8), count * rows), :] = conv_send[
            seq_place, pl.ds(pl.multiple_of(slot * rows, 8), count * rows), :
        ]
        lag_recv[pl.ds(lag_row(channel), count * sub_rows), :] = lag_send[
            flat_place, pl.ds(pl.multiple_of(slot * sub_rows, 8), count * sub_rows), :
        ]

    keep_back(split_channel(side_place, 0), 0, per)

    @pl.when(on_inner)
    def _():
        keep_back((seq_place - inner) * mixed_per, per, mixed_per)

    def expect(recv, unit, own_side, whole, across):
        for place, count in (
            (on_outer, own_side * per + whole * mixed_per + across * per),
            (on_inner, own_side * per + (whole - 1) * mixed_per + across * per),
            (on_right, own_side * per + whole * mixed_per),
        ):

            @pl.when(place)
            def _():
                counted(count * unit, send_sem.at[0], recv).wait_recv()

    def sent(index, outer_count, inner_count, right_count):
        for place, count in (
            (on_outer, outer_count),
            (on_inner, inner_count),
            (on_right, right_count),
        ):
            if count:

                @pl.when(place)
                def _():
                    counted(count, send_sem.at[index], back_sem.at[0]).wait_send()

    expect(back_sem.at[1], sub_rows, left_total - 1, inner * ch_count, left_total)
    weight = split_value(weight_ref[...])
    for index in range(sub_rows):
        tile = (
            lag_recv[pl.ds(index, all_channels, stride=sub_rows), :]
            + lag_recv[pl.ds(all_channels * sub_rows + index, all_channels, stride=sub_rows), :]
        ) * window_buf[index]
        feat_grad_ref[:, index * lanes : (index + 1) * lanes] = dot_split(
            weight, split_value(tile)
        )
    expect(back_sem.at[0], rows, half - 1, inner, 0)
    local_bias = bias_buf[pl.ds(first_chan, channels), :]
    for index in range(rows):
        span = slice(index * lanes, (index + 1) * lanes)
        in_grad_ref[:, span] = (
            conv_recv[pl.ds(index, channels, stride=rows), :] + local_bias * grad_ref[:, span]
        )

    @pl.when(on_left)
    def _():
        counted(half * per * rows, send_sem.at[0], back_sem.at[2]).wait_recv()
        for index in range(rows):
            span = slice(index * lanes, (index + 1) * lanes)
            in_grad_ref[:, span] = (
                in_grad_ref[:, span]
                + conv_recv[pl.ds(channels * rows + index, channels, stride=rows), :]
            )

    left_sent = 2 * half * per * rows
    own_side = 3 * (half - 1) * per * rows
    to_inner = 3 * mixed * rows
    to_inner_own = 3 * (mixed - mixed_per) * rows
    sent(0, left_sent, left_sent, own_side)
    sent(1, own_side, own_side, 0)
    sent(2, to_inner, to_inner_own, to_inner)
    side_back = (half - 1) * per * rows
    sent(
        3,
        side_back,
        side_back + (seq_count - 1) * mixed_per * rows,
        (seq_count - 1) * per * rows,
    )
    side_lag = (left_total - 1) * per * sub_rows
    sent(
        4,
        side_lag,
        side_lag + (total - 1) * mixed_per * sub_rows,
        (total - 1) * per * sub_rows,
    )


def local_whole(seq_count, ch_count, tables, *args):
    out_grad, gated_input, features, filter_weight, rates, skip_bias = args
    channels, local_len = out_grad.shape
    rows = local_len // lanes
    feats, all_channels = filter_weight.shape
    half, inner, mixed, mixed_per, per = plan(seq_count, channels)
    slots = per + mixed_per
    data_rows = rows * seq_count
    sub_rows = rows // ch_count
    total = seq_count * ch_count
    sizes = (seq_count, ch_count, channels, rows)
    in_vmem = pl.BlockSpec(memory_space=pltpu.VMEM)
    anywhere = pl.BlockSpec(memory_space=pl.ANY)
    dma = pltpu.SemaphoreType.DMA
    f32 = jnp.float32
    longest = max(
        3 * channels * rows,
        2 * channels * rows,
        2 * all_channels * sub_rows,
        seq_count * slots * rows,
        total * slots * sub_rows,
    )
    held = pl.pallas_call(
        functools.partial(whole_kernel, sizes),
        out_shape=(
            pltpu.VMEM((channels, local_len), f32),
            pltpu.VMEM((feats, sub_rows * lanes), f32),
        ),
        in_specs=[anywhere] * (6 + len(tables)),
        out_specs=(in_vmem, in_vmem),
        scratch_shapes=[
            pltpu.VMEM((channels, local_len), f32),
            pltpu.VMEM((channels, local_len), f32),
            pltpu.VMEM((feats, local_len), f32),
            *[pltpu.VMEM(table.shape, table.dtype) for table in tables],
            pltpu.VMEM((feats, all_channels), f32),
            pltpu.VMEM((1, all_channels), f32),
            pltpu.VMEM((1, all_channels), f32),
            dma((6 + len(tables),)),
            pltpu.VMEM((3, channels * rows, lanes), f32),
            pltpu.VMEM((3, per, data_rows, lanes), f32),
            pltpu.VMEM((3, per, half * rows, lanes), f32),
            pltpu.VMEM((seq_count, slots * rows, lanes), f32),
            pltpu.VMEM((total, slots * sub_rows, lanes), f32),
            pltpu.VMEM((2 * channels * rows, lanes), f32),
            pltpu.VMEM((2 * all_channels * sub_rows, lanes), f32),
            pltpu.VMEM((sub_rows, all_channels, lanes), f32),
            pltpu.VMEM((all_channels, lanes), f32),
            pltpu.VMEM((all_channels, lanes), f32),
            pltpu.VMEM((all_channels, feats), f32),
            pltpu.VMEM((longest, lanes), f32),
            pltpu.VMEM((data_rows, 2 * lanes), f32),
            dma((per,)),
            dma((per,)),
            dma((per,)),
            dma((5,)),
            dma((3,)),
            pltpu.SemaphoreType.REGULAR((1,)),
        ],
        compiler_params=pltpu.CompilerParams(collective_id=0, has_side_effects=True),
    )(
        out_grad,
        gated_input,
        features,
        filter_weight,
        rates.reshape(1, all_channels),
        skip_bias.reshape(1, all_channels),
        *[jnp.asarray(table) for table in tables],
    )
    held = [pltpu.with_memory_space_constraint(value, pltpu.VMEM) for value in held]
    return pl.pallas_call(
        store_kernel,
        out_shape=tuple(jax.ShapeDtypeStruct(value.shape, f32) for value in held),
        in_specs=[in_vmem] * 2,
        out_specs=(anywhere, anywhere),
        scratch_shapes=[dma((2,))],
    )(*held)


def store_kernel(first_ref, second_ref, first_hbm, second_hbm, sem):
    stores = [
        pltpu.make_async_copy(first_ref, first_hbm, sem.at[0]),
        pltpu.make_async_copy(second_ref, second_hbm, sem.at[1]),
    ]
    for store in stores:
        store.start()
    for store in stores:
        store.wait()


def solution(mesh):
    seq_count, ch_count = mesh.shape["seq"], mesh.shape["ch"]
    in_specs = (P("ch", "seq"), P("ch", "seq"), P(None, "seq"), P(), P(), P())
    out_specs = (P("ch", "seq"), P(None, ("seq", "ch")))

    def whole(*args):
        channels, full_len = args[0].shape
        channels = channels // ch_count
        local_len = full_len // seq_count
        half, inner, mixed, mixed_per, per = plan(seq_count, channels)
        fits = (
            seq_count % 4 == 0
            and channels % 8 == 0
            and mixed == inner * mixed_per
            and mixed_per == 2
            and mixed + half * per == channels
            and per % 2 == 1
            and per >= 5
            and local_len % (8 * lanes * ch_count) == 0
            and full_len <= 512 * lanes
        )
        body = local
        if fits:
            row, row_back, lane, lane_back, twist = make_tables(full_len // lanes)
            half_row, half_back, _, _, half_twist = make_tables(full_len // lanes // 2)
            tables = (row, row_back, lane, lane_back, twist, half_row, half_back * 2, half_twist)
            body = functools.partial(local_whole, seq_count, ch_count, tables)
        return jax.shard_map(
            body, mesh=mesh, in_specs=in_specs, out_specs=out_specs, check_vma=False
        )(*args)

    return whole
```
